32 devices in a mesh: mem: 8 (over z, y), lev: 4 (over x, core).
Axes of the slice: x: 2, y: 2, z: 4, core: 2. Of those that a mesh axis runs over, the one named last changes fastest.
Arguments:
- prior_ensemble_stack: float32 [16, 20, 64, 512], P('mem', 'lev'), may hold values from -6 to 6
- vertical_cfl_ratio: float32 [20, 64, 512], P('lev'), may hold values from -0.35 to 0.35
- horizontal_cfl_ratio: float32 [20, 64, 512], P('lev'), may hold values from -0.35 to 0.35
- spreading_coefficient: float32 [20], P('lev'), may hold values from 0.02 to 0.2
- obs_cells: int32 [2, 16], replicated, may hold values from 0 to 32767
- obs_slabs: int32 [2, 16], replicated, may hold values from 0 to 19
- obs_values: float32 [2, 16], replicated, may hold values from -6 to 6
- obs_error: float32 [2, 16], replicated, may hold values from 0.25 to 2
Outputs:
- analysis: float32 [16, 20, 64, 512], P('mem', 'lev')
The draws below stay inside these ranges and needn't reach their ends.
All inputs are finite; a program needn't handle non-finite values.
Results may differ from the reference program's by a relative error of at most 0.0001.
Values sent between devices are 32-bit elements; how exact they have to be, the bound alone decides.
No kernel may reach another device: no remote copies, remote signals or barrier semaphores. Data moves between devices by JAX's collectives and lax.ppermute only.
A program may use at most 256 MiB of HBM per device.

```python
import math
import jax
import jax.numpy as jnp
from jax import lax

NY = 64
NX = 512
STEPS = 2
BATCHES = 2
OBS = 16
MEMBERS = 16
SLABS = 20
LOC_HALF = 64


def place_ends(array, own_key, smallest, high):
    index_at = [jax.random.randint(jax.random.fold_in(own_key, axis), (), 0, length) for axis, length in enumerate(array.shape)]
    widest = array.shape.index(max(array.shape))
    beside = index_at[:widest] + [(index_at[widest] + 1) % array.shape[widest]] + index_at[widest + 1:]
    return array.at[tuple(index_at)].set(smallest).at[tuple(beside)].set(high)


def block_scale(stream_key, shape, cuts, low, high):
    factor_of = 1.0
    for axis_at, blocks in cuts:
        heights = jax.random.uniform(jax.random.fold_in(jax.random.fold_in(stream_key, 6), axis_at), (blocks,), jnp.float32, low / len(cuts), high / len(cuts))
        factor_of = factor_of * jnp.repeat(jnp.exp(heights), shape[axis_at] // blocks).reshape((-1,) + (1,) * (len(shape) - 1 - axis_at))
    return factor_of


def centred(key, shape, scale, limit, pieces=(), kind=jnp.bfloat16):
    entries = scale * jax.random.normal(key, shape, jnp.float32)
    if pieces:
        entries = entries * block_scale(key, shape, pieces, -0.22, 0.18)
    return jnp.clip(entries, -limit, limit).astype(kind)


def setup_inputs(seed: int = 0) -> dict:
    splits = jax.random.split(jax.random.key(seed), 9)
    return {
        "prior_ensemble_stack": centred(splits[0], (MEMBERS, SLABS, NY, NX), 1.0, 6.0, ((0, 8), (1, 4)), jnp.float32),
        "vertical_cfl_ratio": jnp.clip(jax.random.uniform(splits[1], (SLABS, NY, NX), jnp.float32, -0.35, 0.35) * block_scale(splits[1], (SLABS, NY, NX), ((0, 4),), -0.4, 0.0), -0.35, 0.35),
        "horizontal_cfl_ratio": jnp.clip(jax.random.uniform(splits[2], (SLABS, NY, NX), jnp.float32, -0.35, 0.35) * block_scale(splits[2], (SLABS, NY, NX), ((0, 4),), -0.4, 0.0), -0.35, 0.35),
        "spreading_coefficient": jnp.clip(jnp.exp(math.log(0.2) - 2.3025851 * jax.random.uniform(splits[3], (SLABS,), jnp.float32) ** block_scale(splits[3], (SLABS,), ((0, 4),), -0.2, 0.2)), 0.02, 0.2),
        "obs_cells": place_ends(jax.random.randint(splits[4], (BATCHES, OBS), 0, NY * NX), jax.random.fold_in(splits[4], 1), 0, (NY * NX) - 1).astype(jnp.int32),
        "obs_slabs": place_ends(jax.random.randint(splits[5], (BATCHES, OBS), 0, SLABS), jax.random.fold_in(splits[5], 1), 0, SLABS - 1).astype(jnp.int32),
        "obs_values": centred(splits[6], (BATCHES, OBS), 1.5, 6.0, (), jnp.float32),
        "obs_error": jnp.clip(jnp.exp(jax.random.uniform(splits[7], (BATCHES, OBS), jnp.float32, math.log(0.25), math.log(2.0))), 0.25, 2.0),
    }


def predicted_model_vector(ensemble_gridded_values, vertical_cfl_ratio, horizontal_cfl_ratio, spreading_coefficient):
    diffuse = spreading_coefficient[:, None, None]
    for time_step in range(STEPS):
        widths = [(0, 0)] * (ensemble_gridded_values.ndim - 2) + [(1, 1), (1, 1)]
        padded = jnp.pad(ensemble_gridded_values, widths, mode='edge')
        east_cell = padded[..., 1:-1, 2:]
        west_cell = padded[..., 1:-1, :-2]
        north_cell = padded[..., 2:, 1:-1]
        south_cell = padded[..., :-2, 1:-1]
        ensemble_gridded_values = ensemble_gridded_values - 0.5 * vertical_cfl_ratio * (east_cell - west_cell) - 0.5 * horizontal_cfl_ratio * (north_cell - south_cell) + diffuse * (east_cell + west_cell + north_cell + south_cell - 4.0 * ensemble_gridded_values)
    return ensemble_gridded_values

def grid_distance(cells_a, cells_b):
    row_gap = (cells_a[:, None] // NX - cells_b[None, :] // NX).astype(jnp.float32)
    col_gap = (cells_a[:, None] % NX - cells_b[None, :] % NX).astype(jnp.float32)
    return jnp.sqrt(row_gap * row_gap + col_gap * col_gap)

def gaspari_taper(dist):
    scaled = dist / LOC_HALF
    inner_portion = (((-0.25 * scaled + 0.5) * scaled + 0.625) * scaled - 5.0 / 3.0) * scaled * scaled + 1.0
    safe_ratio = jnp.maximum(scaled, 1.0)
    outer_portion = ((((scaled / 12.0 - 0.5) * scaled + 0.625) * scaled + 5.0 / 3.0) * scaled - 5.0) * scaled + 4.0 - 2.0 / (3.0 * safe_ratio)
    return jnp.where(scaled <= 1.0, inner_portion, jnp.where(scaled < 2.0, outer_portion, 0.0))

def obs_space(prior_rows, row_cells, first_row, obs_cell, obs_value, obs_var):
    member_count = prior_rows.shape[1]
    reach_table = gaspari_taper(grid_distance(row_cells, obs_cell))

    def advance_obs(current, position):
        own_row = lax.dynamic_index_in_dim(current, first_row + position, 0, False)
        row_mean = jnp.mean(own_row)
        anomaly = own_row - row_mean
        spread = jnp.sum(anomaly * anomaly) / (member_count - 1) + 1e-06
        error_var = lax.dynamic_index_in_dim(obs_var, position, 0, False)
        seen_value = lax.dynamic_index_in_dim(obs_value, position, 0, False)
        shrink = jnp.sqrt(error_var / (spread + error_var))
        increment = (row_mean * error_var + seen_value * spread) / (spread + error_var) - row_mean + (shrink - 1.0) * anomaly
        centered = current - lax.optimization_barrier(jnp.mean(current, axis=1, keepdims=True))
        slopes = jnp.dot(centered, anomaly, precision=lax.Precision.HIGHEST) / ((member_count - 1) * spread)
        weight = lax.dynamic_index_in_dim(reach_table, position, 1, False)
        current = current + (weight * slopes)[:, None] * increment[None, :]
        return (current, (anomaly, spread, increment))
    positions = jnp.arange(obs_cell.shape[0], dtype=jnp.int32)
    prior_rows, obs_plan = lax.scan(advance_obs, prior_rows, positions)
    return (obs_plan, prior_rows)

def settle(state_rows, obs_plan, cell_loc):
    prior_anoms, spreads, increments = obs_plan
    member_count = state_rows.shape[0]
    centered = state_rows - lax.optimization_barrier(jnp.mean(state_rows, axis=0, keepdims=True))
    cross_cov = jnp.einsum('km,msc->ksc', prior_anoms, centered, precision=lax.Precision.HIGHEST) / (member_count - 1)
    incr_anom = increments - lax.optimization_barrier(jnp.mean(increments, axis=1, keepdims=True))
    incr_link = jnp.dot(incr_anom, prior_anoms.T, precision=lax.Precision.HIGHEST) / (member_count - 1)

    def solve_step(weights, position):
        column = lax.dynamic_index_in_dim(incr_link, position, 1, False)
        summed_total = lax.dynamic_index_in_dim(cross_cov, position, 0, False) + jnp.einsum('j,jsc->sc', column, weights, precision=lax.Precision.HIGHEST)
        taper_row = lax.dynamic_index_in_dim(cell_loc, position, 0, False)
        update_row = taper_row[None, :] * summed_total / lax.dynamic_index_in_dim(spreads, position, 0, False)
        return (lax.dynamic_update_index_in_dim(weights, update_row, position, 0), None)
    positions = jnp.arange(cross_cov.shape[0], dtype=jnp.int32)
    weights, unused = lax.scan(solve_step, jnp.zeros_like(cross_cov), positions)
    return state_rows + jnp.einsum('km,ksc->msc', increments, weights, precision=lax.Precision.HIGHEST)

def reference(prior_ensemble_stack, vertical_cfl_ratio, horizontal_cfl_ratio, spreading_coefficient, obs_cells, obs_slabs, obs_values, obs_error):

    def advance_member(lone_realization_vector):
        return predicted_model_vector(lone_realization_vector, vertical_cfl_ratio, horizontal_cfl_ratio, spreading_coefficient)
    ensemble_gridded_values = lax.map(advance_member, prior_ensemble_stack)
    member_count = prior_ensemble_stack.shape[0]
    state_rows = ensemble_gridded_values.reshape(member_count, SLABS, NY * NX)
    grid_cells = jnp.arange(NY * NX, dtype=jnp.int32)
    for batch_no in range(BATCHES):
        prior_rows = state_rows[:, obs_slabs[batch_no], obs_cells[batch_no]].T
        obs_plan, carried = obs_space(prior_rows, obs_cells[batch_no], 0, obs_cells[batch_no], obs_values[batch_no], obs_error[batch_no])
        cell_loc = gaspari_taper(grid_distance(obs_cells[batch_no], grid_cells))
        state_rows = settle(state_rows, obs_plan, cell_loc)
    return state_rows.reshape(prior_ensemble_stack.shape)
```

```python
import functools

import jax
import jax.numpy as jnp
from jax import lax
from jax.experimental import pallas as pl
from jax.experimental.pallas import tpu as pltpu
from jax.sharding import PartitionSpec as P

STEPS = 2
LOC_HALF = 64
LANES = 128
TILE = 8
VMEM = pl.BlockSpec(memory_space=pltpu.VMEM)
SMEM = pl.BlockSpec(memory_space=pltpu.SMEM)


def cost(flops, nbytes):
    return pl.CostEstimate(flops=flops, bytes_accessed=nbytes, transcendentals=0)


def taper(row_gap, col_gap):
    scaled = jnp.sqrt(row_gap * row_gap + col_gap * col_gap) * (1.0 / LOC_HALF)
    inner = (
        ((-0.25 * scaled + 0.5) * scaled + 0.625) * scaled - 5.0 / 3.0
    ) * scaled * scaled + 1.0
    safe = jnp.maximum(scaled, 1.0)
    outer = (
        ((((scaled * (1.0 / 12.0) - 0.5) * scaled + 0.625) * scaled + 5.0 / 3.0) * scaled - 5.0)
        * scaled
        + 4.0
        - (2.0 / 3.0) / safe
    )
    return jnp.where(scaled <= 1.0, inner, jnp.where(scaled < 2.0, outer, 0.0))


def chunks_of(slab_dev):
    first = max(1, (2 * slab_dev) // 5)
    return ((0, first), (first, slab_dev - first)) if slab_dev > 1 else ((0, 1),)


def forecast_kernel(
    parts, n, cells_ref, slabs_ref, base_ref, spread_ref, x_ref, cv_ref, ch_ref, *rest
):
    outs, (field, picks) = rest[: len(parts)], rest[len(parts) :]
    mem_dev, _, ny, nx = x_ref.shape
    block = ny // n
    tiles = nx // LANES
    depth = block * tiles
    slab = pl.program_id(0)
    diffuse = spread_ref[slab]
    rows = lax.broadcasted_iota(jnp.int32, (ny, nx), 0)
    cols = lax.broadcasted_iota(jnp.int32, (ny, nx), 1)
    half_v = 0.5 * cv_ref[0]
    half_h = 0.5 * ch_ref[0]
    east_w, west_w = diffuse - half_v, diffuse + half_v
    north_w, south_w = diffuse - half_h, diffuse + half_h
    for m in range(mem_dev):
        f = x_ref[m, 0]
        for _ in range(STEPS):
            east = jnp.where(cols == nx - 1, f, pltpu.roll(f, nx - 1, 1))
            west = jnp.where(cols == 0, f, pltpu.roll(f, 1, 1))
            north = jnp.where(rows == ny - 1, f, pltpu.roll(f, ny - 1, 0))
            south = jnp.where(rows == 0, f, pltpu.roll(f, 1, 0))
            f = (
                (1.0 - 4.0 * diffuse) * f
                + east_w * east
                + west_w * west
                + north_w * north
                + south_w * south
            )
        for t in range(tiles):
            field[slab * mem_dev + m, pl.ds(t * ny, ny), :] = f[:, t * LANES : (t + 1) * LANES]
        for (start, count), out in zip(parts, outs):

            @pl.when((slab >= start) & (slab < start + count))
            def _():
                at = (m * count + slab - start) * depth
                for d in range(n):
                    for t in range(tiles):
                        out[d, pl.ds(at + t * block, block), :] = f[
                            d * block : (d + 1) * block, t * LANES : (t + 1) * LANES
                        ]

    @pl.when(slab == pl.num_programs(0) - 1)
    def _():
        slab_dev = pl.num_programs(0)
        total = cells_ref.shape[0]
        lane = lax.broadcasted_iota(jnp.int32, (1, LANES), 1)
        for k in range(total):
            cell = cells_ref[k]
            row, col = cell // nx, cell % nx
            off = slabs_ref[k] - base_ref[1] * slab_dev
            inside = (off >= 0) & (off < slab_dev)
            wanted = jnp.where(inside, col % LANES, LANES)
            off = jnp.clip(off, 0, slab_dev - 1)
            for m in range(mem_dev):
                line = field[off * mem_dev + m, pl.ds((col // LANES) * ny + row, 1), :]
                picks[m, pl.ds(k, 1), :] = jnp.where(lane == wanted, line, 0.0)
        diagonal = lax.broadcasted_iota(jnp.int32, (total, LANES), 0) == lax.broadcasted_iota(
            jnp.int32, (total, LANES), 1
        )
        place = lax.broadcasted_iota(jnp.int32, (TILE, LANES), 0)
        seen = jnp.zeros((TILE, LANES), jnp.float32)
        for m in range(mem_dev):
            value = jnp.sum(picks[m], axis=1, keepdims=True)
            value = jnp.sum(jnp.where(diagonal, value, 0.0), axis=0, keepdims=True)
            seen = jnp.where(place == (base_ref[0] * mem_dev + m) % TILE, value, seen)
        for d in range(n):
            outs[0][d, pl.ds(mem_dev * parts[0][1] * depth, TILE), :] = seen


def forecast(parts, n, cells, slabs, base, spread, x, cv, ch):
    mem_dev, slab_dev, ny, nx = x.shape
    depth = ny // n * nx // LANES
    shapes = [
        (n, mem_dev * count * depth + (TILE if i == 0 else 0), LANES)
        for i, (_, count) in enumerate(parts)
    ]
    return pl.pallas_call(
        functools.partial(forecast_kernel, parts, n),
        grid=(slab_dev,),
        in_specs=[
            SMEM,
            SMEM,
            SMEM,
            SMEM,
            pl.BlockSpec((mem_dev, 1, ny, nx), lambda s: (0, s, 0, 0)),
            pl.BlockSpec((1, ny, nx), lambda s: (s, 0, 0)),
            pl.BlockSpec((1, ny, nx), lambda s: (s, 0, 0)),
        ],
        out_specs=[pl.BlockSpec(shape, lambda s: (0, 0, 0)) for shape in shapes],
        out_shape=[jax.ShapeDtypeStruct(shape, jnp.float32) for shape in shapes],
        scratch_shapes=[
            pltpu.VMEM((slab_dev * mem_dev, ny * nx // LANES, LANES), jnp.float32),
            pltpu.VMEM((mem_dev, cells.shape[0], LANES), jnp.float32),
        ],
        cost_estimate=cost(60 * x.size, 4 * (2 * x.size + 2 * cv.size)),
        name="forecast",
    )(cells, slabs, base, spread, x, cv, ch)


def taper_kernel(nx, block, cells_ref, base_ref, out_ref):
    depth = out_ref.shape[1]
    at = lax.broadcasted_iota(jnp.int32, (depth, LANES), 0)
    row = (base_ref[0] * block + at % block).astype(jnp.float32)
    col = (at // block * LANES + lax.broadcasted_iota(jnp.int32, (depth, LANES), 1)).astype(
        jnp.float32
    )

    def one(k, carry):
        cell = cells_ref[k]
        out_ref[k] = taper(
            row - (cell // nx).astype(jnp.float32), col - (cell % nx).astype(jnp.float32)
        )
        return carry

    lax.fori_loop(0, out_ref.shape[0], one, 0)


def taper_table(nx, block, cells, base):
    depth = block * nx // LANES
    total = cells.shape[0]
    return pl.pallas_call(
        functools.partial(taper_kernel, nx, block),
        in_specs=[SMEM, SMEM],
        out_specs=VMEM,
        out_shape=jax.ShapeDtypeStruct((total, depth, LANES), jnp.float32),
        cost_estimate=cost(60 * total * depth * LANES, 4 * total * depth * LANES),
        name="taper_table",
    )(cells, base)


def plan_kernel(nx, batch, cells_ref, values_ref, errors_ref, *refs):
    tiles, (anom_ref, incr_ref) = refs[:-2], refs[-2:]
    total = cells_ref.shape[0]
    rows = tiles[0][...]
    for other in tiles[1:]:
        rows = rows + other[...]
    members = rows.shape[0]
    lane = lax.broadcasted_iota(jnp.int32, (1, LANES), 1)
    row_of = jnp.zeros((1, LANES), jnp.float32)
    col_of = jnp.zeros((1, LANES), jnp.float32)
    where = []
    for k in range(total):
        cell = cells_ref[k]
        row, col = (cell // nx).astype(jnp.float32), (cell % nx).astype(jnp.float32)
        where.append((row, col))
        row_of = jnp.where(lane == k, row, row_of)
        col_of = jnp.where(lane == k, col, col_of)
    mean = jnp.sum(rows, axis=0, keepdims=True) * (1.0 / members)
    rows = rows - mean
    for k in range(total):
        loc = taper(row_of - where[k][0], col_of - where[k][1])
        anomaly = jnp.broadcast_to(rows[:, k : k + 1], rows.shape)
        ybar = jnp.broadcast_to(mean[:, k : k + 1], mean.shape)
        variance = jnp.sum(anomaly * anomaly, axis=0, keepdims=True) / (members - 1) + 1e-06
        shared = jnp.sum(rows * anomaly, axis=0, keepdims=True)
        error, value = errors_ref[k], values_ref[k]
        scale = 1.0 / ((members - 1) * variance)
        shift = (ybar * error + value * variance) / (variance + error) - ybar
        shrink = jnp.sqrt(error / (variance + error)) - 1.0
        anom_ref[k] = anomaly * scale
        incr_ref[k] = shift + shrink * anomaly
        weight = loc * shared * scale
        mean = mean + weight * shift
        rows = rows + (weight * shrink) * anomaly


def filter_plan(nx, batch, cells, values, errors, tiles):
    members = tiles[0].shape[0]
    total = cells.shape[0]
    table = jax.ShapeDtypeStruct((total, members, LANES), jnp.float32)
    return pl.pallas_call(
        functools.partial(plan_kernel, nx, batch),
        in_specs=[SMEM] * 3 + [VMEM] * len(tiles),
        out_specs=[VMEM, VMEM],
        out_shape=[table, table],
        cost_estimate=cost(20_000_000, 4 * 2 * total * members * LANES),
        name="filter_plan",
    )(cells, values, errors, *tiles)


def settle_kernel(mem_dev, count, depth, anom_ref, incr_ref, loc_ref, x_ref, out_ref):
    total = loc_ref.shape[0]
    members = anom_ref.shape[1]
    group = 2 if depth % (2 * TILE) == 0 and members <= 16 else 1
    span = group * TILE
    per_slab = depth // span

    def spread(ref, k, m):
        return ref[k, pl.ds(m, TILE, stride=0), :]

    def part(i, carry):
        slab, at = i // per_slab, (i % per_slab) * span

        def spot(m, g):
            row = ((m % mem_dev) * count + slab) * depth + at + g * TILE
            return m // mem_dev, pl.ds(pl.multiple_of(row, TILE), TILE)

        xs = []
        for m in range(members):
            for g in range(group):
                src, row = spot(m, g)
                xs.append(x_ref[src, row, :])

        def step(k, xs):
            sums = [None] * group
            for m in range(members):
                a = spread(anom_ref, k, m)
                for g in range(group):
                    term = a * xs[m * group + g]
                    sums[g] = term if m == 0 else sums[g] + term
            sums = [
                s * loc_ref[k, pl.ds(pl.multiple_of(at + g * TILE, TILE), TILE), :]
                for g, s in enumerate(sums)
            ]
            new = []
            for m in range(members):
                b = spread(incr_ref, k, m)
                for g in range(group):
                    new.append(xs[m * group + g] + b * sums[g])
            return tuple(new)

        xs = lax.fori_loop(0, total, step, tuple(xs), unroll=2)
        for m in range(members):
            for g in range(group):
                src, row = spot(m, g)
                out_ref[src, row, :] = xs[m * group + g]
        return carry

    lax.fori_loop(0, count * per_slab, part, 0)


def settle(mem_dev, count, depth, anom, incr, loc, x):
    n = x.shape[0]
    shape = (n, mem_dev * count * depth, LANES)
    size = n * mem_dev * count * depth * LANES
    return pl.pallas_call(
        functools.partial(settle_kernel, mem_dev, count, depth),
        in_specs=[VMEM] * 4,
        out_specs=VMEM,
        out_shape=jax.ShapeDtypeStruct(shape, jnp.float32),
        cost_estimate=cost(4 * loc.shape[0] * size, 8 * size),
        name="settle",
    )(anom, incr, loc, x)


def assemble_kernel(n, recv_ref, *refs):
    out_ref = refs[-1]
    mem_dev, _, ny, nx = out_ref.shape
    block = ny // n
    tiles = nx // LANES
    depth = block * tiles
    count = recv_ref.shape[1] // (mem_dev * depth)
    slab = pl.program_id(0)
    for m in range(mem_dev):
        at = (m * count + slab) * depth
        for d in range(n):
            for t in range(tiles):
                out_ref[m, 0, d * block : (d + 1) * block, t * LANES : (t + 1) * LANES] = recv_ref[
                    d, pl.ds(at + t * block, block), :
                ]


def assemble(n, start, count, recv, shape, before):
    mem_dev, _, ny, nx = shape
    extra = [] if before is None else [before]
    return pl.pallas_call(
        functools.partial(assemble_kernel, n),
        grid=(count,),
        in_specs=[pl.BlockSpec(recv.shape, lambda s: (0, 0, 0))]
        + [pl.BlockSpec(memory_space=pl.ANY)] * len(extra),
        out_specs=pl.BlockSpec((mem_dev, 1, ny, nx), lambda s: (0, start + s, 0, 0)),
        out_shape=jax.ShapeDtypeStruct(shape, jnp.float32),
        input_output_aliases={} if before is None else {1: 0},
        cost_estimate=cost(0, 8 * recv.size),
        name="assemble",
    )(recv, *extra)


def body(x, cv, ch, spread, obs_cells, obs_slabs, obs_values, obs_error):
    mem_dev, slab_dev, ny, nx = x.shape
    n, lev = lax.axis_size("mem"), lax.axis_size("lev")
    batch = obs_cells.shape[1]
    block = ny // n
    depth = block * nx // LANES
    members = n * mem_dev
    parts = chunks_of(slab_dev)
    cells, slabs = obs_cells.reshape(-1), obs_slabs.reshape(-1)
    base = jnp.stack([lax.axis_index("mem"), lax.axis_index("lev")]).astype(jnp.int32)
    sends = forecast(parts, n, cells, slabs, base, spread, x, cv, ch)
    states = [lax.all_to_all(s, "mem", split_axis=0, concat_axis=0, tiled=True) for s in sends]
    loc = taper_table(nx, block, cells, base)
    seen = states[0][:, mem_dev * parts[0][1] * depth :, :]
    seen = seen.reshape(members // TILE, -1, TILE, LANES).sum(axis=1).reshape(members, LANES)
    tiles = [seen] + [
        lax.ppermute(seen, "lev", [(i, (i + d) % lev) for i in range(lev)]) for d in range(1, lev)
    ]
    anom, incr = filter_plan(
        nx, batch, cells, obs_values.reshape(-1), obs_error.reshape(-1), tiles
    )
    result = None
    for (start, count), state in zip(parts, states):
        new = settle(mem_dev, count, depth, anom, incr, loc, state)
        back = lax.all_to_all(new, "mem", split_axis=0, concat_axis=0, tiled=True)
        result = assemble(n, start, count, back, x.shape, result)
    return result


def solution(mesh):
    in_specs = (
        P("mem", "lev", None, None),
        P("lev", None, None),
        P("lev", None, None),
        P("lev"),
        P(),
        P(),
        P(),
        P(),
    )
    out_specs = P("mem", "lev", None, None)
    return jax.shard_map(body, mesh=mesh, in_specs=in_specs, out_specs=out_specs, check_vma=False)
```

```python
import functools

import jax
import jax.numpy as jnp
from jax import lax
from jax.experimental import pallas as pl
from jax.experimental.pallas import tpu as pltpu
from jax.sharding import PartitionSpec as P


STEPS = 2
LOC_HALF = 64
LANES = 128
GRANT = 24 * 1024 * 1024
TILE = 8
VMEM = pl.BlockSpec(memory_space=pltpu.VMEM)
SMEM = pl.BlockSpec(memory_space=pltpu.SMEM)


def cost(flops, nbytes):
    return pl.CostEstimate(flops=flops, bytes_accessed=nbytes, transcendentals=0)


def taper(row_gap, col_gap):
    scaled = jnp.sqrt(row_gap * row_gap + col_gap * col_gap) * (1.0 / LOC_HALF)
    inner = (
        ((-0.25 * scaled + 0.5) * scaled + 0.625) * scaled - 5.0 / 3.0
    ) * scaled * scaled + 1.0
    safe = jnp.maximum(scaled, 1.0)
    outer = (
        ((((scaled * (1.0 / 12.0) - 0.5) * scaled + 0.625) * scaled + 5.0 / 3.0) * scaled - 5.0)
        * scaled
        + 4.0
        - (2.0 / 3.0) / safe
    )
    return jnp.where(scaled <= 1.0, inner, jnp.where(scaled < 2.0, outer, 0.0))


def chunks_of(slab_dev):
    first = max(1, (2 * slab_dev) // 5)
    return ((0, first), (first, slab_dev - first)) if slab_dev > 1 else ((0, 1),)


def place(ref, k):
    return ref[k // ref.shape[1], k % ref.shape[1]]


def params():
    return pltpu.CompilerParams(vmem_limit_bytes=GRANT)


def forecast_kernel(parts, n, cells_ref, slabs_ref, spread_ref, x_ref, cv_ref, ch_ref, *rest):
    outs, (field, picks) = rest[: len(parts) * n], rest[len(parts) * n :]
    mem_dev, _, ny, nx = x_ref.shape
    block = ny // n
    tiles = nx // LANES
    depth = block * tiles
    me = lax.axis_index("mem")
    slab = pl.program_id(0)
    diffuse = spread_ref[slab]
    rows = lax.broadcasted_iota(jnp.int32, (ny, nx), 0)
    cols = lax.broadcasted_iota(jnp.int32, (ny, nx), 1)
    half_v = 0.5 * cv_ref[0]
    half_h = 0.5 * ch_ref[0]
    east_w, west_w = diffuse - half_v, diffuse + half_v
    north_w, south_w = diffuse - half_h, diffuse + half_h
    for m in range(mem_dev):
        f = x_ref[m, 0]
        for _ in range(STEPS):
            east = jnp.where(cols == nx - 1, f, pltpu.roll(f, nx - 1, 1))
            west = jnp.where(cols == 0, f, pltpu.roll(f, 1, 1))
            north = jnp.where(rows == ny - 1, f, pltpu.roll(f, ny - 1, 0))
            south = jnp.where(rows == 0, f, pltpu.roll(f, 1, 0))
            f = (
                (1.0 - 4.0 * diffuse) * f
                + east_w * east
                + west_w * west
                + north_w * north
                + south_w * south
            )
        for t in range(tiles):
            field[slab * mem_dev + m, pl.ds(t * ny, ny), :] = f[:, t * LANES : (t + 1) * LANES]
    for c, (start, count) in enumerate(parts):

        @pl.when((slab >= start) & (slab < start + count))
        def _():
            for m in range(mem_dev):
                at = pl.multiple_of((m * count + slab - start) * depth, TILE)
                for j in range(n):
                    for t in range(tiles):
                        row = pl.multiple_of(t * ny + (me ^ j) * block, block)
                        outs[c * n + j][pl.ds(at + t * block, block), :] = field[
                            slab * mem_dev + m, pl.ds(row, block), :
                        ]

    @pl.when(slab == pl.num_programs(0) - 1)
    def _():
        slab_dev = pl.num_programs(0)
        total = cells_ref.shape[0] * cells_ref.shape[1]
        lane = lax.broadcasted_iota(jnp.int32, (1, LANES), 1)
        for k in range(total):
            cell = place(cells_ref, k)
            row, col = cell // nx, cell % nx
            off = place(slabs_ref, k) - lax.axis_index("lev") * slab_dev
            inside = (off >= 0) & (off < slab_dev)
            wanted = jnp.where(inside, col % LANES, LANES)
            off = jnp.clip(off, 0, slab_dev - 1)
            for m in range(mem_dev):
                line = field[off * mem_dev + m, pl.ds((col // LANES) * ny + row, 1), :]
                picks[m, pl.ds(k, 1), :] = jnp.where(lane == wanted, line, 0.0)
        diagonal = lax.broadcasted_iota(jnp.int32, (total, LANES), 0) == lax.broadcasted_iota(
            jnp.int32, (total, LANES), 1
        )
        values = []
        for m in range(mem_dev):
            value = jnp.sum(picks[m], axis=1, keepdims=True)
            values.append(jnp.sum(jnp.where(diagonal, value, 0.0), axis=0, keepdims=True))
        line = lax.broadcasted_iota(jnp.int32, (TILE, LANES), 0)
        for j in range(n):
            seen = jnp.zeros((TILE, LANES), jnp.float32)
            for m in range(mem_dev):
                seen = jnp.where(line == (j * mem_dev + m) % TILE, values[m], seen)
            outs[j][pl.ds(mem_dev * parts[0][1] * depth, TILE), :] = seen


def forecast(parts, n, cells, slabs, spread, x, cv, ch):
    mem_dev, slab_dev, ny, nx = x.shape
    depth = ny // n * nx // LANES
    shapes = [
        (mem_dev * count * depth + (TILE if i == 0 else 0), LANES)
        for i, (_, count) in enumerate(parts)
        for _ in range(n)
    ]
    outs = pl.pallas_call(
        functools.partial(forecast_kernel, parts, n),
        grid=(slab_dev,),
        in_specs=[
            SMEM,
            SMEM,
            SMEM,
            pl.BlockSpec((mem_dev, 1, ny, nx), lambda s: (0, s, 0, 0)),
            pl.BlockSpec((1, ny, nx), lambda s: (s, 0, 0)),
            pl.BlockSpec((1, ny, nx), lambda s: (s, 0, 0)),
        ],
        out_specs=[VMEM for shape in shapes],
        out_shape=[jax.ShapeDtypeStruct(shape, jnp.float32) for shape in shapes],
        scratch_shapes=[
            pltpu.VMEM((slab_dev * mem_dev, ny * nx // LANES, LANES), jnp.float32),
            pltpu.VMEM((mem_dev, cells.size, LANES), jnp.float32),
        ],
        cost_estimate=cost(60 * x.size, 4 * (2 * x.size + 2 * cv.size)),
        compiler_params=params(),
        name="forecast",
    )(cells, slabs, spread, x, cv, ch)
    return [outs[c * n : (c + 1) * n] for c in range(len(parts))]


def taper_kernel(nx, block, cells_ref, out_ref):
    depth = out_ref.shape[1]
    at = lax.broadcasted_iota(jnp.int32, (depth, LANES), 0)
    row = (lax.axis_index("mem") * block + at % block).astype(jnp.float32)
    col = (at // block * LANES + lax.broadcasted_iota(jnp.int32, (depth, LANES), 1)).astype(
        jnp.float32
    )

    def one(k, carry):
        cell = place(cells_ref, k)
        out_ref[k] = taper(
            row - (cell // nx).astype(jnp.float32), col - (cell % nx).astype(jnp.float32)
        )
        return carry

    lax.fori_loop(0, out_ref.shape[0], one, 0)


def taper_table(nx, block, cells):
    depth = block * nx // LANES
    total = cells.size
    return pl.pallas_call(
        functools.partial(taper_kernel, nx, block),
        in_specs=[SMEM],
        out_specs=VMEM,
        out_shape=jax.ShapeDtypeStruct((total, depth, LANES), jnp.float32),
        cost_estimate=cost(60 * total * depth * LANES, 4 * total * depth * LANES),
        compiler_params=params(),
        name="taper_table",
    )(cells)


def plan_kernel(nx, cells_ref, values_ref, errors_ref, *refs):
    tiles, (anom_ref, incr_ref) = refs[:-2], refs[-2:]
    total = cells_ref.shape[0] * cells_ref.shape[1]
    rows = tiles[0][...]
    for other in tiles[1:]:
        rows = rows + other[...]
    members = rows.shape[0]
    lane = lax.broadcasted_iota(jnp.int32, (1, LANES), 1)
    row_of = jnp.zeros((1, LANES), jnp.float32)
    col_of = jnp.zeros((1, LANES), jnp.float32)
    where = []
    for k in range(total):
        cell = place(cells_ref, k)
        row, col = (cell // nx).astype(jnp.float32), (cell % nx).astype(jnp.float32)
        where.append((row, col))
        row_of = jnp.where(lane == k, row, row_of)
        col_of = jnp.where(lane == k, col, col_of)
    mean = jnp.sum(rows, axis=0, keepdims=True) * (1.0 / members)
    rows = rows - mean
    for k in range(total):
        loc = taper(row_of - where[k][0], col_of - where[k][1])
        anomaly = jnp.broadcast_to(rows[:, k : k + 1], rows.shape)
        ybar = jnp.broadcast_to(mean[:, k : k + 1], mean.shape)
        variance = jnp.sum(anomaly * anomaly, axis=0, keepdims=True) / (members - 1) + 1e-06
        shared = jnp.sum(rows * anomaly, axis=0, keepdims=True)
        error, value = place(errors_ref, k), place(values_ref, k)
        scale = 1.0 / ((members - 1) * variance)
        shift = (ybar * error + value * variance) / (variance + error) - ybar
        shrink = jnp.sqrt(error / (variance + error)) - 1.0
        anom_ref[k] = anomaly * scale
        incr_ref[k] = shift + shrink * anomaly
        weight = loc * shared * scale
        mean = mean + weight * shift
        rows = rows + (weight * shrink) * anomaly


def filter_plan(nx, cells, values, errors, tiles):
    members = tiles[0].shape[0]
    total = cells.size
    table = jax.ShapeDtypeStruct((total, members, LANES), jnp.float32)
    return pl.pallas_call(
        functools.partial(plan_kernel, nx),
        in_specs=[SMEM] * 3 + [VMEM] * len(tiles),
        out_specs=[VMEM, VMEM],
        out_shape=[table, table],
        cost_estimate=cost(20_000_000, 4 * 2 * total * members * LANES),
        compiler_params=params(),
        name="filter_plan",
    )(cells, values, errors, *tiles)


def settle_kernel(n, mem_dev, count, depth, anom_ref, incr_ref, loc_ref, *refs):
    x_refs, out_refs = refs[:n], refs[n:]
    total = loc_ref.shape[0]
    members = n * mem_dev
    group = 2 if depth % (2 * TILE) == 0 and members <= 16 else 1
    span = group * TILE
    per_slab = depth // span

    def spread(ref, k, m):
        return ref[k, pl.ds(m, TILE, stride=0), :]

    def part(i, carry):
        slab, at = i // per_slab, (i % per_slab) * span

        def spot(m, g):
            row = ((m % mem_dev) * count + slab) * depth + at + g * TILE
            return m // mem_dev, pl.ds(pl.multiple_of(row, TILE), TILE)

        xs = []
        for m in range(members):
            for g in range(group):
                src, row = spot(m, g)
                xs.append(x_refs[src][row, :])

        def step(k, xs):
            sums = [None] * group
            for m in range(members):
                a = spread(anom_ref, k, m)
                for g in range(group):
                    term = a * xs[m * group + g]
                    sums[g] = term if m == 0 else sums[g] + term
            sums = [
                s * loc_ref[k, pl.ds(pl.multiple_of(at + g * TILE, TILE), TILE), :]
                for g, s in enumerate(sums)
            ]
            new = []
            for m in range(members):
                b = spread(incr_ref, k, m)
                for g in range(group):
                    new.append(xs[m * group + g] + b * sums[g])
            return tuple(new)

        xs = lax.fori_loop(0, total, step, tuple(xs), unroll=2)
        for m in range(members):
            for g in range(group):
                src, row = spot(m, g)
                out_refs[src][row, :] = xs[m * group + g]
        return carry

    lax.fori_loop(0, count * per_slab, part, 0)


def settle(mem_dev, count, depth, anom, incr, loc, xs):
    n = len(xs)
    shape = jax.ShapeDtypeStruct((mem_dev * count * depth, LANES), jnp.float32)
    size = n * mem_dev * count * depth * LANES
    return pl.pallas_call(
        functools.partial(settle_kernel, n, mem_dev, count, depth),
        in_specs=[VMEM] * (3 + n),
        out_specs=[VMEM] * n,
        out_shape=[shape] * n,
        cost_estimate=cost(4 * loc.shape[0] * size, 8 * size),
        compiler_params=params(),
        name="settle",
    )(anom, incr, loc, *xs)


def assemble_kernel(n, *refs):
    recv, out_ref, turn = refs[:n], refs[-2], refs[-1]
    mem_dev, _, ny, nx = out_ref.shape
    block = ny // n
    tiles = nx // LANES
    depth = block * tiles
    count = recv[0].shape[0] // (mem_dev * depth)
    slab = pl.program_id(0)
    me = lax.axis_index("mem")
    for m in range(mem_dev):
        at = pl.multiple_of((m * count + slab) * depth, TILE)
        for t in range(tiles):
            lanes = slice(t * LANES, (t + 1) * LANES)
            lines = pl.ds(at + t * block, block)
            for j in range(n):
                if block % TILE == 0:
                    row = pl.multiple_of((me ^ j) * block, block)
                    out_ref[m, 0, pl.ds(row, block), lanes] = recv[j][lines, :]
                else:
                    turn[pl.ds(j * block, block), :] = recv[j][lines, :]
            if block % TILE:
                for d in range(n):
                    out_ref[m, 0, d * block : (d + 1) * block, lanes] = turn[
                        pl.ds((me ^ d) * block, block), :
                    ]


def assemble(start, count, recv, shape, before):
    mem_dev, _, ny, nx = shape
    n = len(recv)
    extra = [] if before is None else [before]
    return pl.pallas_call(
        functools.partial(assemble_kernel, n),
        grid=(count,),
        in_specs=[VMEM] * n + [pl.BlockSpec(memory_space=pl.ANY)] * len(extra),
        out_specs=pl.BlockSpec((mem_dev, 1, ny, nx), lambda s: (0, start + s, 0, 0)),
        out_shape=jax.ShapeDtypeStruct(shape, jnp.float32),
        scratch_shapes=[pltpu.VMEM((ny, LANES), jnp.float32)],
        input_output_aliases={} if before is None else {n: 0},
        cost_estimate=cost(0, 8 * n * recv[0].size),
        compiler_params=params(),
        name="assemble",
    )(*recv, *extra)


def exchange(blocks):
    n = len(blocks)
    order = sorted(range(1, n), reverse=True)
    got = {
        j: lax.ppermute(blocks[j], "mem", [(i, i ^ j) for i in range(n)]) for j in order
    }
    return blocks[:1] + [got[j] for j in range(1, n)]


def body(x, cv, ch, spread, obs_cells, obs_slabs, obs_values, obs_error):
    mem_dev, slab_dev, ny, nx = x.shape
    n, lev = lax.axis_size("mem"), lax.axis_size("lev")
    block = ny // n
    depth = block * nx // LANES
    parts = chunks_of(slab_dev)
    sends = forecast(parts, n, obs_cells, obs_slabs, spread, x, cv, ch)
    states = []
    for blocks in sends:
        states.append(exchange(list(blocks)))
    loc = taper_table(nx, block, obs_cells)
    per = TILE // mem_dev
    seen = [s[mem_dev * parts[0][1] * depth :, :] for s in states[0]]
    seen = jnp.concatenate([sum(seen[g : g + per]) for g in range(0, n, per)])
    tiles = [seen] + [
        lax.ppermute(seen, "lev", [(i, (i + d) % lev) for i in range(lev)])
        for d in range(1, lev)
    ]
    anom, incr = filter_plan(nx, obs_cells, obs_values, obs_error, tiles)
    result = None
    for (start, count), state in zip(parts, states):
        new = settle(mem_dev, count, depth, anom, incr, loc, state)
        back = exchange(list(new))
        anom, _ = lax.optimization_barrier((anom, new[0]))
        result = assemble(start, count, back, x.shape, result)
    return result


def solution(mesh):
    in_specs = (
        P("mem", "lev", None, None),
        P("lev", None, None),
        P("lev", None, None),
        P("lev"),
        P(),
        P(),
        P(),
        P(),
    )
    out_specs = P("mem", "lev", None, None)
    return jax.shard_map(body, mesh=mesh, in_specs=in_specs, out_specs=out_specs, check_vma=False)
```

```python
import functools

import jax
import jax.numpy as jnp
from jax import lax
from jax.experimental import pallas as pl
from jax.experimental.pallas import tpu as pltpu
from jax.sharding import PartitionSpec as P


STEPS = 2
LOC_HALF = 64
LANES = 128
GRANT = 24 * 1024 * 1024
TILE = 8
VMEM = pl.BlockSpec(memory_space=pltpu.VMEM)
SMEM = pl.BlockSpec(memory_space=pltpu.SMEM)


def cost(flops, nbytes):
    return pl.CostEstimate(flops=flops, bytes_accessed=nbytes, transcendentals=0)


def taper(row_gap, col_gap):
    scaled = jnp.sqrt(row_gap * row_gap + col_gap * col_gap) * (1.0 / LOC_HALF)
    inner = (
        ((-0.25 * scaled + 0.5) * scaled + 0.625) * scaled - 5.0 / 3.0
    ) * scaled * scaled + 1.0
    safe = jnp.maximum(scaled, 1.0)
    outer = (
        ((((scaled * (1.0 / 12.0) - 0.5) * scaled + 0.625) * scaled + 5.0 / 3.0) * scaled - 5.0)
        * scaled
        + 4.0
        - (2.0 / 3.0) / safe
    )
    return jnp.where(scaled <= 1.0, inner, jnp.where(scaled < 2.0, outer, 0.0))


def chunks_of(slab_dev):
    first = max(1, (2 * slab_dev) // 5)
    if slab_dev == 1:
        return ((0, 1, True),)
    return ((0, first, True), (first, slab_dev - first, False))


def place(ref, k):
    return ref[k // ref.shape[1], k % ref.shape[1]]


def params():
    return pltpu.CompilerParams(vmem_limit_bytes=GRANT)


def blocks_in(refs, n, whole):
    me = lax.axis_index("mem")
    if whole:
        return [(refs[0].at[d], d) for d in range(n)]
    return [(refs[j], me ^ j) for j in range(n)]


def block_shapes(n, whole, rows):
    if whole:
        return [jax.ShapeDtypeStruct((n, rows, LANES), jnp.float32)]
    return [jax.ShapeDtypeStruct((rows, LANES), jnp.float32)] * n


def forecast_kernel(parts, n, cells_hbm, slabs_hbm, spread_hbm, x_hbm, cv_hbm, ch_hbm, *rest):
    outs = []
    for start, count, whole in parts:
        width = 1 if whole else n
        outs.append(blocks_in(rest[:width], n, whole))
        rest = rest[width:]
    x_buf, cv_buf, ch_buf, cells, slabs, spread, field, picks, sem, small = rest
    slab_dev, mem_dev, ny, nx = x_buf.shape
    block = ny // n
    tiles = nx // LANES
    depth = block * tiles
    total = cells.shape[0] * cells.shape[1]

    def loads(s):
        return (
            pltpu.make_async_copy(x_hbm.at[:, s], x_buf.at[s], sem.at[0, s]),
            pltpu.make_async_copy(cv_hbm.at[s], cv_buf.at[s], sem.at[1, s]),
            pltpu.make_async_copy(ch_hbm.at[s], ch_buf.at[s], sem.at[2, s]),
        )

    lists = (
        pltpu.make_async_copy(spread_hbm, spread, small.at[0]),
        pltpu.make_async_copy(cells_hbm, cells, small.at[1]),
        pltpu.make_async_copy(slabs_hbm, slabs, small.at[2]),
    )
    for copy in lists:
        copy.start()
    for s in range(slab_dev):
        for copy in loads(s):
            copy.start()
    for copy in lists:
        copy.wait()
    rows = lax.broadcasted_iota(jnp.int32, (ny, nx), 0)
    cols = lax.broadcasted_iota(jnp.int32, (ny, nx), 1)

    for (start, count, whole), blocks in zip(parts, outs):

        def one(s, carry):
            slab = start + s
            for copy in loads(slab):
                copy.wait()
            diffuse = spread[slab]
            half_v = 0.5 * cv_buf[slab]
            half_h = 0.5 * ch_buf[slab]
            east_w, west_w = diffuse - half_v, diffuse + half_v
            north_w, south_w = diffuse - half_h, diffuse + half_h
            for m in range(mem_dev):
                f = x_buf[slab, m]
                for _ in range(STEPS):
                    east = jnp.where(cols == nx - 1, f, pltpu.roll(f, nx - 1, 1))
                    west = jnp.where(cols == 0, f, pltpu.roll(f, 1, 1))
                    north = jnp.where(rows == ny - 1, f, pltpu.roll(f, ny - 1, 0))
                    south = jnp.where(rows == 0, f, pltpu.roll(f, 1, 0))
                    f = (
                        (1.0 - 4.0 * diffuse) * f
                        + east_w * east
                        + west_w * west
                        + north_w * north
                        + south_w * south
                    )
                for t in range(tiles):
                    field[slab * mem_dev + m, pl.ds(t * ny, ny), :] = f[
                        :, t * LANES : (t + 1) * LANES
                    ]
                at = pl.multiple_of((m * count + s) * depth, TILE)
                for ref, d in blocks:
                    for t in range(tiles):
                        row = t * ny + d * block
                        if not whole:
                            row = pl.multiple_of(row, block)
                        ref[pl.ds(at + t * block, block), :] = field[
                            slab * mem_dev + m, pl.ds(row, block), :
                        ]
            return carry

        lax.fori_loop(0, count, one, 0)

    lane = lax.broadcasted_iota(jnp.int32, (1, LANES), 1)
    for k in range(total):
        cell = place(cells, k)
        row, col = cell // nx, cell % nx
        off = place(slabs, k) - lax.axis_index("lev") * slab_dev
        inside = (off >= 0) & (off < slab_dev)
        wanted = jnp.where(inside, col % LANES, LANES)
        off = jnp.clip(off, 0, slab_dev - 1)
        for m in range(mem_dev):
            line = field[off * mem_dev + m, pl.ds((col // LANES) * ny + row, 1), :]
            picks[m, pl.ds(k, 1), :] = jnp.where(lane == wanted, line, 0.0)
    diagonal = lax.broadcasted_iota(jnp.int32, (total, LANES), 0) == lax.broadcasted_iota(
        jnp.int32, (total, LANES), 1
    )
    line = lax.broadcasted_iota(jnp.int32, (TILE, LANES), 0)
    seen = jnp.zeros((TILE, LANES), jnp.float32)
    for m in range(mem_dev):
        value = jnp.sum(picks[m], axis=1, keepdims=True)
        value = jnp.sum(jnp.where(diagonal, value, 0.0), axis=0, keepdims=True)
        seen = jnp.where(line == (lax.axis_index("mem") * mem_dev + m) % TILE, value, seen)
    for ref, d in outs[0]:
        ref[pl.ds(mem_dev * parts[0][1] * depth, TILE), :] = seen


def forecast(parts, n, cells, slabs, spread, x, cv, ch):
    mem_dev, slab_dev, ny, nx = x.shape
    depth = ny // n * nx // LANES
    shapes = []
    for i, (_, count, whole) in enumerate(parts):
        shapes.append(block_shapes(n, whole, mem_dev * count * depth + (0 if i else TILE)))
    outs = pl.pallas_call(
        functools.partial(forecast_kernel, parts, n),
        in_specs=[pl.BlockSpec(memory_space=pltpu.HBM)] * 6,
        out_specs=[VMEM for group in shapes for _ in group],
        out_shape=[shape for group in shapes for shape in group],
        scratch_shapes=[
            pltpu.VMEM((slab_dev, mem_dev, ny, nx), jnp.float32),
            pltpu.VMEM(cv.shape, jnp.float32),
            pltpu.VMEM(ch.shape, jnp.float32),
            pltpu.SMEM(cells.shape, jnp.int32),
            pltpu.SMEM(slabs.shape, jnp.int32),
            pltpu.SMEM(spread.shape, jnp.float32),
            pltpu.VMEM((slab_dev * mem_dev, ny * nx // LANES, LANES), jnp.float32),
            pltpu.VMEM((mem_dev, cells.size, LANES), jnp.float32),
            pltpu.SemaphoreType.DMA((3, slab_dev)),
            pltpu.SemaphoreType.DMA((3,)),
        ],
        cost_estimate=cost(60 * x.size, 4 * (2 * x.size + 2 * cv.size)),
        compiler_params=params(),
        name="forecast",
    )(*[pltpu.with_memory_space_constraint(a, pltpu.HBM) for a in (cells, slabs, spread, x, cv, ch)])
    sends = []
    for group in shapes:
        sends.append(list(outs[: len(group)]))
        outs = outs[len(group) :]
    return sends


def taper_kernel(nx, block, cells_ref, out_ref):
    depth = out_ref.shape[1]
    at = lax.broadcasted_iota(jnp.int32, (depth, LANES), 0)
    row = (lax.axis_index("mem") * block + at % block).astype(jnp.float32)
    col = (at // block * LANES + lax.broadcasted_iota(jnp.int32, (depth, LANES), 1)).astype(
        jnp.float32
    )

    def one(k, carry):
        cell = place(cells_ref, k)
        out_ref[k] = taper(
            row - (cell // nx).astype(jnp.float32), col - (cell % nx).astype(jnp.float32)
        )
        return carry

    lax.fori_loop(0, out_ref.shape[0], one, 0)


def taper_table(nx, block, cells):
    depth = block * nx // LANES
    total = cells.size
    return pl.pallas_call(
        functools.partial(taper_kernel, nx, block),
        in_specs=[SMEM],
        out_specs=VMEM,
        out_shape=jax.ShapeDtypeStruct((total, depth, LANES), jnp.float32),
        cost_estimate=cost(60 * total * depth * LANES, 4 * total * depth * LANES),
        compiler_params=params(),
        name="taper_table",
    )(cells)


def plan_kernel(nx, cells_ref, values_ref, errors_ref, *refs):
    tiles, (anom_ref, incr_ref) = refs[:-2], refs[-2:]
    total = cells_ref.shape[0] * cells_ref.shape[1]
    rows = tiles[0][...]
    for other in tiles[1:]:
        rows = rows + other[...]
    members = rows.shape[0]
    lane = lax.broadcasted_iota(jnp.int32, (1, LANES), 1)
    row_of = jnp.zeros((1, LANES), jnp.float32)
    col_of = jnp.zeros((1, LANES), jnp.float32)
    where = []
    for k in range(total):
        cell = place(cells_ref, k)
        row, col = (cell // nx).astype(jnp.float32), (cell % nx).astype(jnp.float32)
        where.append((row, col))
        row_of = jnp.where(lane == k, row, row_of)
        col_of = jnp.where(lane == k, col, col_of)
    mean = jnp.sum(rows, axis=0, keepdims=True) * (1.0 / members)
    rows = rows - mean
    for k in range(total):
        loc = taper(row_of - where[k][0], col_of - where[k][1])
        anomaly = jnp.broadcast_to(rows[:, k : k + 1], rows.shape)
        ybar = jnp.broadcast_to(mean[:, k : k + 1], mean.shape)
        variance = jnp.sum(anomaly * anomaly, axis=0, keepdims=True) / (members - 1) + 1e-06
        shared = jnp.sum(rows * anomaly, axis=0, keepdims=True)
        error, value = place(errors_ref, k), place(values_ref, k)
        scale = 1.0 / ((members - 1) * variance)
        shift = (ybar * error + value * variance) / (variance + error) - ybar
        shrink = jnp.sqrt(error / (variance + error)) - 1.0
        anom_ref[k, 0:members, :] = anomaly * scale
        incr_ref[k, 0:members, :] = shift + shrink * anomaly
        weight = loc * shared * scale
        mean = mean + weight * shift
        rows = rows + (weight * shrink) * anomaly


def filter_plan(nx, cells, values, errors, tiles):
    members = tiles[0].shape[0]
    total = cells.size
    table = jax.ShapeDtypeStruct((total, members + TILE, LANES), jnp.float32)
    return pl.pallas_call(
        functools.partial(plan_kernel, nx),
        in_specs=[SMEM] * 3 + [VMEM] * len(tiles),
        out_specs=[VMEM, VMEM],
        out_shape=[table, table],
        cost_estimate=cost(20_000_000, 4 * 2 * total * members * LANES),
        compiler_params=params(),
        name="filter_plan",
    )(cells, values, errors, *tiles)


def settle_kernel(n, mem_dev, count, depth, whole, anom_ref, incr_ref, loc_ref, *refs):
    width = 1 if whole else n
    ins, outs = blocks_in(refs[:width], n, whole), blocks_in(refs[width:], n, whole)
    total = loc_ref.shape[0]
    members = n * mem_dev
    group = 2 if depth % (2 * TILE) == 0 and members <= 16 else 1
    span = group * TILE
    per_slab = depth // span

    def spread(ref, k, m):
        member = ins[m // mem_dev][1] * mem_dev + m % mem_dev
        return ref[k, pl.ds(member, TILE, stride=0), :]

    def part(i, carry):
        slab, at = i // per_slab, (i % per_slab) * span

        def spot(m, g):
            row = ((m % mem_dev) * count + slab) * depth + at + g * TILE
            return m // mem_dev, pl.ds(pl.multiple_of(row, TILE), TILE)

        xs = []
        for m in range(members):
            for g in range(group):
                src, row = spot(m, g)
                xs.append(ins[src][0][row, :])

        def step(k, xs):
            sums = [None] * group
            for m in range(members):
                a = spread(anom_ref, k, m)
                for g in range(group):
                    term = a * xs[m * group + g]
                    sums[g] = term if m == 0 else sums[g] + term
            sums = [
                s * loc_ref[k, pl.ds(pl.multiple_of(at + g * TILE, TILE), TILE), :]
                for g, s in enumerate(sums)
            ]
            new = []
            for m in range(members):
                b = spread(incr_ref, k, m)
                for g in range(group):
                    new.append(xs[m * group + g] + b * sums[g])
            return tuple(new)

        xs = lax.fori_loop(0, total, step, tuple(xs), unroll=2)
        for m in range(members):
            for g in range(group):
                src, row = spot(m, g)
                outs[src][0][row, :] = xs[m * group + g]
        return carry

    lax.fori_loop(0, count * per_slab, part, 0)


def settle(n, mem_dev, count, depth, whole, anom, incr, loc, xs):
    shapes = block_shapes(n, whole, mem_dev * count * depth)
    size = n * mem_dev * count * depth * LANES
    return pl.pallas_call(
        functools.partial(settle_kernel, n, mem_dev, count, depth, whole),
        in_specs=[VMEM] * (3 + len(xs)),
        out_specs=[VMEM] * len(shapes),
        out_shape=shapes,
        cost_estimate=cost(4 * loc.shape[0] * size, 8 * size),
        compiler_params=params(),
        name="settle",
    )(anom, incr, loc, *xs)


def assemble_kernel(n, count, whole, *refs):
    recv, out_ref, turn = refs[: 1 if whole else n], refs[-2], refs[-1]
    blocks = blocks_in(recv, n, whole)
    mem_dev, _, ny, nx = out_ref.shape
    block = ny // n
    tiles = nx // LANES
    depth = block * tiles
    slab = pl.program_id(0)
    for m in range(mem_dev):
        at = pl.multiple_of((m * count + slab) * depth, TILE)
        for t in range(tiles):
            lanes = slice(t * LANES, (t + 1) * LANES)
            lines = pl.ds(at + t * block, block)
            for j, (ref, d) in enumerate(blocks):
                if whole:
                    out_ref[m, 0, d * block : (d + 1) * block, lanes] = ref[lines, :]
                elif block % TILE == 0:
                    row = pl.multiple_of(d * block, block)
                    out_ref[m, 0, pl.ds(row, block), lanes] = ref[lines, :]
                else:
                    turn[pl.ds(j * block, block), :] = ref[lines, :]
            if block % TILE and not whole:
                for d, (_, j) in enumerate(blocks):
                    out_ref[m, 0, d * block : (d + 1) * block, lanes] = turn[
                        pl.ds(j * block, block), :
                    ]


def assemble(n, start, count, whole, recv, shape, before):
    mem_dev, _, ny, nx = shape
    extra = [] if before is None else [before]
    return pl.pallas_call(
        functools.partial(assemble_kernel, n, count, whole),
        grid=(count,),
        in_specs=[VMEM] * len(recv) + [pl.BlockSpec(memory_space=pl.ANY)] * len(extra),
        out_specs=pl.BlockSpec((mem_dev, 1, ny, nx), lambda s: (0, start + s, 0, 0)),
        out_shape=jax.ShapeDtypeStruct(shape, jnp.float32),
        scratch_shapes=[pltpu.VMEM((ny, LANES), jnp.float32)],
        input_output_aliases={} if before is None else {len(recv): 0},
        cost_estimate=cost(0, 8 * len(recv) * recv[0].size),
        compiler_params=params(),
        name="assemble",
    )(*recv, *extra)


def exchange(blocks, n, whole):
    if whole:
        return [lax.all_to_all(blocks[0], "mem", split_axis=0, concat_axis=0, tiled=True)]
    got = {}
    for j in range(n - 1, 0, -1):
        got[j] = lax.ppermute(blocks[j], "mem", [(i, i ^ j) for i in range(n)])
    return blocks[:1] + [got[j] for j in range(1, n)]


def body(x, cv, ch, spread, obs_cells, obs_slabs, obs_values, obs_error):
    mem_dev, slab_dev, ny, nx = x.shape
    n, lev = lax.axis_size("mem"), lax.axis_size("lev")
    block = ny // n
    depth = block * nx // LANES
    parts = chunks_of(slab_dev)
    sends = forecast(parts, n, obs_cells, obs_slabs, spread, x, cv, ch)
    states = []
    for c, blocks in enumerate(sends):
        states.append(exchange(blocks, n, parts[c][2]))
    loc = taper_table(nx, block, obs_cells)
    per = TILE // mem_dev
    seen = states[0][0][:, mem_dev * parts[0][1] * depth :, :]
    seen = seen.reshape(n // per, per, TILE, LANES).sum(axis=1).reshape(-1, LANES)
    tiles = [seen] + [
        lax.ppermute(seen, "lev", [(i, (i + d) % lev) for i in range(lev)])
        for d in range(1, lev)
    ]
    anom, incr = filter_plan(nx, obs_cells, obs_values, obs_error, tiles)
    result = None
    for (start, count, whole), state in zip(parts, states):
        new = settle(n, mem_dev, count, depth, whole, anom, incr, loc, state)
        back = exchange(list(new), n, whole)
        anom, _ = lax.optimization_barrier((anom, new[0]))
        result = assemble(n, start, count, whole, back, x.shape, result)
    return result


def solution(mesh):
    in_specs = (
        P("mem", "lev", None, None),
        P("lev", None, None),
        P("lev", None, None),
        P("lev"),
        P(),
        P(),
        P(),
        P(),
    )
    out_specs = P("mem", "lev", None, None)
    return jax.shard_map(body, mesh=mesh, in_specs=in_specs, out_specs=out_specs, check_vma=False)
```

```python
import functools

import jax
import jax.numpy as jnp
from jax import lax
from jax.experimental import pallas as pl
from jax.experimental.pallas import tpu as pltpu
from jax.sharding import PartitionSpec as P


STEPS = 2
LOC_HALF = 64
LANES = 128
GRANT = 24 * 1024 * 1024
TILE = 8
VMEM = pl.BlockSpec(memory_space=pltpu.VMEM)
SMEM = pl.BlockSpec(memory_space=pltpu.SMEM)


def cost(flops, nbytes):
    return pl.CostEstimate(flops=flops, bytes_accessed=nbytes, transcendentals=0)


def taper(row_gap, col_gap):
    scaled = jnp.sqrt(row_gap * row_gap + col_gap * col_gap) * (1.0 / LOC_HALF)
    inner = (
        ((-0.25 * scaled + 0.5) * scaled + 0.625) * scaled - 5.0 / 3.0
    ) * scaled * scaled + 1.0
    safe = jnp.maximum(scaled, 1.0)
    outer = (
        ((((scaled * (1.0 / 12.0) - 0.5) * scaled + 0.625) * scaled + 5.0 / 3.0) * scaled - 5.0)
        * scaled
        + 4.0
        - (2.0 / 3.0) / safe
    )
    return jnp.where(scaled <= 1.0, inner, jnp.where(scaled < 2.0, outer, 0.0))


def chunks_of(slab_dev):
    first = max(1, (3 * slab_dev) // 5)
    if slab_dev == 1:
        return ((0, 1, False),)
    return ((0, first, False), (first, slab_dev - first, True))


def place(ref, k):
    return ref[k // ref.shape[1], k % ref.shape[1]]


def params():
    return pltpu.CompilerParams(vmem_limit_bytes=GRANT)


def blocks_in(refs, n, whole):
    me = lax.axis_index("mem")
    if whole:
        return [(refs[0].at[d], d) for d in range(n)]
    return [(refs[j], me ^ j) for j in range(n)]


def block_shapes(n, whole, rows):
    if whole:
        return [jax.ShapeDtypeStruct((n, rows, LANES), jnp.float32)]
    return [jax.ShapeDtypeStruct((rows, LANES), jnp.float32)] * n


def forecast_kernel(parts, n, cells_hbm, slabs_hbm, spread_hbm, x_hbm, cv_hbm, ch_hbm, *rest):
    outs = []
    for start, count, whole in parts:
        width = 1 if whole else n
        outs.append(blocks_in(rest[:width], n, whole))
        rest = rest[width:]
    seen_ref, rest = rest[0], rest[1:]
    x_buf, cv_buf, ch_buf, cells, slabs, spread, field, picks, sem, small = rest
    slab_dev, mem_dev, ny, nx = x_buf.shape
    block = ny // n
    tiles = nx // LANES
    depth = block * tiles
    total = cells.shape[0] * cells.shape[1]

    def loads(s):
        return (
            pltpu.make_async_copy(x_hbm.at[:, s], x_buf.at[s], sem.at[0, s]),
            pltpu.make_async_copy(cv_hbm.at[s], cv_buf.at[s], sem.at[1, s]),
            pltpu.make_async_copy(ch_hbm.at[s], ch_buf.at[s], sem.at[2, s]),
        )

    lists = (
        pltpu.make_async_copy(spread_hbm, spread, small.at[0]),
        pltpu.make_async_copy(cells_hbm, cells, small.at[1]),
        pltpu.make_async_copy(slabs_hbm, slabs, small.at[2]),
    )
    for copy in lists:
        copy.start()
    for s in range(slab_dev):
        for copy in loads(s):
            copy.start()
    for copy in lists:
        copy.wait()
    rows = lax.broadcasted_iota(jnp.int32, (ny, nx), 0)
    cols = lax.broadcasted_iota(jnp.int32, (ny, nx), 1)

    for (start, count, whole), blocks in zip(parts, outs):

        def one(s, carry):
            slab = start + s
            for copy in loads(slab):
                copy.wait()
            diffuse = spread[slab]
            half_v = 0.5 * cv_buf[slab]
            half_h = 0.5 * ch_buf[slab]
            east_w, west_w = diffuse - half_v, diffuse + half_v
            north_w, south_w = diffuse - half_h, diffuse + half_h
            for m in range(mem_dev):
                f = x_buf[slab, m]
                for _ in range(STEPS):
                    east = jnp.where(cols == nx - 1, f, pltpu.roll(f, nx - 1, 1))
                    west = jnp.where(cols == 0, f, pltpu.roll(f, 1, 1))
                    north = jnp.where(rows == ny - 1, f, pltpu.roll(f, ny - 1, 0))
                    south = jnp.where(rows == 0, f, pltpu.roll(f, 1, 0))
                    f = (
                        (1.0 - 4.0 * diffuse) * f
                        + east_w * east
                        + west_w * west
                        + north_w * north
                        + south_w * south
                    )
                for t in range(tiles):
                    field[slab * mem_dev + m, pl.ds(t * ny, ny), :] = f[
                        :, t * LANES : (t + 1) * LANES
                    ]
                at = pl.multiple_of((m * count + s) * depth, TILE)
                for ref, d in blocks:
                    for t in range(tiles):
                        row = t * ny + d * block
                        if not whole:
                            row = pl.multiple_of(row, block)
                        ref[pl.ds(at + t * block, block), :] = field[
                            slab * mem_dev + m, pl.ds(row, block), :
                        ]
            return carry

        lax.fori_loop(0, count, one, 0)

    lane = lax.broadcasted_iota(jnp.int32, (1, LANES), 1)
    for k in range(total):
        cell = place(cells, k)
        row, col = cell // nx, cell % nx
        off = place(slabs, k) - lax.axis_index("lev") * slab_dev
        inside = (off >= 0) & (off < slab_dev)
        wanted = jnp.where(inside, col % LANES, LANES)
        off = jnp.clip(off, 0, slab_dev - 1)
        for m in range(mem_dev):
            line = field[off * mem_dev + m, pl.ds((col // LANES) * ny + row, 1), :]
            picks[m, pl.ds(k, 1), :] = jnp.where(lane == wanted, line, 0.0)
    diagonal = lax.broadcasted_iota(jnp.int32, (total, LANES), 0) == lax.broadcasted_iota(
        jnp.int32, (total, LANES), 1
    )
    line = lax.broadcasted_iota(jnp.int32, (TILE, LANES), 0)
    seen = jnp.zeros((TILE, LANES), jnp.float32)
    for m in range(mem_dev):
        value = jnp.sum(picks[m], axis=1, keepdims=True)
        value = jnp.sum(jnp.where(diagonal, value, 0.0), axis=0, keepdims=True)
        seen = jnp.where(line == (lax.axis_index("mem") * mem_dev + m) % TILE, value, seen)
    for d in range(seen_ref.shape[0]):
        seen_ref[d] = seen


def forecast(parts, n, lev, cells, slabs, spread, x, cv, ch):
    mem_dev, slab_dev, ny, nx = x.shape
    depth = ny // n * nx // LANES
    shapes = []
    for _, count, whole in parts:
        shapes.append(block_shapes(n, whole, mem_dev * count * depth))
    shapes.append([jax.ShapeDtypeStruct((n * lev, TILE, LANES), jnp.float32)])
    outs = pl.pallas_call(
        functools.partial(forecast_kernel, parts, n),
        in_specs=[pl.BlockSpec(memory_space=pltpu.HBM)] * 6,
        out_specs=[VMEM for group in shapes for _ in group],
        out_shape=[shape for group in shapes for shape in group],
        scratch_shapes=[
            pltpu.VMEM((slab_dev, mem_dev, ny, nx), jnp.float32),
            pltpu.VMEM(cv.shape, jnp.float32),
            pltpu.VMEM(ch.shape, jnp.float32),
            pltpu.SMEM(cells.shape, jnp.int32),
            pltpu.SMEM(slabs.shape, jnp.int32),
            pltpu.SMEM(spread.shape, jnp.float32),
            pltpu.VMEM((slab_dev * mem_dev, ny * nx // LANES, LANES), jnp.float32),
            pltpu.VMEM((mem_dev, cells.size, LANES), jnp.float32),
            pltpu.SemaphoreType.DMA((3, slab_dev)),
            pltpu.SemaphoreType.DMA((3,)),
        ],
        cost_estimate=cost(60 * x.size, 4 * (2 * x.size + 2 * cv.size)),
        compiler_params=params(),
        name="forecast",
    )(*[pltpu.with_memory_space_constraint(a, pltpu.HBM) for a in (cells, slabs, spread, x, cv, ch)])
    sends = []
    for group in shapes:
        sends.append(list(outs[: len(group)]))
        outs = outs[len(group) :]
    return sends


def taper_kernel(nx, block, cells_ref, out_ref):
    depth = out_ref.shape[1]
    at = lax.broadcasted_iota(jnp.int32, (depth, LANES), 0)
    row = (lax.axis_index("mem") * block + at % block).astype(jnp.float32)
    col = (at // block * LANES + lax.broadcasted_iota(jnp.int32, (depth, LANES), 1)).astype(
        jnp.float32
    )

    def one(k, carry):
        cell = place(cells_ref, k)
        out_ref[k] = taper(
            row - (cell // nx).astype(jnp.float32), col - (cell % nx).astype(jnp.float32)
        )
        return carry

    lax.fori_loop(0, out_ref.shape[0], one, 0)


def taper_table(nx, block, cells):
    depth = block * nx // LANES
    total = cells.size
    return pl.pallas_call(
        functools.partial(taper_kernel, nx, block),
        in_specs=[SMEM],
        out_specs=VMEM,
        out_shape=jax.ShapeDtypeStruct((total, depth, LANES), jnp.float32),
        cost_estimate=cost(60 * total * depth * LANES, 4 * total * depth * LANES),
        compiler_params=params(),
        name="taper_table",
    )(cells)


def plan_kernel(nx, members, cells_ref, values_ref, errors_ref, seen_ref, anom_ref, incr_ref):
    total = cells_ref.shape[0] * cells_ref.shape[1]
    per = seen_ref.shape[0] * TILE // members
    rows = []
    for g in range(members // TILE):
        tile = seen_ref[g * per]
        for i in range(1, per):
            tile = tile + seen_ref[g * per + i]
        rows.append(tile)
    rows = jnp.concatenate(rows)
    lane = lax.broadcasted_iota(jnp.int32, (1, LANES), 1)
    row_of = jnp.zeros((1, LANES), jnp.float32)
    col_of = jnp.zeros((1, LANES), jnp.float32)
    where = []
    for k in range(total):
        cell = place(cells_ref, k)
        row, col = (cell // nx).astype(jnp.float32), (cell % nx).astype(jnp.float32)
        where.append((row, col))
        row_of = jnp.where(lane == k, row, row_of)
        col_of = jnp.where(lane == k, col, col_of)
    mean = jnp.sum(rows, axis=0, keepdims=True) * (1.0 / members)
    rows = rows - mean
    for k in range(total):
        loc = taper(row_of - where[k][0], col_of - where[k][1])
        anomaly = jnp.broadcast_to(rows[:, k : k + 1], rows.shape)
        ybar = jnp.broadcast_to(mean[:, k : k + 1], mean.shape)
        variance = jnp.sum(anomaly * anomaly, axis=0, keepdims=True) / (members - 1) + 1e-06
        shared = jnp.sum(rows * anomaly, axis=0, keepdims=True)
        error, value = place(errors_ref, k), place(values_ref, k)
        scale = 1.0 / ((members - 1) * variance)
        shift = (ybar * error + value * variance) / (variance + error) - ybar
        shrink = jnp.sqrt(error / (variance + error)) - 1.0
        anom_ref[k, 0:members, :] = anomaly * scale
        incr_ref[k, 0:members, :] = shift + shrink * anomaly
        weight = loc * shared * scale
        mean = mean + weight * shift
        rows = rows + (weight * shrink) * anomaly


def filter_plan(nx, members, cells, values, errors, seen):
    total = cells.size
    table = jax.ShapeDtypeStruct((total, members + TILE, LANES), jnp.float32)
    return pl.pallas_call(
        functools.partial(plan_kernel, nx, members),
        in_specs=[SMEM] * 3 + [VMEM],
        out_specs=[VMEM, VMEM],
        out_shape=[table, table],
        cost_estimate=cost(20_000_000, 4 * 2 * total * members * LANES),
        compiler_params=params(),
        name="filter_plan",
    )(cells, values, errors, seen)


def settle_kernel(n, mem_dev, count, depth, whole, anom_ref, incr_ref, loc_ref, *refs):
    width = 1 if whole else n
    ins, outs = blocks_in(refs[:width], n, whole), blocks_in(refs[width:], n, whole)
    total = loc_ref.shape[0]
    members = n * mem_dev
    group = 2 if depth % (2 * TILE) == 0 and members <= 16 else 1
    span = group * TILE
    per_slab = depth // span

    def spread(ref, k, m):
        member = ins[m // mem_dev][1] * mem_dev + m % mem_dev
        return ref[k, pl.ds(member, TILE, stride=0), :]

    def part(i, carry):
        slab, at = i // per_slab, (i % per_slab) * span

        def spot(m, g):
            row = ((m % mem_dev) * count + slab) * depth + at + g * TILE
            return m // mem_dev, pl.ds(pl.multiple_of(row, TILE), TILE)

        xs = []
        for m in range(members):
            for g in range(group):
                src, row = spot(m, g)
                xs.append(ins[src][0][row, :])

        def step(k, xs):
            sums = [None] * group
            for m in range(members):
                a = spread(anom_ref, k, m)
                for g in range(group):
                    term = a * xs[m * group + g]
                    sums[g] = term if m == 0 else sums[g] + term
            sums = [
                s * loc_ref[k, pl.ds(pl.multiple_of(at + g * TILE, TILE), TILE), :]
                for g, s in enumerate(sums)
            ]
            new = []
            for m in range(members):
                b = spread(incr_ref, k, m)
                for g in range(group):
                    new.append(xs[m * group + g] + b * sums[g])
            return tuple(new)

        xs = lax.fori_loop(0, total, step, tuple(xs), unroll=2)
        for m in range(members):
            for g in range(group):
                src, row = spot(m, g)
                outs[src][0][row, :] = xs[m * group + g]
        return carry

    lax.fori_loop(0, count * per_slab, part, 0)


def settle(n, mem_dev, count, depth, whole, anom, incr, loc, xs):
    shapes = block_shapes(n, whole, mem_dev * count * depth)
    size = n * mem_dev * count * depth * LANES
    return pl.pallas_call(
        functools.partial(settle_kernel, n, mem_dev, count, depth, whole),
        in_specs=[VMEM] * (3 + len(xs)),
        out_specs=[VMEM] * len(shapes),
        out_shape=shapes,
        cost_estimate=cost(4 * loc.shape[0] * size, 8 * size),
        compiler_params=params(),
        name="settle",
    )(anom, incr, loc, *xs)


def assemble_kernel(n, count, whole, *refs):
    recv, out_ref, turn = refs[: 1 if whole else n], refs[-2], refs[-1]
    blocks = blocks_in(recv, n, whole)
    mem_dev, _, ny, nx = out_ref.shape
    block = ny // n
    tiles = nx // LANES
    depth = block * tiles
    slab = pl.program_id(0)
    for m in range(mem_dev):
        at = pl.multiple_of((m * count + slab) * depth, TILE)
        for t in range(tiles):
            lanes = slice(t * LANES, (t + 1) * LANES)
            lines = pl.ds(at + t * block, block)
            for j, (ref, d) in enumerate(blocks):
                if whole:
                    out_ref[m, 0, d * block : (d + 1) * block, lanes] = ref[lines, :]
                elif block % TILE == 0:
                    row = pl.multiple_of(d * block, block)
                    out_ref[m, 0, pl.ds(row, block), lanes] = ref[lines, :]
                else:
                    turn[pl.ds(j * block, block), :] = ref[lines, :]
            if block % TILE and not whole:
                for d, (_, j) in enumerate(blocks):
                    out_ref[m, 0, d * block : (d + 1) * block, lanes] = turn[
                        pl.ds(j * block, block), :
                    ]


def assemble(n, start, count, whole, recv, shape, before):
    mem_dev, _, ny, nx = shape
    extra = [] if before is None else [before]
    return pl.pallas_call(
        functools.partial(assemble_kernel, n, count, whole),
        grid=(count,),
        in_specs=[VMEM] * len(recv) + [pl.BlockSpec(memory_space=pl.ANY)] * len(extra),
        out_specs=pl.BlockSpec((mem_dev, 1, ny, nx), lambda s: (0, start + s, 0, 0)),
        out_shape=jax.ShapeDtypeStruct(shape, jnp.float32),
        scratch_shapes=[pltpu.VMEM((ny, LANES), jnp.float32)],
        input_output_aliases={} if before is None else {len(recv): 0},
        cost_estimate=cost(0, 8 * len(recv) * recv[0].size),
        compiler_params=params(),
        name="assemble",
    )(*recv, *extra)


def exchange(blocks, n, whole):
    if whole:
        return [lax.all_to_all(blocks[0], "mem", split_axis=0, concat_axis=0, tiled=True)]
    got = {}
    for j in range(n - 1, 0, -1):
        got[j] = lax.ppermute(blocks[j], "mem", [(i, i ^ j) for i in range(n)])
    return blocks[:1] + [got[j] for j in range(1, n)]


def body(x, cv, ch, spread, obs_cells, obs_slabs, obs_values, obs_error):
    mem_dev, slab_dev, ny, nx = x.shape
    n, lev = lax.axis_size("mem"), lax.axis_size("lev")
    block = ny // n
    depth = block * nx // LANES
    parts = chunks_of(slab_dev)
    sends = forecast(parts, n, lev, obs_cells, obs_slabs, spread, x, cv, ch)
    seen = lax.all_to_all(sends[-1][0], ("mem", "lev"), 0, 0, tiled=True)
    states = []
    for c, blocks in enumerate(sends[:-1]):
        states.append(exchange(blocks, n, parts[c][2]))
    loc = taper_table(nx, block, obs_cells)
    anom, incr = filter_plan(
        nx, n * mem_dev, obs_cells, obs_values, obs_error, seen
    )
    result = None
    for (start, count, whole), state in zip(parts, states):
        new = settle(n, mem_dev, count, depth, whole, anom, incr, loc, state)
        back = exchange(list(new), n, whole)
        anom, _ = lax.optimization_barrier((anom, new[0]))
        result = assemble(n, start, count, whole, back, x.shape, result)
    return result


def solution(mesh):
    in_specs = (
        P("mem", "lev", None, None),
        P("lev", None, None),
        P("lev", None, None),
        P("lev"),
        P(),
        P(),
        P(),
        P(),
    )
    out_specs = P("mem", "lev", None, None)
    return jax.shard_map(body, mesh=mesh, in_specs=in_specs, out_specs=out_specs, check_vma=False)
```

```python
import functools

import jax
import jax.numpy as jnp
from jax import lax
from jax.experimental import pallas as pl
from jax.experimental.pallas import tpu as pltpu
from jax.sharding import PartitionSpec as P


STEPS = 2
LOC_HALF = 64
LANES = 128
GRANT = 24 * 1024 * 1024
TILE = 8
VMEM = pl.BlockSpec(memory_space=pltpu.VMEM)
SMEM = pl.BlockSpec(memory_space=pltpu.SMEM)


def cost(flops, nbytes):
    return pl.CostEstimate(flops=flops, bytes_accessed=nbytes, transcendentals=0)


def taper(row_gap, col_gap):
    scaled = jnp.sqrt(row_gap * row_gap + col_gap * col_gap) * (1.0 / LOC_HALF)
    inner = (
        ((-0.25 * scaled + 0.5) * scaled + 0.625) * scaled - 5.0 / 3.0
    ) * scaled * scaled + 1.0
    safe = jnp.maximum(scaled, 1.0)
    outer = (
        ((((scaled * (1.0 / 12.0) - 0.5) * scaled + 0.625) * scaled + 5.0 / 3.0) * scaled - 5.0)
        * scaled
        + 4.0
        - (2.0 / 3.0) / safe
    )
    return jnp.where(scaled <= 1.0, inner, jnp.where(scaled < 2.0, outer, 0.0))


def chunks_of(slab_dev):
    first = max(1, (3 * slab_dev) // 5)
    if slab_dev == 1:
        return ((0, 1, False),)
    return ((0, first, False), (first, slab_dev - first, True))


def place(ref, k):
    return ref[k // ref.shape[1], k % ref.shape[1]]


def params():
    return pltpu.CompilerParams(vmem_limit_bytes=GRANT)


def blocks_in(refs, n, whole):
    me = lax.axis_index("mem")
    if whole:
        return [(refs[0].at[d], d) for d in range(n)]
    return [(refs[j], me ^ j) for j in range(n)]


def block_shapes(n, whole, rows):
    if whole:
        return [jax.ShapeDtypeStruct((n, rows, LANES), jnp.float32)]
    return [jax.ShapeDtypeStruct((rows, LANES), jnp.float32)] * n


def forecast_kernel(parts, n, cells_hbm, slabs_hbm, spread_hbm, x_hbm, cv_hbm, ch_hbm, *rest):
    outs = []
    for start, count, whole in parts:
        width = 1 if whole else n
        outs.append(blocks_in(rest[:width], n, whole))
        rest = rest[width:]
    seen_ref, rest = rest[0], rest[1:]
    x_buf, cv_buf, ch_buf, cells, slabs, spread, field, picks, sem, small = rest
    slab_dev, mem_dev, ny, nx = x_buf.shape
    block = ny // n
    tiles = nx // LANES
    depth = block * tiles
    total = cells.shape[0] * cells.shape[1]

    def loads(s):
        return (
            pltpu.make_async_copy(x_hbm.at[:, s], x_buf.at[s], sem.at[0, s]),
            pltpu.make_async_copy(cv_hbm.at[s], cv_buf.at[s], sem.at[1, s]),
            pltpu.make_async_copy(ch_hbm.at[s], ch_buf.at[s], sem.at[2, s]),
        )

    lists = (
        pltpu.make_async_copy(spread_hbm, spread, small.at[0]),
        pltpu.make_async_copy(cells_hbm, cells, small.at[1]),
        pltpu.make_async_copy(slabs_hbm, slabs, small.at[2]),
    )
    for copy in lists:
        copy.start()
    for s in range(slab_dev):
        for copy in loads(s):
            copy.start()
    for copy in lists:
        copy.wait()
    rows = lax.broadcasted_iota(jnp.int32, (ny, nx), 0)
    cols = lax.broadcasted_iota(jnp.int32, (ny, nx), 1)

    for (start, count, whole), blocks in zip(parts, outs):

        def one(s, carry):
            slab = start + s
            for copy in loads(slab):
                copy.wait()
            diffuse = spread[slab]
            half_v = 0.5 * cv_buf[slab]
            half_h = 0.5 * ch_buf[slab]
            east_w, west_w = diffuse - half_v, diffuse + half_v
            north_w, south_w = diffuse - half_h, diffuse + half_h
            for m in range(mem_dev):
                f = x_buf[slab, m]
                for _ in range(STEPS):
                    east = jnp.where(cols == nx - 1, f, pltpu.roll(f, nx - 1, 1))
                    west = jnp.where(cols == 0, f, pltpu.roll(f, 1, 1))
                    north = jnp.where(rows == ny - 1, f, pltpu.roll(f, ny - 1, 0))
                    south = jnp.where(rows == 0, f, pltpu.roll(f, 1, 0))
                    f = (
                        (1.0 - 4.0 * diffuse) * f
                        + east_w * east
                        + west_w * west
                        + north_w * north
                        + south_w * south
                    )
                for t in range(tiles):
                    field[slab * mem_dev + m, pl.ds(t * ny, ny), :] = f[
                        :, t * LANES : (t + 1) * LANES
                    ]
                at = pl.multiple_of((m * count + s) * depth, TILE)
                for ref, d in blocks:
                    for t in range(tiles):
                        row = t * ny + d * block
                        if not whole:
                            row = pl.multiple_of(row, block)
                        ref[pl.ds(at + t * block, block), :] = field[
                            slab * mem_dev + m, pl.ds(row, block), :
                        ]
            return carry

        lax.fori_loop(0, count, one, 0)

    lane = lax.broadcasted_iota(jnp.int32, (1, LANES), 1)
    for k in range(total):
        cell = place(cells, k)
        row, col = cell // nx, cell % nx
        off = place(slabs, k) - lax.axis_index("lev") * slab_dev
        inside = (off >= 0) & (off < slab_dev)
        wanted = jnp.where(inside, col % LANES, LANES)
        off = jnp.clip(off, 0, slab_dev - 1)
        for m in range(mem_dev):
            line = field[off * mem_dev + m, pl.ds((col // LANES) * ny + row, 1), :]
            picks[m, pl.ds(k, 1), :] = jnp.where(lane == wanted, line, 0.0)
    diagonal = lax.broadcasted_iota(jnp.int32, (total, LANES), 0) == lax.broadcasted_iota(
        jnp.int32, (total, LANES), 1
    )
    line = lax.broadcasted_iota(jnp.int32, (TILE, LANES), 0)
    seen = jnp.zeros((TILE, LANES), jnp.float32)
    for m in range(mem_dev):
        value = jnp.sum(picks[m], axis=1, keepdims=True)
        value = jnp.sum(jnp.where(diagonal, value, 0.0), axis=0, keepdims=True)
        seen = jnp.where(line == (lax.axis_index("mem") * mem_dev + m) % TILE, value, seen)
    for d in range(seen_ref.shape[0]):
        seen_ref[d] = seen


def forecast(parts, n, cells, slabs, spread, x, cv, ch):
    mem_dev, slab_dev, ny, nx = x.shape
    depth = ny // n * nx // LANES
    shapes = []
    for _, count, whole in parts:
        shapes.append(block_shapes(n, whole, mem_dev * count * depth))
    shapes.append([jax.ShapeDtypeStruct((n, TILE, LANES), jnp.float32)])
    outs = pl.pallas_call(
        functools.partial(forecast_kernel, parts, n),
        in_specs=[pl.BlockSpec(memory_space=pltpu.HBM)] * 6,
        out_specs=[VMEM for group in shapes for _ in group],
        out_shape=[shape for group in shapes for shape in group],
        scratch_shapes=[
            pltpu.VMEM((slab_dev, mem_dev, ny, nx), jnp.float32),
            pltpu.VMEM(cv.shape, jnp.float32),
            pltpu.VMEM(ch.shape, jnp.float32),
            pltpu.SMEM(cells.shape, jnp.int32),
            pltpu.SMEM(slabs.shape, jnp.int32),
            pltpu.SMEM(spread.shape, jnp.float32),
            pltpu.VMEM((slab_dev * mem_dev, ny * nx // LANES, LANES), jnp.float32),
            pltpu.VMEM((mem_dev, cells.size, LANES), jnp.float32),
            pltpu.SemaphoreType.DMA((3, slab_dev)),
            pltpu.SemaphoreType.DMA((3,)),
        ],
        cost_estimate=cost(60 * x.size, 4 * (2 * x.size + 2 * cv.size)),
        compiler_params=params(),
        name="forecast",
    )(*[pltpu.with_memory_space_constraint(a, pltpu.HBM) for a in (cells, slabs, spread, x, cv, ch)])
    sends = []
    for group in shapes:
        sends.append(list(outs[: len(group)]))
        outs = outs[len(group) :]
    return sends


def plan_kernel(nx, block, cells_ref, values_ref, errors_ref, *refs):
    seen_refs, (anom_ref, incr_ref, loc_ref) = refs[:-3], refs[-3:]
    total = cells_ref.shape[0] * cells_ref.shape[1]
    rows = seen_refs[0][...]
    for other in seen_refs[1:]:
        rows = rows + other[...]
    members = rows.shape[0]
    depth = loc_ref.shape[1]
    at = lax.broadcasted_iota(jnp.int32, (depth, LANES), 0)
    cell_row = (lax.axis_index("mem") * block + at % block).astype(jnp.float32)
    cell_col = (
        at // block * LANES + lax.broadcasted_iota(jnp.int32, (depth, LANES), 1)
    ).astype(jnp.float32)
    lane = lax.broadcasted_iota(jnp.int32, (1, LANES), 1)
    row_of = jnp.zeros((1, LANES), jnp.float32)
    col_of = jnp.zeros((1, LANES), jnp.float32)
    where = []
    for k in range(total):
        cell = place(cells_ref, k)
        row, col = (cell // nx).astype(jnp.float32), (cell % nx).astype(jnp.float32)
        where.append((row, col))
        row_of = jnp.where(lane == k, row, row_of)
        col_of = jnp.where(lane == k, col, col_of)
    mean = jnp.sum(rows, axis=0, keepdims=True) * (1.0 / members)
    rows = rows - mean
    for k in range(total):
        loc_ref[k] = taper(cell_row - where[k][0], cell_col - where[k][1])
        loc = taper(row_of - where[k][0], col_of - where[k][1])
        anomaly = jnp.broadcast_to(rows[:, k : k + 1], rows.shape)
        ybar = jnp.broadcast_to(mean[:, k : k + 1], mean.shape)
        variance = jnp.sum(anomaly * anomaly, axis=0, keepdims=True) / (members - 1) + 1e-06
        shared = jnp.sum(rows * anomaly, axis=0, keepdims=True)
        error, value = place(errors_ref, k), place(values_ref, k)
        scale = 1.0 / ((members - 1) * variance)
        shift = (ybar * error + value * variance) / (variance + error) - ybar
        shrink = jnp.sqrt(error / (variance + error)) - 1.0
        anom_ref[k, 0:members, :] = anomaly * scale
        incr_ref[k, 0:members, :] = shift + shrink * anomaly
        weight = loc * shared * scale
        mean = mean + weight * shift
        rows = rows + (weight * shrink) * anomaly


def filter_plan(nx, block, cells, values, errors, seen):
    members = seen[0].shape[0]
    total = cells.size
    depth = block * nx // LANES
    table = jax.ShapeDtypeStruct((total, members + TILE, LANES), jnp.float32)
    tapers = jax.ShapeDtypeStruct((total, depth, LANES), jnp.float32)
    return pl.pallas_call(
        functools.partial(plan_kernel, nx, block),
        in_specs=[SMEM] * 3 + [VMEM] * len(seen),
        out_specs=[VMEM] * 3,
        out_shape=[table, table, tapers],
        cost_estimate=cost(20_000_000, 4 * total * (2 * members + depth) * LANES),
        compiler_params=params(),
        name="filter_plan",
    )(cells, values, errors, *seen)


def settle_kernel(n, mem_dev, count, depth, whole, anom_ref, incr_ref, loc_ref, *refs):
    width = 1 if whole else n
    ins, outs = blocks_in(refs[:width], n, whole), blocks_in(refs[width:], n, whole)
    total = loc_ref.shape[0]
    members = n * mem_dev
    group = 2 if depth % (2 * TILE) == 0 and members <= 16 else 1
    span = group * TILE
    per_slab = depth // span

    def spread(ref, k, m):
        member = ins[m // mem_dev][1] * mem_dev + m % mem_dev
        return ref[k, pl.ds(member, TILE, stride=0), :]

    def part(i, carry):
        slab, at = i // per_slab, (i % per_slab) * span

        def spot(m, g):
            row = ((m % mem_dev) * count + slab) * depth + at + g * TILE
            return m // mem_dev, pl.ds(pl.multiple_of(row, TILE), TILE)

        xs = []
        for m in range(members):
            for g in range(group):
                src, row = spot(m, g)
                xs.append(ins[src][0][row, :])

        def step(k, xs):
            sums = [None] * group
            for m in range(members):
                a = spread(anom_ref, k, m)
                for g in range(group):
                    term = a * xs[m * group + g]
                    sums[g] = term if m == 0 else sums[g] + term
            sums = [
                s * loc_ref[k, pl.ds(pl.multiple_of(at + g * TILE, TILE), TILE), :]
                for g, s in enumerate(sums)
            ]
            new = []
            for m in range(members):
                b = spread(incr_ref, k, m)
                for g in range(group):
                    new.append(xs[m * group + g] + b * sums[g])
            return tuple(new)

        xs = lax.fori_loop(0, total, step, tuple(xs), unroll=2)
        for m in range(members):
            for g in range(group):
                src, row = spot(m, g)
                outs[src][0][row, :] = xs[m * group + g]
        return carry

    lax.fori_loop(0, count * per_slab, part, 0)


def settle(n, mem_dev, count, depth, whole, anom, incr, loc, xs):
    shapes = block_shapes(n, whole, mem_dev * count * depth)
    size = n * mem_dev * count * depth * LANES
    return pl.pallas_call(
        functools.partial(settle_kernel, n, mem_dev, count, depth, whole),
        in_specs=[VMEM] * (3 + len(xs)),
        out_specs=[VMEM] * len(shapes),
        out_shape=shapes,
        cost_estimate=cost(4 * loc.shape[0] * size, 8 * size),
        compiler_params=params(),
        name="settle",
    )(anom, incr, loc, *xs)


def assemble_kernel(n, count, whole, *refs):
    recv, out_ref, turn = refs[: 1 if whole else n], refs[-2], refs[-1]
    blocks = blocks_in(recv, n, whole)
    mem_dev, _, ny, nx = out_ref.shape
    block = ny // n
    tiles = nx // LANES
    depth = block * tiles
    slab = pl.program_id(0)
    for m in range(mem_dev):
        at = pl.multiple_of((m * count + slab) * depth, TILE)
        for t in range(tiles):
            lanes = slice(t * LANES, (t + 1) * LANES)
            lines = pl.ds(at + t * block, block)
            for j, (ref, d) in enumerate(blocks):
                if whole:
                    out_ref[m, 0, d * block : (d + 1) * block, lanes] = ref[lines, :]
                elif block % TILE == 0:
                    row = pl.multiple_of(d * block, block)
                    out_ref[m, 0, pl.ds(row, block), lanes] = ref[lines, :]
                else:
                    turn[pl.ds(j * block, block), :] = ref[lines, :]
            if block % TILE and not whole:
                for d, (_, j) in enumerate(blocks):
                    out_ref[m, 0, d * block : (d + 1) * block, lanes] = turn[
                        pl.ds(j * block, block), :
                    ]


def assemble(n, start, count, whole, recv, shape, before):
    mem_dev, _, ny, nx = shape
    extra = [] if before is None else [before]
    return pl.pallas_call(
        functools.partial(assemble_kernel, n, count, whole),
        grid=(count,),
        in_specs=[VMEM] * len(recv) + [pl.BlockSpec(memory_space=pl.ANY)] * len(extra),
        out_specs=pl.BlockSpec((mem_dev, 1, ny, nx), lambda s: (0, start + s, 0, 0)),
        out_shape=jax.ShapeDtypeStruct(shape, jnp.float32),
        scratch_shapes=[pltpu.VMEM((ny, LANES), jnp.float32)],
        input_output_aliases={} if before is None else {len(recv): 0},
        cost_estimate=cost(0, 8 * len(recv) * recv[0].size),
        compiler_params=params(),
        name="assemble",
    )(*recv, *extra)


def exchange(blocks, n, whole):
    if whole:
        return [lax.all_to_all(blocks[0], "mem", split_axis=0, concat_axis=0, tiled=True)]
    got = {}
    for j in range(n - 1, 0, -1):
        got[j] = lax.ppermute(blocks[j], "mem", [(i, i ^ j) for i in range(n)])
    return blocks[:1] + [got[j] for j in range(1, n)]


def body(x, cv, ch, spread, obs_cells, obs_slabs, obs_values, obs_error):
    mem_dev, slab_dev, ny, nx = x.shape
    n, lev = lax.axis_size("mem"), lax.axis_size("lev")
    block = ny // n
    depth = block * nx // LANES
    parts = chunks_of(slab_dev)
    sends = forecast(parts, n, obs_cells, obs_slabs, spread, x, cv, ch)
    seen = lax.all_to_all(sends[-1][0], "mem", 0, 0, tiled=True)
    states = []
    for c, blocks in enumerate(sends[:-1]):
        states.append(exchange(blocks, n, parts[c][2]))
    per = TILE // mem_dev
    seen = seen.reshape(n // per, per, TILE, LANES).sum(axis=1).reshape(-1, LANES)
    tiles = [seen] + [
        lax.ppermute(seen, "lev", [(i, (i + d) % lev) for i in range(lev)])
        for d in range(1, lev)
    ]
    anom, incr, loc = filter_plan(nx, block, obs_cells, obs_values, obs_error, tiles)
    result = None
    for (start, count, whole), state in zip(parts, states):
        new = settle(n, mem_dev, count, depth, whole, anom, incr, loc, state)
        back = exchange(list(new), n, whole)
        anom, _ = lax.optimization_barrier((anom, new[0]))
        result = assemble(n, start, count, whole, back, x.shape, result)
    return result


def solution(mesh):
    in_specs = (
        P("mem", "lev", None, None),
        P("lev", None, None),
        P("lev", None, None),
        P("lev"),
        P(),
        P(),
        P(),
        P(),
    )
    out_specs = P("mem", "lev", None, None)
    return jax.shard_map(body, mesh=mesh, in_specs=in_specs, out_specs=out_specs, check_vma=False)
```

```python
import functools

import jax
import jax.numpy as jnp
from jax import lax
from jax.experimental import pallas as pl
from jax.experimental.pallas import tpu as pltpu
from jax.sharding import PartitionSpec as P


STEPS = 2
LOC_HALF = 64
LANES = 128
GRANT = 24 * 1024 * 1024
TILE = 8
VMEM = pl.BlockSpec(memory_space=pltpu.VMEM)
SMEM = pl.BlockSpec(memory_space=pltpu.SMEM)


def cost(flops, nbytes):
    return pl.CostEstimate(flops=flops, bytes_accessed=nbytes, transcendentals=0)


def taper(row_gap, col_gap):
    scaled = jnp.sqrt(row_gap * row_gap + col_gap * col_gap) * (1.0 / LOC_HALF)
    inner = (
        ((-0.25 * scaled + 0.5) * scaled + 0.625) * scaled - 5.0 / 3.0
    ) * scaled * scaled + 1.0
    safe = jnp.maximum(scaled, 1.0)
    outer = (
        ((((scaled * (1.0 / 12.0) - 0.5) * scaled + 0.625) * scaled + 5.0 / 3.0) * scaled - 5.0)
        * scaled
        + 4.0
        - (2.0 / 3.0) / safe
    )
    return jnp.where(scaled <= 1.0, inner, jnp.where(scaled < 2.0, outer, 0.0))


def chunks_of(slab_dev):
    first = max(1, (2 * slab_dev) // 5)
    if slab_dev == 1:
        return ((0, 1, False),)
    return ((0, first, False), (first, slab_dev - first, True))


def row_col(cell, nx):
    if nx & (nx - 1):
        return cell // nx, cell % nx
    return lax.shift_right_logical(cell, nx.bit_length() - 1), cell & (nx - 1)


def place(ref, k):
    return ref[k // ref.shape[1], k % ref.shape[1]]


def params():
    return pltpu.CompilerParams(vmem_limit_bytes=GRANT)


def blocks_in(refs, n, whole):
    me = lax.axis_index("mem")
    return [(refs[0].at[me ^ j] if whole else refs[j], me ^ j) for j in range(n)]


def block_shapes(n, whole, rows):
    if whole:
        return [jax.ShapeDtypeStruct((n, rows, LANES), jnp.float32)]
    return [jax.ShapeDtypeStruct((rows, LANES), jnp.float32)] * n


def forecast_kernel(parts, n, cells_hbm, slabs_hbm, spread_hbm, x_hbm, cv_hbm, ch_hbm, *rest):
    outs = []
    for start, count, whole in parts:
        width = 1 if whole else n
        outs.append(blocks_in(rest[:width], n, whole))
        rest = rest[width:]
    x_buf, cv_buf, ch_buf, cells, slabs, spread, field, half, weights, picks, sem, small = rest
    slab_dev, mem_dev, ny, nx = x_buf.shape
    block = ny // n
    tiles = nx // LANES
    depth = block * tiles
    total = cells.shape[0] * cells.shape[1]

    def loads(s):
        return (
            pltpu.make_async_copy(x_hbm.at[:, s], x_buf.at[s], sem.at[0, s]),
            pltpu.make_async_copy(cv_hbm.at[s], cv_buf.at[s], sem.at[1, s]),
            pltpu.make_async_copy(ch_hbm.at[s], ch_buf.at[s], sem.at[2, s]),
        )

    lists = (
        pltpu.make_async_copy(spread_hbm, spread, small.at[0]),
        pltpu.make_async_copy(cells_hbm, cells, small.at[1]),
        pltpu.make_async_copy(slabs_hbm, slabs, small.at[2]),
    )
    for copy in lists:
        copy.start()
    for s in range(slab_dev):
        for copy in loads(s):
            copy.start()
    for copy in lists:
        copy.wait()
    sub = lax.broadcasted_iota(jnp.int32, (TILE, LANES), 0)
    lane = lax.broadcasted_iota(jnp.int32, (TILE, LANES), 1)
    east_edge, west_edge = lane == LANES - 1, lane == 0
    north_edge, south_edge = sub == TILE - 1, sub == 0
    high = ny // TILE

    def spot(r, t):
        return slice(t * ny + r * TILE, t * ny + (r + 1) * TILE)

    def advance(load, keep, store):
        known = {}

        def turned(r, t, by, axis):
            key = (r, t, by, axis)
            if key not in known:
                known[key] = pltpu.roll(load(r, t), by, axis)
            return known[key]

        def beyond(inside, r, t, by, axis, here):
            return turned(r, t, by, axis) if inside else here

        for r in range(high):
            for t in range(tiles):
                f = load(r, t)
                east = jnp.where(
                    east_edge,
                    beyond(t + 1 < tiles, r, t + 1, LANES - 1, 1, f),
                    turned(r, t, LANES - 1, 1),
                )
                west = jnp.where(
                    west_edge, beyond(t > 0, r, t - 1, 1, 1, f), turned(r, t, 1, 1)
                )
                north = jnp.where(
                    north_edge,
                    beyond(r + 1 < high, r + 1, t, TILE - 1, 0, f),
                    turned(r, t, TILE - 1, 0),
                )
                south = jnp.where(
                    south_edge, beyond(r > 0, r - 1, t, 1, 0, f), turned(r, t, 1, 0)
                )
                at = spot(r, t)
                store(
                    r,
                    t,
                    (keep * f + weights[0, at, :] * east)
                    + (weights[1, at, :] * west + weights[2, at, :] * north)
                    + weights[3, at, :] * south,
                )

    for (start, count, whole), blocks in zip(parts, outs):

        def one(s, carry):
            slab = start + s
            for copy in loads(slab):
                copy.wait()
            diffuse = spread[slab]
            keep = 1.0 - 4.0 * diffuse
            for r in range(high):
                for t in range(tiles):
                    tile = (slice(r * TILE, (r + 1) * TILE), slice(t * LANES, (t + 1) * LANES))
                    half_v, half_h = 0.5 * cv_buf[slab, *tile], 0.5 * ch_buf[slab, *tile]
                    weights[0, spot(r, t), :] = diffuse - half_v
                    weights[1, spot(r, t), :] = diffuse + half_v
                    weights[2, spot(r, t), :] = diffuse - half_h
                    weights[3, spot(r, t), :] = diffuse + half_h
            for m in range(mem_dev):
                level = slab * mem_dev + m

                def first(r, t):
                    return x_buf[
                        slab, m, r * TILE : (r + 1) * TILE, t * LANES : (t + 1) * LANES
                    ]

                def later(r, t):
                    return half[spot(r, t), :]

                def between(r, t, value):
                    half[spot(r, t), :] = value

                def final(r, t, value):
                    field[level, spot(r, t), :] = value

                for step in range(STEPS):
                    advance(
                        later if step else first, keep, between if step < STEPS - 1 else final
                    )
                at = pl.multiple_of((m * count + s) * depth, TILE)
                for ref, d in blocks:
                    for t in range(tiles):
                        row = pl.multiple_of(t * ny + d * block, block)
                        ref[pl.ds(at + t * block, block), :] = field[level, pl.ds(row, block), :]
            return carry

        lax.fori_loop(0, count, one, 0)

    lane = lax.broadcasted_iota(jnp.int32, (1, LANES), 1)
    for k in range(total):
        cell = place(cells, k)
        row, col = row_col(cell, nx)
        off = place(slabs, k) - lax.axis_index("lev") * slab_dev
        inside = (off >= 0) & (off < slab_dev)
        across, wanted = row_col(col, LANES)
        wanted = jnp.where(inside, wanted, LANES)
        off = jnp.where(inside, off, 0)
        for m in range(mem_dev):
            line = field[off * mem_dev + m, pl.ds(across * ny + row, 1), :]
            picks[m, pl.ds(k, 1), :] = jnp.where(lane == wanted, line, 0.0)
    diagonal = lax.broadcasted_iota(jnp.int32, (total, LANES), 0) == lax.broadcasted_iota(
        jnp.int32, (total, LANES), 1
    )
    values = []
    for m in range(mem_dev):
        value = jnp.sum(picks[m], axis=1, keepdims=True)
        values.append(jnp.sum(jnp.where(diagonal, value, 0.0), axis=0, keepdims=True))
    for j in range(n):
        seen = jnp.zeros((TILE, LANES), jnp.float32)
        for m in range(mem_dev):
            seen = jnp.where(sub == (j * mem_dev + m) % TILE, values[m], seen)
        outs[0][j][0][pl.ds(mem_dev * parts[0][1] * depth, TILE), :] = seen


def forecast(parts, n, cells, slabs, spread, x, cv, ch):
    mem_dev, slab_dev, ny, nx = x.shape
    depth = ny // n * nx // LANES
    shapes = []
    for i, (_, count, whole) in enumerate(parts):
        shapes.append(block_shapes(n, whole, mem_dev * count * depth + (0 if i else TILE)))
    outs = pl.pallas_call(
        functools.partial(forecast_kernel, parts, n),
        in_specs=[pl.BlockSpec(memory_space=pltpu.HBM)] * 6,
        out_specs=[VMEM for group in shapes for _ in group],
        out_shape=[shape for group in shapes for shape in group],
        scratch_shapes=[
            pltpu.VMEM((slab_dev, mem_dev, ny, nx), jnp.float32),
            pltpu.VMEM(cv.shape, jnp.float32),
            pltpu.VMEM(ch.shape, jnp.float32),
            pltpu.SMEM(cells.shape, jnp.int32),
            pltpu.SMEM(slabs.shape, jnp.int32),
            pltpu.SMEM(spread.shape, jnp.float32),
            pltpu.VMEM((slab_dev * mem_dev, ny * nx // LANES, LANES), jnp.float32),
            pltpu.VMEM((ny * nx // LANES, LANES), jnp.float32),
            pltpu.VMEM((4, ny * nx // LANES, LANES), jnp.float32),
            pltpu.VMEM((mem_dev, cells.size, LANES), jnp.float32),
            pltpu.SemaphoreType.DMA((3, slab_dev)),
            pltpu.SemaphoreType.DMA((3,)),
        ],
        cost_estimate=cost(60 * x.size, 4 * (2 * x.size + 2 * cv.size)),
        compiler_params=params(),
        name="forecast",
    )(*[pltpu.with_memory_space_constraint(a, pltpu.HBM) for a in (cells, slabs, spread, x, cv, ch)])
    sends = []
    for group in shapes:
        sends.append(list(outs[: len(group)]))
        outs = outs[len(group) :]
    return sends


def reach(cells, lists, nx, block, groups):
    total = cells.shape[0] * cells.shape[1]
    me = lax.axis_index("mem")
    for g in range(groups):
        count = jnp.int32(0)
        low_col = g * TILE // block * LANES
        high_col = (g * TILE + TILE - 1) // block * LANES + LANES - 1
        low_row = me * block + g * TILE % block
        high_row = low_row + min(block, TILE) - 1
        for k in range(total):
            row, col = row_col(place(cells, k), nx)
            down = jnp.maximum(jnp.maximum(low_row - row, row - high_row), 0)
            across = jnp.maximum(jnp.maximum(low_col - col, col - high_col), 0)
            lists[g, count] = jnp.int32(k)
            near = down * down + across * across < (2 * LOC_HALF) ** 2
            count = count + near.astype(jnp.int32)
        lists[g, count] = jnp.int32(total)
        lists[g, total + 1] = count


def settle_blocks(n, mem_dev, count, depth, lists, anom_ref, incr_ref, loc_ref, ins, outs):
    total = loc_ref.shape[0] - 1
    members = n * mem_dev
    group = max(g for g in range(1, count + 1) if count % g == 0 and (g == 1 or g * members <= 48))
    turns = count // group

    def spread(ref, k, m):
        return ref[k, pl.ds(m, TILE, stride=0), :]

    def part(i, carry):
        tile, slab = i // turns, i % turns * group
        at = tile * TILE

        def spot(m, g):
            row = ((m % mem_dev) * count + slab + g) * depth + at
            return m // mem_dev, pl.ds(pl.multiple_of(row, TILE), TILE)

        xs = []
        for m in range(members):
            for g in range(group):
                src, row = spot(m, g)
                xs.append(ins[src][0][row, :])

        def step(k, xs):
            terms = [[] for _ in range(group)]
            for m in range(members):
                a = spread(anom_ref, k, m)
                for g in range(group):
                    terms[g].append(a * xs[m * group + g])
            loc = loc_ref[k, pl.ds(pl.multiple_of(at, TILE), TILE), :]
            for g in range(group):
                while len(terms[g]) > 1:
                    odd = terms[g][len(terms[g]) // 2 * 2 :]
                    terms[g] = [a + b for a, b in zip(terms[g][::2], terms[g][1::2])] + odd
            sums = [terms[g][0] * loc for g in range(group)]
            new = []
            for m in range(members):
                b = spread(incr_ref, k, m)
                for g in range(group):
                    new.append(xs[m * group + g] + b * sums[g])
            return new

        def two(i, xs):
            return tuple(step(lists[tile, 2 * i + 1], step(lists[tile, 2 * i], list(xs))))

        xs = lax.fori_loop(
            0, lax.shift_right_logical(lists[tile, total + 1] + 1, 1), two, tuple(xs)
        )
        for m in range(members):
            for g in range(group):
                src, row = spot(m, g)
                outs[src][0][row, :] = xs[m * group + g]
        return carry

    lax.fori_loop(0, depth // TILE * turns, part, 0)


def plan_kernel(nx, block, n, mem_dev, count, lev, cells, values_ref, errors_ref, *refs):
    seen_refs, refs = refs[:lev], refs[lev:]
    ins, refs = blocks_in(refs[:n], n, False), refs[n:]
    anom_ref, incr_ref, loc_ref = refs[:3]
    outs, lists = blocks_in(refs[3 : 3 + n], n, False), refs[3 + n]
    total = cells.shape[0] * cells.shape[1]
    rows = seen_refs[0][...]
    for other in seen_refs[1:]:
        rows = rows + other[...]
    members = rows.shape[0]
    depth = loc_ref.shape[1]
    at = lax.broadcasted_iota(jnp.int32, (depth, LANES), 0)
    cell_row = (lax.axis_index("mem") * block + at % block).astype(jnp.float32)
    cell_col = (
        at // block * LANES + lax.broadcasted_iota(jnp.int32, (depth, LANES), 1)
    ).astype(jnp.float32)
    lane = lax.broadcasted_iota(jnp.int32, (1, LANES), 1)
    row_of = jnp.zeros((1, LANES), jnp.float32)
    col_of = jnp.zeros((1, LANES), jnp.float32)
    where = []
    for k in range(total):
        row, col = row_col(place(cells, k), nx)
        row, col = row.astype(jnp.float32), col.astype(jnp.float32)
        where.append((row, col))
        row_of = jnp.where(lane == k, row, row_of)
        col_of = jnp.where(lane == k, col, col_of)
    mean = jnp.sum(rows, axis=0, keepdims=True) * (1.0 / members)
    rows = rows - mean
    for k in range(total):
        loc_ref[k] = taper(cell_row - where[k][0], cell_col - where[k][1])
        loc = taper(row_of - where[k][0], col_of - where[k][1])
        anomaly = jnp.broadcast_to(rows[:, k : k + 1], rows.shape)
        ybar = jnp.broadcast_to(mean[:, k : k + 1], mean.shape)
        variance = jnp.sum(anomaly * anomaly, axis=0, keepdims=True) / (members - 1) + 1e-06
        shared = jnp.sum(rows * anomaly, axis=0, keepdims=True)
        error, value = place(errors_ref, k), place(values_ref, k)
        scale = 1.0 / ((members - 1) * variance)
        shift = (ybar * error + value * variance) / (variance + error) - ybar
        shrink = jnp.sqrt(error / (variance + error)) - 1.0
        anom_ref[k, 0:members, :] = anomaly * scale
        incr_ref[k, 0:members, :] = shift + shrink * anomaly
        weight = loc * shared * scale
        mean = mean + weight * shift
        rows = rows + (weight * shrink) * anomaly
    anom_ref[total] = jnp.zeros(anom_ref.shape[1:], jnp.float32)
    incr_ref[total] = jnp.zeros(incr_ref.shape[1:], jnp.float32)
    loc_ref[total] = jnp.zeros(loc_ref.shape[1:], jnp.float32)
    reach(cells, lists, nx, block, depth // TILE)
    settle_blocks(n, mem_dev, count, depth, lists, anom_ref, incr_ref, loc_ref, ins, outs)


def filter_plan(nx, block, mem_dev, count, cells, values, errors, seen, xs):
    members = seen[0].shape[0]
    n = len(xs)
    total = cells.size
    depth = block * nx // LANES
    table = jax.ShapeDtypeStruct((total + 1, members + TILE, LANES), jnp.float32)
    tapers = jax.ShapeDtypeStruct((total + 1, depth, LANES), jnp.float32)
    shapes = [table, table, tapers] + block_shapes(n, False, mem_dev * count * depth)
    got = pl.pallas_call(
        functools.partial(plan_kernel, nx, block, n, mem_dev, count, len(seen)),
        in_specs=[SMEM] * 3 + [VMEM] * (len(seen) + n),
        out_specs=[VMEM] * len(shapes),
        out_shape=shapes,
        scratch_shapes=[pltpu.SMEM((depth // TILE, total + 2), jnp.int32)],
        cost_estimate=cost(20_000_000, 4 * total * (2 * members + depth) * LANES),
        compiler_params=params(),
        name="filter_plan",
    )(cells, values, errors, *seen, *xs)
    return got[:3], list(got[3:])


def settle_kernel(nx, block, n, mem_dev, count, depth, whole, cells, anom, incr, loc, *refs):
    width = 1 if whole else n
    ins, outs = blocks_in(refs[:width], n, whole), blocks_in(refs[width:-1], n, False)
    lists = refs[-1]
    reach(cells, lists, nx, block, depth // TILE)
    settle_blocks(n, mem_dev, count, depth, lists, anom, incr, loc, ins, outs)


def settle(nx, block, n, mem_dev, count, whole, cells, tables, xs):
    depth = block * nx // LANES
    shapes = block_shapes(n, False, mem_dev * count * depth)
    size = n * mem_dev * count * depth * LANES
    return pl.pallas_call(
        functools.partial(settle_kernel, nx, block, n, mem_dev, count, depth, whole),
        in_specs=[SMEM] + [VMEM] * (3 + len(xs)),
        out_specs=[VMEM] * len(shapes),
        out_shape=shapes,
        scratch_shapes=[pltpu.SMEM((depth // TILE, cells.size + 2), jnp.int32)],
        cost_estimate=cost(4 * cells.size * size, 8 * size),
        compiler_params=params(),
        name="settle",
    )(cells, *tables, *xs)


def assemble_kernel(n, count, *refs):
    out_ref, turn = refs[-2], refs[-1]
    blocks = blocks_in(refs[:n], n, False)
    mem_dev, _, ny, nx = out_ref.shape
    block = ny // n
    tiles = nx // LANES
    depth = block * tiles
    slab = pl.program_id(0)
    for m in range(mem_dev):
        at = pl.multiple_of((m * count + slab) * depth, TILE)
        for t in range(tiles):
            lanes = slice(t * LANES, (t + 1) * LANES)
            lines = pl.ds(at + t * block, block)
            for j, (ref, d) in enumerate(blocks):
                if block % TILE == 0:
                    row = pl.multiple_of(d * block, block)
                    out_ref[m, 0, pl.ds(row, block), lanes] = ref[lines, :]
                else:
                    turn[pl.ds(j * block, block), :] = ref[lines, :]
            if block % TILE:
                for d, (_, j) in enumerate(blocks):
                    out_ref[m, 0, d * block : (d + 1) * block, lanes] = turn[
                        pl.ds(j * block, block), :
                    ]


def assemble(n, start, count, recv, shape, before):
    mem_dev, _, ny, nx = shape
    extra = [] if before is None else [before]
    return pl.pallas_call(
        functools.partial(assemble_kernel, n, count),
        grid=(count,),
        in_specs=[VMEM] * n + [pl.BlockSpec(memory_space=pl.ANY)] * len(extra),
        out_specs=pl.BlockSpec((mem_dev, 1, ny, nx), lambda s: (0, start + s, 0, 0)),
        out_shape=jax.ShapeDtypeStruct(shape, jnp.float32),
        scratch_shapes=[pltpu.VMEM((ny, LANES), jnp.float32)],
        input_output_aliases={} if before is None else {n: 0},
        cost_estimate=cost(0, 8 * n * recv[0].size),
        compiler_params=params(),
        name="assemble",
    )(*recv, *extra)


def exchange(blocks, n, whole):
    if whole:
        return [lax.all_to_all(blocks[0], "mem", split_axis=0, concat_axis=0, tiled=True)]
    got = {}
    for j in range(n - 1, 0, -1):
        got[j] = lax.ppermute(blocks[j], "mem", [(i, i ^ j) for i in range(n)])
    return blocks[:1] + [got[j] for j in range(1, n)]


def body(x, cv, ch, spread, obs_cells, obs_slabs, obs_values, obs_error):
    mem_dev, slab_dev, ny, nx = x.shape
    n, lev = lax.axis_size("mem"), lax.axis_size("lev")
    block = ny // n
    depth = block * nx // LANES
    parts = chunks_of(slab_dev)
    sends = forecast(parts, n, obs_cells, obs_slabs, spread, x, cv, ch)
    states = []
    for c, blocks in enumerate(sends):
        states.append(exchange(blocks, n, parts[c][2]))
    per = TILE // mem_dev
    seen = [s[mem_dev * parts[0][1] * depth :, :] for s in states[0]]
    seen = jnp.concatenate([sum(seen[g : g + per]) for g in range(0, n, per)])
    tiles = [seen] + [
        lax.ppermute(seen, "lev", [(i, (i + d) % lev) for i in range(lev)])
        for d in range(1, lev)
    ]
    result = None
    for c, ((start, count, whole), state) in enumerate(zip(parts, states)):
        if c == 0:
            tables, new = filter_plan(
                nx, block, mem_dev, count, obs_cells, obs_values, obs_error, tiles, state
            )
        else:
            new = settle(
                nx, block, n, mem_dev, count, whole, obs_cells, tables, state
            )
        back = exchange(list(new), n, False)
        result = assemble(n, start, count, back, x.shape, result)
    return result


def solution(mesh):
    in_specs = (
        P("mem", "lev", None, None),
        P("lev", None, None),
        P("lev", None, None),
        P("lev"),
        P(),
        P(),
        P(),
        P(),
    )
    out_specs = P("mem", "lev", None, None)
    return jax.shard_map(body, mesh=mesh, in_specs=in_specs, out_specs=out_specs, check_vma=False)
```

```python
import functools

import jax
import jax.numpy as jnp
from jax import lax
from jax.experimental import pallas as pl
from jax.experimental.pallas import tpu as pltpu
from jax.sharding import PartitionSpec as P


STEPS = 2
LOC_HALF = 64
LANES = 128
GRANT = 24 * 1024 * 1024
TILE = 8
VMEM = pl.BlockSpec(memory_space=pltpu.VMEM)
SMEM = pl.BlockSpec(memory_space=pltpu.SMEM)


def cost(flops, nbytes):
    return pl.CostEstimate(flops=flops, bytes_accessed=nbytes, transcendentals=0)


def taper(row_gap, col_gap):
    scaled = jnp.sqrt(row_gap * row_gap + col_gap * col_gap) * (1.0 / LOC_HALF)
    inner = (
        ((-0.25 * scaled + 0.5) * scaled + 0.625) * scaled - 5.0 / 3.0
    ) * scaled * scaled + 1.0
    safe = jnp.maximum(scaled, 1.0)
    outer = (
        ((((scaled * (1.0 / 12.0) - 0.5) * scaled + 0.625) * scaled + 5.0 / 3.0) * scaled - 5.0)
        * scaled
        + 4.0
        - (2.0 / 3.0) / safe
    )
    return jnp.where(scaled <= 1.0, inner, jnp.where(scaled < 2.0, outer, 0.0))


def chunks_of(slab_dev):
    first = max(1, (2 * slab_dev) // 5)
    if slab_dev == 1:
        return ((0, 1, False),)
    return ((0, first, False), (first, slab_dev - first, True))


def row_col(cell, nx):
    if nx & (nx - 1):
        return cell // nx, cell % nx
    return lax.shift_right_logical(cell, nx.bit_length() - 1), cell & (nx - 1)


def place(ref, k):
    return ref[k // ref.shape[1], k % ref.shape[1]]


def params():
    return pltpu.CompilerParams(vmem_limit_bytes=GRANT)


def blocks_in(refs, n, whole):
    me = lax.axis_index("mem")
    return [(refs[0].at[me ^ j] if whole else refs[j], me ^ j) for j in range(n)]


def block_shapes(n, whole, rows):
    if whole:
        return [jax.ShapeDtypeStruct((n, rows, LANES), jnp.float32)]
    return [jax.ShapeDtypeStruct((rows, LANES), jnp.float32)] * n


def forecast_kernel(parts, n, cells_hbm, slabs_hbm, spread_hbm, x_hbm, cv_hbm, ch_hbm, *rest):
    outs = []
    for start, count, whole in parts:
        width = 1 if whole else n
        outs.append(blocks_in(rest[:width], n, whole))
        rest = rest[width:]
    x_buf, cv_buf, ch_buf, cells, slabs, spread, field, half, weights, picks, sem, small = rest
    slab_dev, mem_dev, ny, nx = x_buf.shape
    block = ny // n
    tiles = nx // LANES
    depth = block * tiles
    total = cells.shape[0] * cells.shape[1]

    def loads(s):
        return (
            pltpu.make_async_copy(x_hbm.at[:, s], x_buf.at[s], sem.at[0, s]),
            pltpu.make_async_copy(cv_hbm.at[s], cv_buf.at[s], sem.at[1, s]),
            pltpu.make_async_copy(ch_hbm.at[s], ch_buf.at[s], sem.at[2, s]),
        )

    lists = (
        pltpu.make_async_copy(spread_hbm, spread, small.at[0]),
        pltpu.make_async_copy(cells_hbm, cells, small.at[1]),
        pltpu.make_async_copy(slabs_hbm, slabs, small.at[2]),
    )
    for copy in lists:
        copy.start()
    for s in range(slab_dev):
        for copy in loads(s):
            copy.start()
    for copy in lists:
        copy.wait()
    sub = lax.broadcasted_iota(jnp.int32, (TILE, LANES), 0)
    lane = lax.broadcasted_iota(jnp.int32, (TILE, LANES), 1)
    east_edge, west_edge = lane == LANES - 1, lane == 0
    north_edge, south_edge = sub == TILE - 1, sub == 0
    high = ny // TILE

    def spot(r, t):
        return slice(t * ny + r * TILE, t * ny + (r + 1) * TILE)

    def advance(load, keep, store):
        known = {}

        def turned(r, t, by, axis):
            key = (r, t, by, axis)
            if key not in known:
                known[key] = pltpu.roll(load(r, t), by, axis)
            return known[key]

        def beyond(inside, r, t, by, axis, here):
            return turned(r, t, by, axis) if inside else here

        for r in range(high):
            for t in range(tiles):
                f = load(r, t)
                east = jnp.where(
                    east_edge,
                    beyond(t + 1 < tiles, r, t + 1, LANES - 1, 1, f),
                    turned(r, t, LANES - 1, 1),
                )
                west = jnp.where(
                    west_edge, beyond(t > 0, r, t - 1, 1, 1, f), turned(r, t, 1, 1)
                )
                north = jnp.where(
                    north_edge,
                    beyond(r + 1 < high, r + 1, t, TILE - 1, 0, f),
                    turned(r, t, TILE - 1, 0),
                )
                south = jnp.where(
                    south_edge, beyond(r > 0, r - 1, t, 1, 0, f), turned(r, t, 1, 0)
                )
                at = spot(r, t)
                store(
                    r,
                    t,
                    (keep * f + weights[0, at, :] * east)
                    + (weights[1, at, :] * west + weights[2, at, :] * north)
                    + weights[3, at, :] * south,
                )

    for (start, count, whole), blocks in zip(parts, outs):

        def one(s, carry):
            slab = start + s
            for copy in loads(slab):
                copy.wait()
            diffuse = spread[slab]
            keep = 1.0 - 4.0 * diffuse
            for r in range(high):
                for t in range(tiles):
                    tile = (slice(r * TILE, (r + 1) * TILE), slice(t * LANES, (t + 1) * LANES))
                    half_v, half_h = 0.5 * cv_buf[slab, *tile], 0.5 * ch_buf[slab, *tile]
                    weights[0, spot(r, t), :] = diffuse - half_v
                    weights[1, spot(r, t), :] = diffuse + half_v
                    weights[2, spot(r, t), :] = diffuse - half_h
                    weights[3, spot(r, t), :] = diffuse + half_h
            for m in range(mem_dev):
                level = slab * mem_dev + m

                def first(r, t):
                    return x_buf[
                        slab, m, r * TILE : (r + 1) * TILE, t * LANES : (t + 1) * LANES
                    ]

                def later(r, t):
                    return half[spot(r, t), :]

                def between(r, t, value):
                    half[spot(r, t), :] = value

                def final(r, t, value):
                    field[level, spot(r, t), :] = value

                for step in range(STEPS):
                    advance(
                        later if step else first, keep, between if step < STEPS - 1 else final
                    )
                at = pl.multiple_of((m * count + s) * depth, TILE)
                for ref, d in blocks:
                    for t in range(tiles):
                        row = pl.multiple_of(t * ny + d * block, block)
                        ref[pl.ds(at + t * block, block), :] = field[level, pl.ds(row, block), :]
            return carry

        lax.fori_loop(0, count, one, 0)

    lane = lax.broadcasted_iota(jnp.int32, (1, LANES), 1)
    for k in range(total):
        cell = place(cells, k)
        row, col = row_col(cell, nx)
        off = place(slabs, k) - lax.axis_index("lev") * slab_dev
        inside = (off >= 0) & (off < slab_dev)
        across, wanted = row_col(col, LANES)
        wanted = jnp.where(inside, wanted, LANES)
        off = jnp.where(inside, off, 0)
        for m in range(mem_dev):
            line = field[off * mem_dev + m, pl.ds(across * ny + row, 1), :]
            picks[m, pl.ds(k, 1), :] = jnp.where(lane == wanted, line, 0.0)
    diagonal = lax.broadcasted_iota(jnp.int32, (total, LANES), 0) == lax.broadcasted_iota(
        jnp.int32, (total, LANES), 1
    )
    values = []
    for m in range(mem_dev):
        value = jnp.sum(picks[m], axis=1, keepdims=True)
        values.append(jnp.sum(jnp.where(diagonal, value, 0.0), axis=0, keepdims=True))
    for j in range(n):
        seen = jnp.zeros((TILE, LANES), jnp.float32)
        for m in range(mem_dev):
            seen = jnp.where(sub == (j * mem_dev + m) % TILE, values[m], seen)
        outs[0][j][0][pl.ds(mem_dev * parts[0][1] * depth, TILE), :] = seen


def forecast(parts, n, cells, slabs, spread, x, cv, ch):
    mem_dev, slab_dev, ny, nx = x.shape
    depth = ny // n * nx // LANES
    shapes = []
    for i, (_, count, whole) in enumerate(parts):
        shapes.append(block_shapes(n, whole, mem_dev * count * depth + (0 if i else TILE)))
    outs = pl.pallas_call(
        functools.partial(forecast_kernel, parts, n),
        in_specs=[pl.BlockSpec(memory_space=pltpu.HBM)] * 6,
        out_specs=[VMEM for group in shapes for _ in group],
        out_shape=[shape for group in shapes for shape in group],
        scratch_shapes=[
            pltpu.VMEM((slab_dev, mem_dev, ny, nx), jnp.float32),
            pltpu.VMEM(cv.shape, jnp.float32),
            pltpu.VMEM(ch.shape, jnp.float32),
            pltpu.SMEM(cells.shape, jnp.int32),
            pltpu.SMEM(slabs.shape, jnp.int32),
            pltpu.SMEM(spread.shape, jnp.float32),
            pltpu.VMEM((slab_dev * mem_dev, ny * nx // LANES, LANES), jnp.float32),
            pltpu.VMEM((ny * nx // LANES, LANES), jnp.float32),
            pltpu.VMEM((4, ny * nx // LANES, LANES), jnp.float32),
            pltpu.VMEM((mem_dev, cells.size, LANES), jnp.float32),
            pltpu.SemaphoreType.DMA((3, slab_dev)),
            pltpu.SemaphoreType.DMA((3,)),
        ],
        cost_estimate=cost(60 * x.size, 4 * (2 * x.size + 2 * cv.size)),
        compiler_params=params(),
        name="forecast",
    )(*[pltpu.with_memory_space_constraint(a, pltpu.HBM) for a in (cells, slabs, spread, x, cv, ch)])
    sends = []
    for group in shapes:
        sends.append(list(outs[: len(group)]))
        outs = outs[len(group) :]
    return sends


def reach(cells, lists, nx, block, groups):
    total = cells.shape[0] * cells.shape[1]
    me = lax.axis_index("mem")
    for g in range(groups):
        count = jnp.int32(0)
        low_col = g * TILE // block * LANES
        high_col = (g * TILE + TILE - 1) // block * LANES + LANES - 1
        low_row = me * block + g * TILE % block
        high_row = low_row + min(block, TILE) - 1
        for k in range(total):
            row, col = row_col(place(cells, k), nx)
            down = jnp.maximum(jnp.maximum(low_row - row, row - high_row), 0)
            across = jnp.maximum(jnp.maximum(low_col - col, col - high_col), 0)
            lists[g, count] = jnp.int32(k)
            near = down * down + across * across < (2 * LOC_HALF) ** 2
            count = count + near.astype(jnp.int32)
        lists[g, count] = jnp.int32(total)
        lists[g, total + 1] = count


def taper_kernel(nx, block, cells, values_ref, errors_ref, loc_ref, near_ref, meta_ref, out, lists, sem):
    total = near_ref.shape[0]
    depth = loc_ref.shape[1]
    at = lax.broadcasted_iota(jnp.int32, (depth, LANES), 0)
    cell_row = (lax.axis_index("mem") * block + at % block).astype(jnp.float32)
    cell_col = (
        at // block * LANES + lax.broadcasted_iota(jnp.int32, (depth, LANES), 1)
    ).astype(jnp.float32)
    lane = lax.broadcasted_iota(jnp.int32, (1, LANES), 1)
    row_of = jnp.zeros((1, LANES), jnp.float32)
    col_of = jnp.zeros((1, LANES), jnp.float32)
    for k in range(total):
        row, col = row_col(place(cells, k), nx)
        row, col = row.astype(jnp.float32), col.astype(jnp.float32)
        row_of = jnp.where(lane == k, row, row_of)
        col_of = jnp.where(lane == k, col, col_of)
        loc_ref[k] = taper(cell_row - row, cell_col - col)
        meta_ref[k, 0:1, :] = jnp.full((1, LANES), place(errors_ref, k), jnp.float32)
        meta_ref[k, 1:2, :] = jnp.full((1, LANES), place(values_ref, k), jnp.float32)
    loc_ref[total] = jnp.zeros((depth, LANES), jnp.float32)
    reach(cells, lists, nx, block, depth // TILE)
    copy = pltpu.make_async_copy(lists, out, sem)
    copy.start()
    diagonal = lax.broadcasted_iota(jnp.int32, (total, LANES), 0) == lax.broadcasted_iota(
        jnp.int32, (total, LANES), 1
    )
    own_row = jnp.sum(jnp.where(diagonal, row_of, 0.0), axis=1, keepdims=True)
    own_col = jnp.sum(jnp.where(diagonal, col_of, 0.0), axis=1, keepdims=True)
    near_ref[...] = taper(row_of - own_row, col_of - own_col)
    copy.wait()


def list_shape(depth):
    return (-(-depth // TILE // TILE) * TILE, LANES)


def taper_tables(nx, block, cells, values, errors):
    total = cells.size
    depth = block * nx // LANES
    return pl.pallas_call(
        functools.partial(taper_kernel, nx, block),
        in_specs=[SMEM] * 3,
        out_specs=[VMEM] * 4,
        out_shape=[
            jax.ShapeDtypeStruct((total + 1, depth, LANES), jnp.float32),
            jax.ShapeDtypeStruct((total, LANES), jnp.float32),
            jax.ShapeDtypeStruct((total, TILE, LANES), jnp.float32),
            jax.ShapeDtypeStruct(list_shape(depth), jnp.int32),
        ],
        scratch_shapes=[pltpu.SMEM(list_shape(depth), jnp.int32), pltpu.SemaphoreType.DMA(())],
        cost_estimate=cost(60 * total * depth * LANES, 4 * total * depth * LANES),
        compiler_params=params(),
        name="taper_tables",
    )(cells, values, errors)


def settle_blocks(n, mem_dev, count, depth, lists, anom_ref, incr_ref, loc_ref, ins, outs):
    total = loc_ref.shape[0] - 1
    members = n * mem_dev
    group = max(g for g in range(1, count + 1) if count % g == 0 and (g == 1 or g * members <= 48))
    turns = count // group

    def spread(ref, k, m):
        return ref[k, pl.ds(m, TILE, stride=0), :]

    def part(i, carry):
        tile, slab = i // turns, i % turns * group
        at = tile * TILE

        def spot(m, g):
            row = ((m % mem_dev) * count + slab + g) * depth + at
            return m // mem_dev, pl.ds(pl.multiple_of(row, TILE), TILE)

        xs = []
        for m in range(members):
            for g in range(group):
                src, row = spot(m, g)
                xs.append(ins[src][0][row, :])

        def step(k, xs):
            terms = [[] for _ in range(group)]
            for m in range(members):
                a = spread(anom_ref, k, m)
                for g in range(group):
                    terms[g].append(a * xs[m * group + g])
            loc = loc_ref[k, pl.ds(pl.multiple_of(at, TILE), TILE), :]
            for g in range(group):
                while len(terms[g]) > 1:
                    odd = terms[g][len(terms[g]) // 2 * 2 :]
                    terms[g] = [a + b for a, b in zip(terms[g][::2], terms[g][1::2])] + odd
            sums = [terms[g][0] * loc for g in range(group)]
            new = []
            for m in range(members):
                b = spread(incr_ref, k, m)
                for g in range(group):
                    new.append(xs[m * group + g] + b * sums[g])
            return new

        def two(i, xs):
            return tuple(step(lists[tile, 2 * i + 1], step(lists[tile, 2 * i], list(xs))))

        xs = lax.fori_loop(
            0, lax.shift_right_logical(lists[tile, total + 1] + 1, 1), two, tuple(xs)
        )
        for m in range(members):
            for g in range(group):
                src, row = spot(m, g)
                outs[src][0][row, :] = xs[m * group + g]
        return carry

    lax.fori_loop(0, depth // TILE * turns, part, 0)


def plan_kernel(n, mem_dev, count, lev, loc_ref, near_ref, meta_ref, lists_ref, *refs):
    seen_refs, refs = refs[:lev], refs[lev:]
    ins, refs = blocks_in(refs[:n], n, False), refs[n:]
    anom_ref, incr_ref = refs[:2]
    outs = blocks_in(refs[2 : 2 + n], n, False)
    lists, sem = refs[2 + n :]
    copy = pltpu.make_async_copy(lists_ref, lists, sem)
    copy.start()
    total, depth = near_ref.shape[0], loc_ref.shape[1]
    rows = seen_refs[0][...]
    for other in seen_refs[1:]:
        rows = rows + other[...]
    members = rows.shape[0]
    mean = jnp.sum(rows, axis=0, keepdims=True) * (1.0 / members)
    rows = rows - mean
    for k in range(total):
        error, value = meta_ref[k, 0:1, :], meta_ref[k, 1:2, :]
        anomaly = jnp.broadcast_to(rows[:, k : k + 1], rows.shape)
        ybar = jnp.broadcast_to(mean[:, k : k + 1], mean.shape)
        variance = jnp.sum(anomaly * anomaly, axis=0, keepdims=True) / (members - 1) + 1e-06
        shared = jnp.sum(rows * anomaly, axis=0, keepdims=True)
        scale = 1.0 / ((members - 1) * variance)
        shift = (ybar * error + value * variance) / (variance + error) - ybar
        shrink = jnp.sqrt(error / (variance + error)) - 1.0
        anom_ref[k, 0:members, :] = anomaly * scale
        incr_ref[k, 0:members, :] = shift + shrink * anomaly
        weight = near_ref[k : k + 1, :] * shared * scale
        mean = mean + weight * shift
        rows = rows + (weight * shrink) * anomaly
    anom_ref[total] = jnp.zeros(anom_ref.shape[1:], jnp.float32)
    incr_ref[total] = jnp.zeros(incr_ref.shape[1:], jnp.float32)
    copy.wait()
    settle_blocks(n, mem_dev, count, depth, lists, anom_ref, incr_ref, loc_ref, ins, outs)


def filter_plan(mem_dev, count, places, seen, xs):
    members = seen[0].shape[0]
    n = len(xs)
    total, depth = places[1].shape[0], places[0].shape[1]
    table = jax.ShapeDtypeStruct((total + 1, members + TILE, LANES), jnp.float32)
    shapes = [table, table] + block_shapes(n, False, mem_dev * count * depth)
    got = pl.pallas_call(
        functools.partial(plan_kernel, n, mem_dev, count, len(seen)),
        in_specs=[VMEM] * (4 + len(seen) + n),
        out_specs=[VMEM] * len(shapes),
        out_shape=shapes,
        scratch_shapes=[pltpu.SMEM(list_shape(depth), jnp.int32), pltpu.SemaphoreType.DMA(())],
        cost_estimate=cost(20_000_000, 4 * total * (2 * members + depth) * LANES),
        compiler_params=params(),
        name="filter_plan",
    )(*places, *seen, *xs)
    return got[:2], list(got[2:])


def settle_kernel(n, mem_dev, count, depth, whole, lists_ref, anom, incr, loc, *refs):
    width = 1 if whole else n
    ins, outs = blocks_in(refs[:width], n, whole), blocks_in(refs[width:-2], n, False)
    lists, sem = refs[-2:]
    copy = pltpu.make_async_copy(lists_ref, lists, sem)
    copy.start()
    copy.wait()
    settle_blocks(n, mem_dev, count, depth, lists, anom, incr, loc, ins, outs)


def settle(n, mem_dev, count, whole, places, tables, xs):
    loc, lists = places[0], places[3]
    depth = loc.shape[1]
    shapes = block_shapes(n, False, mem_dev * count * depth)
    size = n * mem_dev * count * depth * LANES
    return pl.pallas_call(
        functools.partial(settle_kernel, n, mem_dev, count, depth, whole),
        in_specs=[VMEM] * (4 + len(xs)),
        out_specs=[VMEM] * len(shapes),
        out_shape=shapes,
        scratch_shapes=[pltpu.SMEM(list_shape(depth), jnp.int32), pltpu.SemaphoreType.DMA(())],
        cost_estimate=cost(4 * loc.shape[0] * size, 8 * size),
        compiler_params=params(),
        name="settle",
    )(lists, *tables, loc, *xs)


def assemble_kernel(n, count, *refs):
    out_ref, turn = refs[-2], refs[-1]
    blocks = blocks_in(refs[:n], n, False)
    mem_dev, _, ny, nx = out_ref.shape
    block = ny // n
    tiles = nx // LANES
    depth = block * tiles
    slab = pl.program_id(0)
    for m in range(mem_dev):
        at = pl.multiple_of((m * count + slab) * depth, TILE)
        for t in range(tiles):
            lanes = slice(t * LANES, (t + 1) * LANES)
            lines = pl.ds(at + t * block, block)
            for j, (ref, d) in enumerate(blocks):
                if block % TILE == 0:
                    row = pl.multiple_of(d * block, block)
                    out_ref[m, 0, pl.ds(row, block), lanes] = ref[lines, :]
                else:
                    turn[pl.ds(j * block, block), :] = ref[lines, :]
            if block % TILE:
                for d, (_, j) in enumerate(blocks):
                    out_ref[m, 0, d * block : (d + 1) * block, lanes] = turn[
                        pl.ds(j * block, block), :
                    ]


def assemble(n, start, count, recv, shape, before):
    mem_dev, _, ny, nx = shape
    extra = [] if before is None else [before]
    return pl.pallas_call(
        functools.partial(assemble_kernel, n, count),
        grid=(count,),
        in_specs=[VMEM] * n + [pl.BlockSpec(memory_space=pl.ANY)] * len(extra),
        out_specs=pl.BlockSpec((mem_dev, 1, ny, nx), lambda s: (0, start + s, 0, 0)),
        out_shape=jax.ShapeDtypeStruct(shape, jnp.float32),
        scratch_shapes=[pltpu.VMEM((ny, LANES), jnp.float32)],
        input_output_aliases={} if before is None else {n: 0},
        cost_estimate=cost(0, 8 * n * recv[0].size),
        compiler_params=params(),
        name="assemble",
    )(*recv, *extra)


def order_of(n):
    return list(range(n // 2, n)) + list(range(n // 2 - 1, 0, -1))


def exchange(blocks, n, whole):
    if whole:
        return [lax.all_to_all(blocks[0], "mem", split_axis=0, concat_axis=0, tiled=True)]
    got = {}
    for j in order_of(n):
        got[j] = lax.ppermute(blocks[j], "mem", [(i, i ^ j) for i in range(n)])
    return blocks[:1] + [got[j] for j in range(1, n)]


def body(x, cv, ch, spread, obs_cells, obs_slabs, obs_values, obs_error):
    mem_dev, slab_dev, ny, nx = x.shape
    n, lev = lax.axis_size("mem"), lax.axis_size("lev")
    block = ny // n
    depth = block * nx // LANES
    parts = chunks_of(slab_dev)
    sends = forecast(parts, n, obs_cells, obs_slabs, spread, x, cv, ch)
    states = []
    for c, blocks in enumerate(sends):
        states.append(exchange(blocks, n, parts[c][2]))
    per = TILE // mem_dev
    seen = [s[mem_dev * parts[0][1] * depth :, :] for s in states[0]]
    seen = jnp.concatenate([sum(seen[g : g + per]) for g in range(0, n, per)])
    tiles = [seen] + [
        lax.ppermute(seen, "lev", [(i, (i + d) % lev) for i in range(lev)])
        for d in range(1, lev)
    ]
    places = taper_tables(nx, block, obs_cells, obs_values, obs_error)
    result = None
    for c, ((start, count, whole), state) in enumerate(zip(parts, states)):
        if c == 0:
            tables, new = filter_plan(mem_dev, count, places, tiles, state)
        else:
            new = settle(n, mem_dev, count, whole, places, tables, state)
        back = exchange(list(new), n, False)
        result = assemble(n, start, count, back, x.shape, result)
    return result


def solution(mesh):
    in_specs = (
        P("mem", "lev", None, None),
        P("lev", None, None),
        P("lev", None, None),
        P("lev"),
        P(),
        P(),
        P(),
        P(),
    )
    out_specs = P("mem", "lev", None, None)
    return jax.shard_map(body, mesh=mesh, in_specs=in_specs, out_specs=out_specs, check_vma=False)
```

```python
import functools

import jax
import jax.numpy as jnp
from jax import lax
from jax.experimental import pallas as pl
from jax.experimental.pallas import tpu as pltpu
from jax.sharding import PartitionSpec as P


STEPS = 2
LOC_HALF = 64
LANES = 128
GRANT = 24 * 1024 * 1024
TILE = 8
VMEM = pl.BlockSpec(memory_space=pltpu.VMEM)
SMEM = pl.BlockSpec(memory_space=pltpu.SMEM)


def cost(flops, nbytes):
    return pl.CostEstimate(flops=flops, bytes_accessed=nbytes, transcendentals=0)


def taper(row_gap, col_gap):
    scaled = jnp.sqrt(row_gap * row_gap + col_gap * col_gap) * (1.0 / LOC_HALF)
    inner = (
        ((-0.25 * scaled + 0.5) * scaled + 0.625) * scaled - 5.0 / 3.0
    ) * scaled * scaled + 1.0
    safe = jnp.maximum(scaled, 1.0)
    outer = (
        ((((scaled * (1.0 / 12.0) - 0.5) * scaled + 0.625) * scaled + 5.0 / 3.0) * scaled - 5.0)
        * scaled
        + 4.0
        - (2.0 / 3.0) / safe
    )
    return jnp.where(scaled <= 1.0, inner, jnp.where(scaled < 2.0, outer, 0.0))


def chunks_of(slab_dev):
    first = max(1, (2 * slab_dev) // 5)
    if slab_dev == 1:
        return ((0, 1, False),)
    return ((0, first, False), (first, slab_dev - first, True))


def row_col(cell, nx):
    if nx & (nx - 1):
        return cell // nx, cell % nx
    return lax.shift_right_logical(cell, nx.bit_length() - 1), cell & (nx - 1)


def place(ref, k):
    return ref[k // ref.shape[1], k % ref.shape[1]]


def params():
    return pltpu.CompilerParams(vmem_limit_bytes=GRANT)


def blocks_in(refs, n, whole):
    me = lax.axis_index("mem")
    return [(refs[0].at[me ^ j] if whole else refs[j], me ^ j) for j in range(n)]


def block_shapes(n, whole, rows):
    if whole:
        return [jax.ShapeDtypeStruct((n, rows, LANES), jnp.float32)]
    return [jax.ShapeDtypeStruct((rows, LANES), jnp.float32)] * n


def forecast_kernel(parts, n, cells_hbm, slabs_hbm, spread_hbm, x_hbm, cv_hbm, ch_hbm, *rest):
    outs = []
    for start, count, whole in parts:
        width = 1 if whole else n
        outs.append(blocks_in(rest[:width], n, whole))
        rest = rest[width:]
    x_buf, cv_buf, ch_buf, cells, slabs, spread, field, half, weights, picks, sem, small = rest
    slab_dev, mem_dev, tiles = x_buf.shape[:3]
    ny, nx = x_buf.shape[3] - 2 * TILE, tiles * LANES
    block = ny // n
    depth = block * tiles
    total = cells.shape[0] * cells.shape[1]

    def loads(s):
        return [
            pltpu.make_async_copy(cv_hbm.at[s], cv_buf.at[s], sem.at[tiles, s]),
            pltpu.make_async_copy(ch_hbm.at[s], ch_buf.at[s], sem.at[tiles + 1, s]),
        ] + [
            pltpu.make_async_copy(
                x_hbm.at[:, s, :, t * LANES : (t + 1) * LANES],
                x_buf.at[s, :, t, TILE : TILE + ny, :],
                sem.at[t, s],
            )
            for t in range(tiles)
        ]

    lists = (
        pltpu.make_async_copy(spread_hbm, spread, small.at[0]),
        pltpu.make_async_copy(cells_hbm, cells, small.at[1]),
        pltpu.make_async_copy(slabs_hbm, slabs, small.at[2]),
    )
    for copy in lists:
        copy.start()
    for s in range(slab_dev):
        for copy in loads(s):
            copy.start()
    for copy in lists:
        copy.wait()
    sub = lax.broadcasted_iota(jnp.int32, (TILE, LANES), 0)
    lane = lax.broadcasted_iota(jnp.int32, (TILE, LANES), 1)
    east_edge, west_edge = lane == LANES - 1, lane == 0
    high = ny // TILE

    def spot(r, t):
        return slice(t * ny + r * TILE, t * ny + (r + 1) * TILE)

    def advance(load, keep, store):
        for r in range(high):
            row = TILE + r * TILE
            centre = [load(t, row) for t in range(tiles)]
            ahead = [pltpu.roll(f, LANES - 1, 1) for f in centre]
            behind = [pltpu.roll(f, 1, 1) for f in centre]
            for t, f in enumerate(centre):
                east = jnp.where(east_edge, ahead[t + 1] if t + 1 < tiles else f, ahead[t])
                west = jnp.where(west_edge, behind[t - 1] if t else f, behind[t])
                at = spot(r, t)
                store(
                    r,
                    t,
                    (keep * f + weights[0, at, :] * east)
                    + (weights[1, at, :] * west + weights[2, at, :] * load(t, row + 1))
                    + weights[3, at, :] * load(t, row - 1),
                )

    for (start, count, whole), blocks in zip(parts, outs):

        def one(s, carry):
            slab = start + s
            for copy in loads(slab):
                copy.wait()
            diffuse = spread[slab]
            keep = 1.0 - 4.0 * diffuse
            for r in range(high):
                for t in range(tiles):
                    tile = (slice(r * TILE, (r + 1) * TILE), slice(t * LANES, (t + 1) * LANES))
                    half_v, half_h = 0.5 * cv_buf[slab, *tile], 0.5 * ch_buf[slab, *tile]
                    weights[0, spot(r, t), :] = diffuse - half_v
                    weights[1, spot(r, t), :] = diffuse + half_v
                    weights[2, spot(r, t), :] = diffuse - half_h
                    weights[3, spot(r, t), :] = diffuse + half_h
            for m in range(mem_dev):
                level = slab * mem_dev + m

                for t in range(tiles):
                    x_buf[slab, m, t, TILE - 1 : TILE, :] = x_buf[slab, m, t, TILE : TILE + 1, :]
                    x_buf[slab, m, t, TILE + ny : TILE + ny + 1, :] = x_buf[
                        slab, m, t, TILE + ny - 1 : TILE + ny, :
                    ]

                def first(t, row):
                    return x_buf[slab, m, t, row : row + TILE, :]

                def later(t, row):
                    return half[m, t, row : row + TILE, :]

                def between(r, t, value):
                    row = TILE + r * TILE
                    half[m, t, row : row + TILE, :] = value
                    if r == 0:
                        half[m, t, TILE - 1 : TILE, :] = value[0:1, :]
                    if r == high - 1:
                        half[m, t, TILE + ny : TILE + ny + 1, :] = value[TILE - 1 : TILE, :]

                def final(r, t, value):
                    field[level, spot(r, t), :] = value

                for step in range(STEPS):
                    advance(
                        later if step else first, keep, between if step < STEPS - 1 else final
                    )
                at = pl.multiple_of((m * count + s) * depth, TILE)
                for ref, d in blocks:
                    for t in range(tiles):
                        row = pl.multiple_of(t * ny + d * block, block)
                        ref[pl.ds(at + t * block, block), :] = field[level, pl.ds(row, block), :]
            return carry

        lax.fori_loop(0, count, one, 0)

    lane = lax.broadcasted_iota(jnp.int32, (1, LANES), 1)
    for k in range(total):
        cell = place(cells, k)
        row, col = row_col(cell, nx)
        off = place(slabs, k) - lax.axis_index("lev") * slab_dev
        inside = (off >= 0) & (off < slab_dev)
        across, wanted = row_col(col, LANES)
        wanted = jnp.where(inside, wanted, LANES)
        off = jnp.where(inside, off, 0)
        for m in range(mem_dev):
            line = field[off * mem_dev + m, pl.ds(across * ny + row, 1), :]
            picks[m, pl.ds(k, 1), :] = jnp.where(lane == wanted, line, 0.0)
    diagonal = lax.broadcasted_iota(jnp.int32, (total, LANES), 0) == lax.broadcasted_iota(
        jnp.int32, (total, LANES), 1
    )
    values = []
    for m in range(mem_dev):
        value = jnp.sum(picks[m], axis=1, keepdims=True)
        values.append(jnp.sum(jnp.where(diagonal, value, 0.0), axis=0, keepdims=True))
    for j in range(n):
        seen = jnp.zeros((TILE, LANES), jnp.float32)
        for m in range(mem_dev):
            seen = jnp.where(sub == (j * mem_dev + m) % TILE, values[m], seen)
        outs[0][j][0][pl.ds(mem_dev * parts[0][1] * depth, TILE), :] = seen


def forecast(parts, n, cells, slabs, spread, x, cv, ch):
    mem_dev, slab_dev, ny, nx = x.shape
    depth = ny // n * nx // LANES
    shapes = []
    for i, (_, count, whole) in enumerate(parts):
        shapes.append(block_shapes(n, whole, mem_dev * count * depth + (0 if i else TILE)))
    outs = pl.pallas_call(
        functools.partial(forecast_kernel, parts, n),
        in_specs=[pl.BlockSpec(memory_space=pltpu.HBM)] * 6,
        out_specs=[VMEM for group in shapes for _ in group],
        out_shape=[shape for group in shapes for shape in group],
        scratch_shapes=[
            pltpu.VMEM((slab_dev, mem_dev, nx // LANES, ny + 2 * TILE, LANES), jnp.float32),
            pltpu.VMEM(cv.shape, jnp.float32),
            pltpu.VMEM(ch.shape, jnp.float32),
            pltpu.SMEM(cells.shape, jnp.int32),
            pltpu.SMEM(slabs.shape, jnp.int32),
            pltpu.SMEM(spread.shape, jnp.float32),
            pltpu.VMEM((slab_dev * mem_dev, ny * nx // LANES, LANES), jnp.float32),
            pltpu.VMEM((mem_dev, nx // LANES, ny + 2 * TILE, LANES), jnp.float32),
            pltpu.VMEM((4, ny * nx // LANES, LANES), jnp.float32),
            pltpu.VMEM((mem_dev, cells.size, LANES), jnp.float32),
            pltpu.SemaphoreType.DMA((2 + nx // LANES, slab_dev)),
            pltpu.SemaphoreType.DMA((3,)),
        ],
        cost_estimate=cost(60 * x.size, 4 * (2 * x.size + 2 * cv.size)),
        compiler_params=params(),
        name="forecast",
    )(*[pltpu.with_memory_space_constraint(a, pltpu.HBM) for a in (cells, slabs, spread, x, cv, ch)])
    sends = []
    for group in shapes:
        sends.append(list(outs[: len(group)]))
        outs = outs[len(group) :]
    return sends


def reach(cells, lists, nx, block, groups):
    total = cells.shape[0] * cells.shape[1]
    me = lax.axis_index("mem")
    for g in range(groups):
        count = jnp.int32(0)
        low_col = g * TILE // block * LANES
        high_col = (g * TILE + TILE - 1) // block * LANES + LANES - 1
        low_row = me * block + g * TILE % block
        high_row = low_row + min(block, TILE) - 1
        for k in range(total):
            row, col = row_col(place(cells, k), nx)
            down = jnp.maximum(jnp.maximum(low_row - row, row - high_row), 0)
            across = jnp.maximum(jnp.maximum(low_col - col, col - high_col), 0)
            lists[g, count] = jnp.int32(k)
            near = down * down + across * across < (2 * LOC_HALF) ** 2
            count = count + near.astype(jnp.int32)
        lists[g, count] = jnp.int32(total)
        lists[g, total + 1] = count


def taper_kernel(nx, block, cells, values_ref, errors_ref, loc_ref, near_ref, meta_ref, out, lists, sem):
    total = near_ref.shape[0]
    depth = loc_ref.shape[1]
    at = lax.broadcasted_iota(jnp.int32, (depth, LANES), 0)
    cell_row = (lax.axis_index("mem") * block + at % block).astype(jnp.float32)
    cell_col = (
        at // block * LANES + lax.broadcasted_iota(jnp.int32, (depth, LANES), 1)
    ).astype(jnp.float32)
    lane = lax.broadcasted_iota(jnp.int32, (1, LANES), 1)
    row_of = jnp.zeros((1, LANES), jnp.float32)
    col_of = jnp.zeros((1, LANES), jnp.float32)
    for k in range(total):
        row, col = row_col(place(cells, k), nx)
        row, col = row.astype(jnp.float32), col.astype(jnp.float32)
        row_of = jnp.where(lane == k, row, row_of)
        col_of = jnp.where(lane == k, col, col_of)
        loc_ref[k] = taper(cell_row - row, cell_col - col)
        meta_ref[k, 0:1, :] = jnp.full((1, LANES), place(errors_ref, k), jnp.float32)
        meta_ref[k, 1:2, :] = jnp.full((1, LANES), place(values_ref, k), jnp.float32)
    loc_ref[total] = jnp.zeros((depth, LANES), jnp.float32)
    reach(cells, lists, nx, block, depth // TILE)
    copy = pltpu.make_async_copy(lists, out, sem)
    copy.start()
    diagonal = lax.broadcasted_iota(jnp.int32, (total, LANES), 0) == lax.broadcasted_iota(
        jnp.int32, (total, LANES), 1
    )
    own_row = jnp.sum(jnp.where(diagonal, row_of, 0.0), axis=1, keepdims=True)
    own_col = jnp.sum(jnp.where(diagonal, col_of, 0.0), axis=1, keepdims=True)
    near_ref[...] = taper(row_of - own_row, col_of - own_col)
    copy.wait()


def list_shape(depth):
    return (-(-depth // TILE // TILE) * TILE, LANES)


def taper_tables(nx, block, cells, values, errors):
    total = cells.size
    depth = block * nx // LANES
    return pl.pallas_call(
        functools.partial(taper_kernel, nx, block),
        in_specs=[SMEM] * 3,
        out_specs=[VMEM] * 4,
        out_shape=[
            jax.ShapeDtypeStruct((total + 1, depth, LANES), jnp.float32),
            jax.ShapeDtypeStruct((total, LANES), jnp.float32),
            jax.ShapeDtypeStruct((total, TILE, LANES), jnp.float32),
            jax.ShapeDtypeStruct(list_shape(depth), jnp.int32),
        ],
        scratch_shapes=[pltpu.SMEM(list_shape(depth), jnp.int32), pltpu.SemaphoreType.DMA(())],
        cost_estimate=cost(60 * total * depth * LANES, 4 * total * depth * LANES),
        compiler_params=params(),
        name="taper_tables",
    )(cells, values, errors)


def settle_blocks(n, mem_dev, count, depth, lists, anom_ref, incr_ref, loc_ref, ins, outs):
    total = loc_ref.shape[0] - 1
    members = n * mem_dev
    group = max(g for g in range(1, count + 1) if count % g == 0 and (g == 1 or g * members <= 48))
    turns = count // group

    def spread(ref, k, m):
        return ref[k, pl.ds(m, TILE, stride=0), :]

    def part(i, carry):
        tile, slab = i // turns, i % turns * group
        at = tile * TILE

        def spot(m, g):
            row = ((m % mem_dev) * count + slab + g) * depth + at
            return m // mem_dev, pl.ds(pl.multiple_of(row, TILE), TILE)

        xs = []
        for m in range(members):
            for g in range(group):
                src, row = spot(m, g)
                xs.append(ins[src][0][row, :])

        def step(k, xs):
            terms = [[] for _ in range(group)]
            for m in range(members):
                a = spread(anom_ref, k, m)
                for g in range(group):
                    terms[g].append(a * xs[m * group + g])
            loc = loc_ref[k, pl.ds(pl.multiple_of(at, TILE), TILE), :]
            for g in range(group):
                while len(terms[g]) > 1:
                    odd = terms[g][len(terms[g]) // 2 * 2 :]
                    terms[g] = [a + b for a, b in zip(terms[g][::2], terms[g][1::2])] + odd
            sums = [terms[g][0] * loc for g in range(group)]
            new = []
            for m in range(members):
                b = spread(incr_ref, k, m)
                for g in range(group):
                    new.append(xs[m * group + g] + b * sums[g])
            return new

        def two(i, xs):
            return tuple(step(lists[tile, 2 * i + 1], step(lists[tile, 2 * i], list(xs))))

        xs = lax.fori_loop(
            0, lax.shift_right_logical(lists[tile, total + 1] + 1, 1), two, tuple(xs)
        )
        for m in range(members):
            for g in range(group):
                src, row = spot(m, g)
                outs[src][0][row, :] = xs[m * group + g]
        return carry

    lax.fori_loop(0, depth // TILE * turns, part, 0)


def plan_kernel(n, mem_dev, count, lev, loc_ref, near_ref, meta_ref, lists_ref, *refs):
    seen_refs, refs = refs[:lev], refs[lev:]
    ins, refs = blocks_in(refs[:n], n, False), refs[n:]
    anom_ref, incr_ref = refs[:2]
    outs = blocks_in(refs[2 : 2 + n], n, False)
    lists, sem = refs[2 + n :]
    copy = pltpu.make_async_copy(lists_ref, lists, sem)
    copy.start()
    total, depth = near_ref.shape[0], loc_ref.shape[1]
    rows = seen_refs[0][...]
    for other in seen_refs[1:]:
        rows = rows + other[...]
    members = rows.shape[0]
    mean = jnp.sum(rows, axis=0, keepdims=True) * (1.0 / members)
    rows = rows - mean
    for k in range(total):
        error, value = meta_ref[k, 0:1, :], meta_ref[k, 1:2, :]
        anomaly = jnp.broadcast_to(rows[:, k : k + 1], rows.shape)
        ybar = jnp.broadcast_to(mean[:, k : k + 1], mean.shape)
        variance = jnp.sum(anomaly * anomaly, axis=0, keepdims=True) / (members - 1) + 1e-06
        shared = jnp.sum(rows * anomaly, axis=0, keepdims=True)
        scale = 1.0 / ((members - 1) * variance)
        shift = (ybar * error + value * variance) / (variance + error) - ybar
        shrink = jnp.sqrt(error / (variance + error)) - 1.0
        anom_ref[k, 0:members, :] = anomaly * scale
        incr_ref[k, 0:members, :] = shift + shrink * anomaly
        weight = near_ref[k : k + 1, :] * shared * scale
        mean = mean + weight * shift
        rows = rows + (weight * shrink) * anomaly
    anom_ref[total] = jnp.zeros(anom_ref.shape[1:], jnp.float32)
    incr_ref[total] = jnp.zeros(incr_ref.shape[1:], jnp.float32)
    copy.wait()
    settle_blocks(n, mem_dev, count, depth, lists, anom_ref, incr_ref, loc_ref, ins, outs)


def filter_plan(mem_dev, count, places, seen, xs):
    members = seen[0].shape[0]
    n = len(xs)
    total, depth = places[1].shape[0], places[0].shape[1]
    table = jax.ShapeDtypeStruct((total + 1, members + TILE, LANES), jnp.float32)
    shapes = [table, table] + block_shapes(n, False, mem_dev * count * depth)
    got = pl.pallas_call(
        functools.partial(plan_kernel, n, mem_dev, count, len(seen)),
        in_specs=[VMEM] * (4 + len(seen) + n),
        out_specs=[VMEM] * len(shapes),
        out_shape=shapes,
        scratch_shapes=[pltpu.SMEM(list_shape(depth), jnp.int32), pltpu.SemaphoreType.DMA(())],
        cost_estimate=cost(20_000_000, 4 * total * (2 * members + depth) * LANES),
        compiler_params=params(),
        name="filter_plan",
    )(*places, *seen, *xs)
    return got[:2], list(got[2:])


def settle_kernel(n, mem_dev, count, depth, whole, lists_ref, anom, incr, loc, *refs):
    width = 1 if whole else n
    ins, outs = blocks_in(refs[:width], n, whole), blocks_in(refs[width:-2], n, False)
    lists, sem = refs[-2:]
    copy = pltpu.make_async_copy(lists_ref, lists, sem)
    copy.start()
    copy.wait()
    settle_blocks(n, mem_dev, count, depth, lists, anom, incr, loc, ins, outs)


def settle(n, mem_dev, count, whole, places, tables, xs):
    loc, lists = places[0], places[3]
    depth = loc.shape[1]
    shapes = block_shapes(n, False, mem_dev * count * depth)
    size = n * mem_dev * count * depth * LANES
    return pl.pallas_call(
        functools.partial(settle_kernel, n, mem_dev, count, depth, whole),
        in_specs=[VMEM] * (4 + len(xs)),
        out_specs=[VMEM] * len(shapes),
        out_shape=shapes,
        scratch_shapes=[pltpu.SMEM(list_shape(depth), jnp.int32), pltpu.SemaphoreType.DMA(())],
        cost_estimate=cost(4 * loc.shape[0] * size, 8 * size),
        compiler_params=params(),
        name="settle",
    )(lists, *tables, loc, *xs)


def assemble_kernel(n, start, count, *refs):
    out_ref, stage, turn, sem = refs[-4:]
    blocks = blocks_in(refs[:n], n, False)
    mem_dev, _, ny, nx = out_ref.shape
    block = ny // n
    tiles = nx // LANES
    depth = block * tiles
    copies = []
    for slab in range(count):
        for m in range(mem_dev):
            at = (m * count + slab) * depth
            for t in range(tiles):
                lanes = slice(t * LANES, (t + 1) * LANES)
                lines = slice(at + t * block, at + (t + 1) * block)
                for j, (ref, d) in enumerate(blocks):
                    if block % TILE == 0:
                        row = pl.multiple_of(d * block, block)
                        stage[m, slab, pl.ds(row, block), lanes] = ref[lines, :]
                    else:
                        turn[j * block : (j + 1) * block, :] = ref[lines, :]
                if block % TILE:
                    for d, (_, j) in enumerate(blocks):
                        stage[m, slab, d * block : (d + 1) * block, lanes] = turn[
                            pl.ds(j * block, block), :
                        ]
        copies.append(
            pltpu.make_async_copy(
                stage.at[:, slab], out_ref.at[:, start + slab], sem.at[slab]
            )
        )
        copies[-1].start()
    for copy in copies:
        copy.wait()


def assemble(n, start, count, recv, shape, before):
    mem_dev, _, ny, nx = shape
    extra = [] if before is None else [before]
    return pl.pallas_call(
        functools.partial(assemble_kernel, n, start, count),
        in_specs=[VMEM] * n + [pl.BlockSpec(memory_space=pl.ANY)] * len(extra),
        out_specs=pl.BlockSpec(memory_space=pl.ANY),
        out_shape=jax.ShapeDtypeStruct(shape, jnp.float32),
        scratch_shapes=[
            pltpu.VMEM((mem_dev, count, ny, nx), jnp.float32),
            pltpu.VMEM((ny, LANES), jnp.float32),
            pltpu.SemaphoreType.DMA((count,)),
        ],
        input_output_aliases={} if before is None else {n: 0},
        cost_estimate=cost(0, 8 * n * recv[0].size),
        compiler_params=params(),
        name="assemble",
    )(*recv, *extra)


def order_of(n, near_first=False):
    far, near = list(range(n // 2, n)), list(range(n // 2 - 1, 0, -1))
    return near + far if near_first else far + near


def exchange(blocks, n, whole, near_first=False):
    if whole:
        return [lax.all_to_all(blocks[0], "mem", split_axis=0, concat_axis=0, tiled=True)]
    got = {}
    for j in order_of(n, near_first):
        got[j] = lax.ppermute(blocks[j], "mem", [(i, i ^ j) for i in range(n)])
    return blocks[:1] + [got[j] for j in range(1, n)]


def body(x, cv, ch, spread, obs_cells, obs_slabs, obs_values, obs_error):
    mem_dev, slab_dev, ny, nx = x.shape
    n, lev = lax.axis_size("mem"), lax.axis_size("lev")
    block = ny // n
    depth = block * nx // LANES
    parts = chunks_of(slab_dev)
    sends = forecast(parts, n, obs_cells, obs_slabs, spread, x, cv, ch)
    states = []
    for c, blocks in enumerate(sends):
        states.append(exchange(blocks, n, parts[c][2]))
    per = TILE // mem_dev
    seen = [s[mem_dev * parts[0][1] * depth :, :] for s in states[0]]
    seen = jnp.concatenate([sum(seen[g : g + per]) for g in range(0, n, per)])
    tiles = [seen] + [
        lax.ppermute(seen, "lev", [(i, (i + d) % lev) for i in range(lev)])
        for d in range(1, lev)
    ]
    places = taper_tables(nx, block, obs_cells, obs_values, obs_error)
    result = None
    for c, ((start, count, whole), state) in enumerate(zip(parts, states)):
        if c == 0:
            tables, new = filter_plan(mem_dev, count, places, tiles, state)
        else:
            new = settle(n, mem_dev, count, whole, places, tables, state)
        back = exchange(list(new), n, False, near_first=c == 0)
        result = assemble(n, start, count, back, x.shape, result)
    return result


def solution(mesh):
    in_specs = (
        P("mem", "lev", None, None),
        P("lev", None, None),
        P("lev", None, None),
        P("lev"),
        P(),
        P(),
        P(),
        P(),
    )
    out_specs = P("mem", "lev", None, None)
    return jax.shard_map(body, mesh=mesh, in_specs=in_specs, out_specs=out_specs, check_vma=False)
```

```python
import functools

import jax
import jax.numpy as jnp
from jax import lax
from jax.experimental import pallas as pl
from jax.experimental.pallas import tpu as pltpu
from jax.sharding import PartitionSpec as P


STEPS = 2
LOC_HALF = 64
LANES = 128
GRANT = 24 * 1024 * 1024
TILE = 8
VMEM = pl.BlockSpec(memory_space=pltpu.VMEM)
SMEM = pl.BlockSpec(memory_space=pltpu.SMEM)


def cost(flops, nbytes):
    return pl.CostEstimate(flops=flops, bytes_accessed=nbytes, transcendentals=0)


def taper(row_gap, col_gap):
    scaled = jnp.sqrt(row_gap * row_gap + col_gap * col_gap) * (1.0 / LOC_HALF)
    inner = (
        ((-0.25 * scaled + 0.5) * scaled + 0.625) * scaled - 5.0 / 3.0
    ) * scaled * scaled + 1.0
    safe = jnp.maximum(scaled, 1.0)
    outer = (
        ((((scaled * (1.0 / 12.0) - 0.5) * scaled + 0.625) * scaled + 5.0 / 3.0) * scaled - 5.0)
        * scaled
        + 4.0
        - (2.0 / 3.0) / safe
    )
    return jnp.where(scaled <= 1.0, inner, jnp.where(scaled < 2.0, outer, 0.0))


def chunks_of(slab_dev):
    first = max(1, (2 * slab_dev) // 5)
    if slab_dev == 1:
        return ((0, 1, False),)
    return ((0, first, False), (first, slab_dev - first, True))


def row_col(cell, nx):
    if nx & (nx - 1):
        return cell // nx, cell % nx
    return lax.shift_right_logical(cell, nx.bit_length() - 1), cell & (nx - 1)


def place(ref, k):
    return ref[k // ref.shape[1], k % ref.shape[1]]


def params():
    return pltpu.CompilerParams(vmem_limit_bytes=GRANT)


def blocks_in(refs, n, whole):
    me = lax.axis_index("mem")
    return [(refs[0].at[me ^ j] if whole else refs[j], me ^ j) for j in range(n)]


def block_shapes(n, whole, rows):
    if whole:
        return [jax.ShapeDtypeStruct((n, rows, LANES), jnp.float32)]
    return [jax.ShapeDtypeStruct((rows, LANES), jnp.float32)] * n


def forecast_kernel(parts, n, cells_hbm, slabs_hbm, spread_hbm, x_hbm, cv_hbm, ch_hbm, *rest):
    outs = []
    for start, count, whole in parts:
        width = 1 if whole else n
        outs.append(blocks_in(rest[:width], n, whole))
        rest = rest[width:]
    x_buf, cv_buf, ch_buf, cells, slabs, spread, spots, field, half, weights, picks = rest[:-2]
    sem, small = rest[-2:]
    slab_dev, mem_dev, tiles = x_buf.shape[:3]
    ny, nx = x_buf.shape[3] - 2 * TILE, tiles * LANES
    block = ny // n
    depth = block * tiles
    total = cells.shape[0] * cells.shape[1]

    def loads(s):
        return [
            pltpu.make_async_copy(cv_hbm.at[s], cv_buf.at[s], sem.at[tiles, s]),
            pltpu.make_async_copy(ch_hbm.at[s], ch_buf.at[s], sem.at[tiles + 1, s]),
        ] + [
            pltpu.make_async_copy(
                x_hbm.at[:, s, :, t * LANES : (t + 1) * LANES],
                x_buf.at[s, :, t, TILE : TILE + ny, :],
                sem.at[t, s],
            )
            for t in range(tiles)
        ]

    lists = (
        pltpu.make_async_copy(spread_hbm, spread, small.at[0]),
        pltpu.make_async_copy(cells_hbm, cells, small.at[1]),
        pltpu.make_async_copy(slabs_hbm, slabs, small.at[2]),
    )
    for copy in lists:
        copy.start()
    for s in range(slab_dev):
        for copy in loads(s):
            copy.start()
    for copy in lists:
        copy.wait()
    for k in range(total):
        row, col = row_col(place(cells, k), nx)
        across, wanted = row_col(col, LANES)
        off = place(slabs, k) - lax.axis_index("lev") * slab_dev
        inside = (off >= 0) & (off < slab_dev)
        spots[0, k] = jnp.where(inside, off, 0) * mem_dev
        spots[1, k] = across * ny + row
        spots[2, k] = jnp.where(inside, wanted, LANES)
    sub = lax.broadcasted_iota(jnp.int32, (TILE, LANES), 0)
    lane = lax.broadcasted_iota(jnp.int32, (TILE, LANES), 1)
    east_edge, west_edge = lane == LANES - 1, lane == 0
    high = ny // TILE

    def spot(r, t):
        return slice(t * ny + r * TILE, t * ny + (r + 1) * TILE)

    def advance(load, keep, store):
        for r in range(high):
            row = TILE + r * TILE
            ahead, behind = {}, {}
            for m in range(mem_dev):
                for t in range(tiles):
                    f = load(m, t, row)
                    ahead[m, t] = pltpu.roll(f, LANES - 1, 1)
                    behind[m, t] = pltpu.roll(f, 1, 1)
            for t in range(tiles):
                at = spot(r, t)
                east_w, west_w = weights[0, at, :], weights[1, at, :]
                north_w, south_w = weights[2, at, :], weights[3, at, :]
                for m in range(mem_dev):
                    f = load(m, t, row)
                    east = jnp.where(east_edge, ahead.get((m, t + 1), f), ahead[m, t])
                    west = jnp.where(west_edge, behind.get((m, t - 1), f), behind[m, t])
                    store(
                        m,
                        r,
                        t,
                        (keep * f + east_w * east)
                        + (west_w * west + north_w * load(m, t, row + 1))
                        + south_w * load(m, t, row - 1),
                    )

    for (start, count, whole), blocks in zip(parts, outs):

        def one(s, carry):
            slab = start + s
            for copy in loads(slab):
                copy.wait()
            diffuse = spread[slab]
            keep = 1.0 - 4.0 * diffuse
            for r in range(high):
                for t in range(tiles):
                    tile = (slice(r * TILE, (r + 1) * TILE), slice(t * LANES, (t + 1) * LANES))
                    half_v, half_h = 0.5 * cv_buf[slab, *tile], 0.5 * ch_buf[slab, *tile]
                    weights[0, spot(r, t), :] = diffuse - half_v
                    weights[1, spot(r, t), :] = diffuse + half_v
                    weights[2, spot(r, t), :] = diffuse - half_h
                    weights[3, spot(r, t), :] = diffuse + half_h
            for m in range(mem_dev):
                for t in range(tiles):
                    x_buf[slab, m, t, TILE - 1 : TILE, :] = x_buf[slab, m, t, TILE : TILE + 1, :]
                    x_buf[slab, m, t, TILE + ny : TILE + ny + 1, :] = x_buf[
                        slab, m, t, TILE + ny - 1 : TILE + ny, :
                    ]

            def first(m, t, row):
                return x_buf[slab, m, t, row : row + TILE, :]

            def later(m, t, row):
                return half[m, t, row : row + TILE, :]

            def between(m, r, t, value):
                row = TILE + r * TILE
                half[m, t, row : row + TILE, :] = value
                if r == 0:
                    half[m, t, TILE - 1 : TILE, :] = value[0:1, :]
                if r == high - 1:
                    half[m, t, TILE + ny : TILE + ny + 1, :] = value[TILE - 1 : TILE, :]

            def final(m, r, t, value):
                field[slab * mem_dev + m, spot(r, t), :] = value

            for step in range(STEPS):
                load, store = later if step else first, between if step < STEPS - 1 else final
                advance(load, keep, store)
            for m in range(mem_dev):
                at = pl.multiple_of((m * count + s) * depth, TILE)
                for ref, d in blocks:
                    for t in range(tiles):
                        row = pl.multiple_of(t * ny + d * block, block)
                        ref[pl.ds(at + t * block, block), :] = field[
                            slab * mem_dev + m, pl.ds(row, block), :
                        ]
            return carry

        lax.fori_loop(0, count, one, 0)

    line_lane = lax.broadcasted_iota(jnp.int32, (1, LANES), 1)
    for k in range(total):
        level, row, wanted = spots[0, k], spots[1, k], spots[2, k]
        for m in range(mem_dev):
            line = field[level + m, pl.ds(row, 1), :]
            picks[m, pl.ds(k, 1), :] = jnp.where(line_lane == wanted, line, 0.0)
    diagonal = lax.broadcasted_iota(jnp.int32, (total, LANES), 0) == lax.broadcasted_iota(
        jnp.int32, (total, LANES), 1
    )
    values = []
    for m in range(mem_dev):
        value = jnp.sum(picks[m], axis=1, keepdims=True)
        values.append(jnp.sum(jnp.where(diagonal, value, 0.0), axis=0, keepdims=True))
    for j in range(n):
        seen = jnp.zeros((TILE, LANES), jnp.float32)
        for m in range(mem_dev):
            seen = jnp.where(sub == (j * mem_dev + m) % TILE, values[m], seen)
        outs[0][j][0][pl.ds(mem_dev * parts[0][1] * depth, TILE), :] = seen


def forecast(parts, n, cells, slabs, spread, x, cv, ch):
    mem_dev, slab_dev, ny, nx = x.shape
    depth = ny // n * nx // LANES
    shapes = []
    for i, (_, count, whole) in enumerate(parts):
        shapes.append(block_shapes(n, whole, mem_dev * count * depth + (0 if i else TILE)))
    outs = pl.pallas_call(
        functools.partial(forecast_kernel, parts, n),
        in_specs=[pl.BlockSpec(memory_space=pltpu.HBM)] * 6,
        out_specs=[VMEM for group in shapes for _ in group],
        out_shape=[shape for group in shapes for shape in group],
        scratch_shapes=[
            pltpu.VMEM((slab_dev, mem_dev, nx // LANES, ny + 2 * TILE, LANES), jnp.float32),
            pltpu.VMEM(cv.shape, jnp.float32),
            pltpu.VMEM(ch.shape, jnp.float32),
            pltpu.SMEM(cells.shape, jnp.int32),
            pltpu.SMEM(slabs.shape, jnp.int32),
            pltpu.SMEM(spread.shape, jnp.float32),
            pltpu.SMEM((3, cells.size), jnp.int32),
            pltpu.VMEM((slab_dev * mem_dev, ny * nx // LANES, LANES), jnp.float32),
            pltpu.VMEM((mem_dev, nx // LANES, ny + 2 * TILE, LANES), jnp.float32),
            pltpu.VMEM((4, ny * nx // LANES, LANES), jnp.float32),
            pltpu.VMEM((mem_dev, cells.size, LANES), jnp.float32),
            pltpu.SemaphoreType.DMA((2 + nx // LANES, slab_dev)),
            pltpu.SemaphoreType.DMA((3,)),
        ],
        cost_estimate=cost(60 * x.size, 4 * (2 * x.size + 2 * cv.size)),
        compiler_params=params(),
        name="forecast",
    )(*[pltpu.with_memory_space_constraint(a, pltpu.HBM) for a in (cells, slabs, spread, x, cv, ch)])
    sends = []
    for group in shapes:
        sends.append(list(outs[: len(group)]))
        outs = outs[len(group) :]
    return sends


def reach(cells, lists, nx, block, groups):
    total = cells.shape[0] * cells.shape[1]
    me = lax.axis_index("mem")
    for g in range(groups):
        count = jnp.int32(0)
        low_col = g * TILE // block * LANES
        high_col = (g * TILE + TILE - 1) // block * LANES + LANES - 1
        low_row = me * block + g * TILE % block
        high_row = low_row + min(block, TILE) - 1
        for k in range(total):
            row, col = row_col(place(cells, k), nx)
            down = jnp.maximum(jnp.maximum(low_row - row, row - high_row), 0)
            across = jnp.maximum(jnp.maximum(low_col - col, col - high_col), 0)
            lists[g, count] = jnp.int32(k)
            near = down * down + across * across < (2 * LOC_HALF) ** 2
            count = count + near.astype(jnp.int32)
        lists[g, count] = jnp.int32(total)
        lists[g, total + 1] = count


def taper_kernel(nx, block, cells, values_ref, errors_ref, loc_ref, near_ref, meta_ref, out, lists, sem):
    total = near_ref.shape[0]
    depth = loc_ref.shape[1]
    at = lax.broadcasted_iota(jnp.int32, (depth, LANES), 0)
    cell_row = (lax.axis_index("mem") * block + at % block).astype(jnp.float32)
    cell_col = (
        at // block * LANES + lax.broadcasted_iota(jnp.int32, (depth, LANES), 1)
    ).astype(jnp.float32)
    lane = lax.broadcasted_iota(jnp.int32, (1, LANES), 1)
    row_of = jnp.zeros((1, LANES), jnp.float32)
    col_of = jnp.zeros((1, LANES), jnp.float32)
    for k in range(total):
        row, col = row_col(place(cells, k), nx)
        row, col = row.astype(jnp.float32), col.astype(jnp.float32)
        row_of = jnp.where(lane == k, row, row_of)
        col_of = jnp.where(lane == k, col, col_of)
        loc_ref[k] = taper(cell_row - row, cell_col - col)
        meta_ref[k, 0:1, :] = jnp.full((1, LANES), place(errors_ref, k), jnp.float32)
        meta_ref[k, 1:2, :] = jnp.full((1, LANES), place(values_ref, k), jnp.float32)
    loc_ref[total] = jnp.zeros((depth, LANES), jnp.float32)
    reach(cells, lists, nx, block, depth // TILE)
    copy = pltpu.make_async_copy(lists, out, sem)
    copy.start()
    diagonal = lax.broadcasted_iota(jnp.int32, (total, LANES), 0) == lax.broadcasted_iota(
        jnp.int32, (total, LANES), 1
    )
    own_row = jnp.sum(jnp.where(diagonal, row_of, 0.0), axis=1, keepdims=True)
    own_col = jnp.sum(jnp.where(diagonal, col_of, 0.0), axis=1, keepdims=True)
    near_ref[...] = taper(row_of - own_row, col_of - own_col)
    copy.wait()


def list_shape(depth):
    return (-(-depth // TILE // TILE) * TILE, LANES)


def taper_tables(nx, block, cells, values, errors):
    total = cells.size
    depth = block * nx // LANES
    return pl.pallas_call(
        functools.partial(taper_kernel, nx, block),
        in_specs=[SMEM] * 3,
        out_specs=[VMEM] * 4,
        out_shape=[
            jax.ShapeDtypeStruct((total + 1, depth, LANES), jnp.float32),
            jax.ShapeDtypeStruct((total, LANES), jnp.float32),
            jax.ShapeDtypeStruct((total, TILE, LANES), jnp.float32),
            jax.ShapeDtypeStruct(list_shape(depth), jnp.int32),
        ],
        scratch_shapes=[pltpu.SMEM(list_shape(depth), jnp.int32), pltpu.SemaphoreType.DMA(())],
        cost_estimate=cost(60 * total * depth * LANES, 4 * total * depth * LANES),
        compiler_params=params(),
        name="taper_tables",
    )(cells, values, errors)


def settle_blocks(n, mem_dev, count, depth, lists, anom_ref, incr_ref, loc_ref, ins, outs):
    total = loc_ref.shape[0] - 1
    members = n * mem_dev
    group = max(g for g in range(1, count + 1) if count % g == 0 and (g == 1 or g * members <= 48))
    turns = count // group

    def spread(ref, k, m):
        return ref[k, pl.ds(m, TILE, stride=0), :]

    def part(i, carry):
        tile, slab = i // turns, i % turns * group
        at = tile * TILE

        def spot(m, g):
            row = ((m % mem_dev) * count + slab + g) * depth + at
            return m // mem_dev, pl.ds(pl.multiple_of(row, TILE), TILE)

        xs = []
        for m in range(members):
            for g in range(group):
                src, row = spot(m, g)
                xs.append(ins[src][0][row, :])

        def step(k, xs):
            terms = [[] for _ in range(group)]
            for m in range(members):
                a = spread(anom_ref, k, m)
                for g in range(group):
                    terms[g].append(a * xs[m * group + g])
            loc = loc_ref[k, pl.ds(pl.multiple_of(at, TILE), TILE), :]
            for g in range(group):
                while len(terms[g]) > 1:
                    odd = terms[g][len(terms[g]) // 2 * 2 :]
                    terms[g] = [a + b for a, b in zip(terms[g][::2], terms[g][1::2])] + odd
            sums = [terms[g][0] * loc for g in range(group)]
            new = []
            for m in range(members):
                b = spread(incr_ref, k, m)
                for g in range(group):
                    new.append(xs[m * group + g] + b * sums[g])
            return new

        def two(i, xs):
            return tuple(step(lists[tile, 2 * i + 1], step(lists[tile, 2 * i], list(xs))))

        xs = lax.fori_loop(
            0, lax.shift_right_logical(lists[tile, total + 1] + 1, 1), two, tuple(xs)
        )
        for m in range(members):
            for g in range(group):
                src, row = spot(m, g)
                outs[src][0][row, :] = xs[m * group + g]
        return carry

    lax.fori_loop(0, depth // TILE * turns, part, 0)


def plan_kernel(n, mem_dev, count, lev, loc_ref, near_ref, meta_ref, lists_ref, *refs):
    seen_refs, refs = refs[:lev], refs[lev:]
    ins, refs = blocks_in(refs[:n], n, False), refs[n:]
    anom_ref, incr_ref = refs[:2]
    outs = blocks_in(refs[2 : 2 + n], n, False)
    lists, sem = refs[2 + n :]
    copy = pltpu.make_async_copy(lists_ref, lists, sem)
    copy.start()
    total, depth = near_ref.shape[0], loc_ref.shape[1]
    rows = seen_refs[0][...]
    for other in seen_refs[1:]:
        rows = rows + other[...]
    members = rows.shape[0]
    mean = jnp.sum(rows, axis=0, keepdims=True) * (1.0 / members)
    rows = rows - mean
    for k in range(total):
        error, value = meta_ref[k, 0:1, :], meta_ref[k, 1:2, :]
        anomaly = jnp.broadcast_to(rows[:, k : k + 1], rows.shape)
        ybar = jnp.broadcast_to(mean[:, k : k + 1], mean.shape)
        variance = jnp.sum(anomaly * anomaly, axis=0, keepdims=True) / (members - 1) + 1e-06
        shared = jnp.sum(rows * anomaly, axis=0, keepdims=True)
        scale = 1.0 / ((members - 1) * variance)
        shift = (ybar * error + value * variance) / (variance + error) - ybar
        shrink = jnp.sqrt(error / (variance + error)) - 1.0
        anom_ref[k, 0:members, :] = anomaly * scale
        incr_ref[k, 0:members, :] = shift + shrink * anomaly
        weight = near_ref[k : k + 1, :] * shared * scale
        mean = mean + weight * shift
        rows = rows + (weight * shrink) * anomaly
    anom_ref[total] = jnp.zeros(anom_ref.shape[1:], jnp.float32)
    incr_ref[total] = jnp.zeros(incr_ref.shape[1:], jnp.float32)
    copy.wait()
    settle_blocks(n, mem_dev, count, depth, lists, anom_ref, incr_ref, loc_ref, ins, outs)


def filter_plan(mem_dev, count, places, seen, xs):
    members = seen[0].shape[0]
    n = len(xs)
    total, depth = places[1].shape[0], places[0].shape[1]
    table = jax.ShapeDtypeStruct((total + 1, members + TILE, LANES), jnp.float32)
    shapes = [table, table] + block_shapes(n, False, mem_dev * count * depth)
    got = pl.pallas_call(
        functools.partial(plan_kernel, n, mem_dev, count, len(seen)),
        in_specs=[VMEM] * (4 + len(seen) + n),
        out_specs=[VMEM] * len(shapes),
        out_shape=shapes,
        scratch_shapes=[pltpu.SMEM(list_shape(depth), jnp.int32), pltpu.SemaphoreType.DMA(())],
        cost_estimate=cost(20_000_000, 4 * total * (2 * members + depth) * LANES),
        compiler_params=params(),
        name="filter_plan",
    )(*places, *seen, *xs)
    return got[:2], list(got[2:])


def settle_kernel(n, mem_dev, count, depth, whole, lists_ref, anom, incr, loc, *refs):
    width = 1 if whole else n
    ins, outs = blocks_in(refs[:width], n, whole), blocks_in(refs[width:-2], n, False)
    lists, sem = refs[-2:]
    copy = pltpu.make_async_copy(lists_ref, lists, sem)
    copy.start()
    copy.wait()
    settle_blocks(n, mem_dev, count, depth, lists, anom, incr, loc, ins, outs)


def settle(n, mem_dev, count, whole, places, tables, xs):
    loc, lists = places[0], places[3]
    depth = loc.shape[1]
    shapes = block_shapes(n, False, mem_dev * count * depth)
    size = n * mem_dev * count * depth * LANES
    return pl.pallas_call(
        functools.partial(settle_kernel, n, mem_dev, count, depth, whole),
        in_specs=[VMEM] * (4 + len(xs)),
        out_specs=[VMEM] * len(shapes),
        out_shape=shapes,
        scratch_shapes=[pltpu.SMEM(list_shape(depth), jnp.int32), pltpu.SemaphoreType.DMA(())],
        cost_estimate=cost(4 * loc.shape[0] * size, 8 * size),
        compiler_params=params(),
        name="settle",
    )(lists, *tables, loc, *xs)


def assemble_kernel(n, start, count, *refs):
    out_ref, stage, turn, sem = refs[-4:]
    blocks = blocks_in(refs[:n], n, False)
    mem_dev, _, ny, nx = out_ref.shape
    block = ny // n
    tiles = nx // LANES
    depth = block * tiles
    copies = []
    for slab in range(count):
        for m in range(mem_dev):
            at = (m * count + slab) * depth
            for t in range(tiles):
                lanes = slice(t * LANES, (t + 1) * LANES)
                lines = slice(at + t * block, at + (t + 1) * block)
                for j, (ref, d) in enumerate(blocks):
                    if block % TILE == 0:
                        row = pl.multiple_of(d * block, block)
                        stage[m, slab, pl.ds(row, block), lanes] = ref[lines, :]
                    else:
                        turn[j * block : (j + 1) * block, :] = ref[lines, :]
                if block % TILE:
                    for d, (_, j) in enumerate(blocks):
                        stage[m, slab, d * block : (d + 1) * block, lanes] = turn[
                            pl.ds(j * block, block), :
                        ]
        copies.append(
            pltpu.make_async_copy(
                stage.at[:, slab], out_ref.at[:, start + slab], sem.at[slab]
            )
        )
        copies[-1].start()
    for copy in copies:
        copy.wait()


def assemble(n, start, count, recv, shape, before):
    mem_dev, _, ny, nx = shape
    extra = [] if before is None else [before]
    return pl.pallas_call(
        functools.partial(assemble_kernel, n, start, count),
        in_specs=[VMEM] * n + [pl.BlockSpec(memory_space=pl.ANY)] * len(extra),
        out_specs=pl.BlockSpec(memory_space=pl.ANY),
        out_shape=jax.ShapeDtypeStruct(shape, jnp.float32),
        scratch_shapes=[
            pltpu.VMEM((mem_dev, count, ny, nx), jnp.float32),
            pltpu.VMEM((ny, LANES), jnp.float32),
            pltpu.SemaphoreType.DMA((count,)),
        ],
        input_output_aliases={} if before is None else {n: 0},
        cost_estimate=cost(0, 8 * n * recv[0].size),
        compiler_params=params(),
        name="assemble",
    )(*recv, *extra)


def order_of(n, near_first=False):
    far, near = list(range(n // 2, n)), list(range(2, n // 2)) + [1]
    if near_first:
        return near + far
    return [j for pair in zip(far, near) for j in pair] + far[len(near) :]


def exchange(blocks, n, whole, near_first=False):
    if whole:
        return [lax.all_to_all(blocks[0], "mem", split_axis=0, concat_axis=0, tiled=True)]
    got = {}
    for j in order_of(n, near_first):
        got[j] = lax.ppermute(blocks[j], "mem", [(i, i ^ j) for i in range(n)])
    return blocks[:1] + [got[j] for j in range(1, n)]


def body(x, cv, ch, spread, obs_cells, obs_slabs, obs_values, obs_error):
    mem_dev, slab_dev, ny, nx = x.shape
    n, lev = lax.axis_size("mem"), lax.axis_size("lev")
    block = ny // n
    depth = block * nx // LANES
    parts = chunks_of(slab_dev)
    sends = forecast(parts, n, obs_cells, obs_slabs, spread, x, cv, ch)
    states = []
    for c, blocks in enumerate(sends):
        states.append(exchange(blocks, n, parts[c][2]))
    per = TILE // mem_dev
    seen = [s[mem_dev * parts[0][1] * depth :, :] for s in states[0]]
    seen = jnp.concatenate([sum(seen[g : g + per]) for g in range(0, n, per)])
    tiles = [seen] + [
        lax.ppermute(seen, "lev", [(i, (i + d) % lev) for i in range(lev)])
        for d in range(1, lev)
    ]
    places = taper_tables(nx, block, obs_cells, obs_values, obs_error)
    result = None
    for c, ((start, count, whole), state) in enumerate(zip(parts, states)):
        if c == 0:
            tables, new = filter_plan(mem_dev, count, places, tiles, state)
        else:
            new = settle(n, mem_dev, count, whole, places, tables, state)
        back = exchange(list(new), n, False, near_first=c == 0)
        result = assemble(n, start, count, back, x.shape, result)
    return result


def solution(mesh):
    in_specs = (
        P("mem", "lev", None, None),
        P("lev", None, None),
        P("lev", None, None),
        P("lev"),
        P(),
        P(),
        P(),
        P(),
    )
    out_specs = P("mem", "lev", None, None)
    return jax.shard_map(body, mesh=mesh, in_specs=in_specs, out_specs=out_specs, check_vma=False)
```

```python
import functools

import jax
import jax.numpy as jnp
from jax import lax
from jax.experimental import pallas as pl
from jax.experimental.pallas import tpu as pltpu
from jax.sharding import PartitionSpec as P


STEPS = 2
LOC_HALF = 64
LANES = 128
GRANT = 24 * 1024 * 1024
TILE = 8
VMEM = pl.BlockSpec(memory_space=pltpu.VMEM)
SMEM = pl.BlockSpec(memory_space=pltpu.SMEM)


def cost(flops, nbytes):
    return pl.CostEstimate(flops=flops, bytes_accessed=nbytes, transcendentals=0)


def taper(row_gap, col_gap):
    scaled = jnp.sqrt(row_gap * row_gap + col_gap * col_gap) * (1.0 / LOC_HALF)
    inner = (
        ((-0.25 * scaled + 0.5) * scaled + 0.625) * scaled - 5.0 / 3.0
    ) * scaled * scaled + 1.0
    safe = jnp.maximum(scaled, 1.0)
    outer = (
        ((((scaled * (1.0 / 12.0) - 0.5) * scaled + 0.625) * scaled + 5.0 / 3.0) * scaled - 5.0)
        * scaled
        + 4.0
        - (2.0 / 3.0) / safe
    )
    return jnp.where(scaled <= 1.0, inner, jnp.where(scaled < 2.0, outer, 0.0))


def chunks_of(slab_dev):
    first = max(1, (2 * slab_dev) // 5)
    if slab_dev == 1:
        return ((0, 1, False),)
    return ((0, first, False), (first, slab_dev - first, True))


def row_col(cell, nx):
    if nx & (nx - 1):
        return cell // nx, cell % nx
    return lax.shift_right_logical(cell, nx.bit_length() - 1), cell & (nx - 1)


def place(ref, k):
    return ref[k // ref.shape[1], k % ref.shape[1]]


def params():
    return pltpu.CompilerParams(vmem_limit_bytes=GRANT)


def blocks_in(refs, n, whole):
    me = lax.axis_index("mem")
    return [(refs[0].at[me ^ j] if whole else refs[j], me ^ j) for j in range(n)]


def block_shapes(n, whole, rows):
    if whole:
        return [jax.ShapeDtypeStruct((n, rows, LANES), jnp.float32)]
    return [jax.ShapeDtypeStruct((rows, LANES), jnp.float32)] * n


def forecast_kernel(parts, n, cells_hbm, slabs_hbm, spread_hbm, x_hbm, cv_hbm, ch_hbm, *rest):
    outs, arrays = [], []
    for start, count, whole in parts:
        width = 1 if whole else n
        arrays.append(rest[:width])
        outs.append(blocks_in(rest[:width], n, whole))
        rest = rest[width:]
    x_buf, cv_buf, ch_buf, cells, slabs, spread, spots, field, half, weights, picks = rest[:-2]
    sem, small = rest[-2:]
    mem_dev, slab_dev, tiles = x_buf.shape[:3]
    ny, nx = x_buf.shape[3] - 2 * TILE, tiles * LANES
    block = ny // n
    depth = block * tiles
    total = cells.shape[0] * cells.shape[1]

    def loads(c):
        slabs_of = slice(parts[c][0], parts[c][0] + parts[c][1])
        return [
            pltpu.make_async_copy(cv_hbm.at[slabs_of], cv_buf.at[slabs_of], sem.at[tiles, c]),
            pltpu.make_async_copy(ch_hbm.at[slabs_of], ch_buf.at[slabs_of], sem.at[tiles + 1, c]),
        ] + [
            pltpu.make_async_copy(
                x_hbm.at[:, slabs_of, :, t * LANES : (t + 1) * LANES],
                x_buf.at[:, slabs_of, t, TILE : TILE + ny, :],
                sem.at[t, c],
            )
            for t in range(tiles)
        ]

    lists = (
        pltpu.make_async_copy(spread_hbm, spread, small.at[0]),
        pltpu.make_async_copy(cells_hbm, cells, small.at[1]),
        pltpu.make_async_copy(slabs_hbm, slabs, small.at[2]),
    )
    for copy in [*loads(0), *lists] + [copy for c in range(1, len(parts)) for copy in loads(c)]:
        copy.start()
    for copy in lists:
        copy.wait()
    for k in range(total):
        row, col = row_col(place(cells, k), nx)
        across, wanted = row_col(col, LANES)
        off = place(slabs, k) - lax.axis_index("lev") * slab_dev
        inside = (off >= 0) & (off < slab_dev)
        spots[0, k] = jnp.where(inside, off, 0) * mem_dev
        spots[1, k] = across * ny + row
        spots[2, k] = jnp.where(inside, wanted, LANES)
    sub = lax.broadcasted_iota(jnp.int32, (TILE, LANES), 0)
    lane = lax.broadcasted_iota(jnp.int32, (TILE, LANES), 1)
    east_edge, west_edge = lane == LANES - 1, lane == 0
    high = ny // TILE

    def spot(r, t):
        return slice(t * ny + r * TILE, t * ny + (r + 1) * TILE)

    def advance(turn, load, keep, store):
        for r in range(high):
            row = TILE + r * TILE
            ahead, behind = {}, {}
            for m in range(mem_dev):
                for t in range(tiles):
                    f = load(m, t, row)
                    ahead[m, t] = pltpu.roll(f, LANES - 1, 1)
                    behind[m, t] = pltpu.roll(f, 1, 1)
            for t in range(tiles):
                at = spot(r, t)
                east_w, west_w = weights[turn, 0, at, :], weights[turn, 1, at, :]
                north_w, south_w = weights[turn, 2, at, :], weights[turn, 3, at, :]
                for m in range(mem_dev):
                    f = load(m, t, row)
                    east = jnp.where(east_edge, ahead.get((m, t + 1), f), ahead[m, t])
                    west = jnp.where(west_edge, behind.get((m, t - 1), f), behind[m, t])
                    if r + 1 < high:
                        north = load(m, t, row + 1)
                    else:
                        north = jnp.where(sub == TILE - 1, f, pltpu.roll(f, TILE - 1, 0))
                    if r > 0:
                        south = load(m, t, row - 1)
                    else:
                        south = jnp.where(sub == 0, f, pltpu.roll(f, 1, 0))
                    store(
                        m,
                        r,
                        t,
                        (keep * f + east_w * east)
                        + (west_w * west + north_w * north)
                        + south_w * south,
                    )

    for c, ((start, count, whole), blocks) in enumerate(zip(parts, outs)):
        direct = whole and block % TILE == 0
        for copy in loads(c):
            copy.wait()
        for s in range(count):
            slab = start + s
            diffuse = spread[slab]
            keep = 1.0 - 4.0 * diffuse
            for r in range(high):
                for t in range(tiles):
                    tile = (slice(r * TILE, (r + 1) * TILE), slice(t * LANES, (t + 1) * LANES))
                    half_v, half_h = 0.5 * cv_buf[slab, *tile], 0.5 * ch_buf[slab, *tile]
                    weights[s % 2, 0, spot(r, t), :] = diffuse - half_v
                    weights[s % 2, 1, spot(r, t), :] = diffuse + half_v
                    weights[s % 2, 2, spot(r, t), :] = diffuse - half_h
                    weights[s % 2, 3, spot(r, t), :] = diffuse + half_h

            def first(m, t, row):
                return x_buf[m, slab, t, row : row + TILE, :]

            def later(m, t, row):
                return half[s % 2 * mem_dev + m, t, row : row + TILE, :]

            def between(m, r, t, value):
                row = TILE + r * TILE
                half[s % 2 * mem_dev + m, t, row : row + TILE, :] = value

            def final(m, r, t, value):
                field[slab * mem_dev + m, spot(r, t), :] = value
                if direct:
                    at = (m * count + s) * depth + t * block + r * TILE % block
                    arrays[c][0][r * TILE // block, at : at + TILE, :] = value

            for step in range(STEPS):
                load, store = later if step else first, between if step < STEPS - 1 else final
                advance(s % 2, load, keep, store)

        def send(i, carry):
            level = start * mem_dev + i
            at = pl.multiple_of((i % mem_dev * count + i // mem_dev) * depth, TILE)
            for ref, d in blocks:
                for t in range(tiles):
                    row = pl.multiple_of(t * ny + d * block, block)
                    ref[pl.ds(at + t * block, block), :] = field[level, pl.ds(row, block), :]
            return carry

        if not direct:
            lax.fori_loop(0, count * mem_dev, send, 0)

    line_lane = lax.broadcasted_iota(jnp.int32, (1, LANES), 1)
    for k in range(total):
        level, row, wanted = spots[0, k], spots[1, k], spots[2, k]
        for m in range(mem_dev):
            line = field[level + m, pl.ds(row, 1), :]
            picks[m, pl.ds(k, 1), :] = jnp.where(line_lane == wanted, line, 0.0)
    diagonal = lax.broadcasted_iota(jnp.int32, (total, LANES), 0) == lax.broadcasted_iota(
        jnp.int32, (total, LANES), 1
    )
    values = []
    for m in range(mem_dev):
        value = jnp.sum(picks[m], axis=1, keepdims=True)
        values.append(jnp.sum(jnp.where(diagonal, value, 0.0), axis=0, keepdims=True))
    for j in range(n):
        seen = jnp.zeros((TILE, LANES), jnp.float32)
        for m in range(mem_dev):
            seen = jnp.where(sub == (j * mem_dev + m) % TILE, values[m], seen)
        outs[0][j][0][pl.ds(mem_dev * parts[0][1] * depth, TILE), :] = seen


def forecast(parts, n, cells, slabs, spread, x, cv, ch):
    mem_dev, slab_dev, ny, nx = x.shape
    depth = ny // n * nx // LANES
    shapes = []
    for i, (_, count, whole) in enumerate(parts):
        shapes.append(block_shapes(n, whole, mem_dev * count * depth + (0 if i else TILE)))
    outs = pl.pallas_call(
        functools.partial(forecast_kernel, parts, n),
        in_specs=[pl.BlockSpec(memory_space=pltpu.HBM)] * 6,
        out_specs=[VMEM for group in shapes for _ in group],
        out_shape=[shape for group in shapes for shape in group],
        scratch_shapes=[
            pltpu.VMEM((mem_dev, slab_dev, nx // LANES, ny + 2 * TILE, LANES), jnp.float32),
            pltpu.VMEM(cv.shape, jnp.float32),
            pltpu.VMEM(ch.shape, jnp.float32),
            pltpu.SMEM(cells.shape, jnp.int32),
            pltpu.SMEM(slabs.shape, jnp.int32),
            pltpu.SMEM(spread.shape, jnp.float32),
            pltpu.SMEM((3, cells.size), jnp.int32),
            pltpu.VMEM((slab_dev * mem_dev, ny * nx // LANES, LANES), jnp.float32),
            pltpu.VMEM((2 * mem_dev, nx // LANES, ny + 2 * TILE, LANES), jnp.float32),
            pltpu.VMEM((2, 4, ny * nx // LANES, LANES), jnp.float32),
            pltpu.VMEM((mem_dev, cells.size, LANES), jnp.float32),
            pltpu.SemaphoreType.DMA((2 + nx // LANES, len(parts))),
            pltpu.SemaphoreType.DMA((3,)),
        ],
        cost_estimate=cost(60 * x.size, 4 * (2 * x.size + 2 * cv.size)),
        compiler_params=params(),
        name="forecast",
    )(*[pltpu.with_memory_space_constraint(a, pltpu.HBM) for a in (cells, slabs, spread, x, cv, ch)])
    sends = []
    for group in shapes:
        sends.append(list(outs[: len(group)]))
        outs = outs[len(group) :]
    return sends


def reach(cells, lists, nx, block, groups):
    total = cells.shape[0] * cells.shape[1]
    me = lax.axis_index("mem")
    for g in range(groups):
        count = jnp.int32(0)
        low_col = g * TILE // block * LANES
        high_col = (g * TILE + TILE - 1) // block * LANES + LANES - 1
        low_row = me * block + g * TILE % block
        high_row = low_row + min(block, TILE) - 1
        for k in range(total):
            row, col = row_col(place(cells, k), nx)
            down = jnp.maximum(jnp.maximum(low_row - row, row - high_row), 0)
            across = jnp.maximum(jnp.maximum(low_col - col, col - high_col), 0)
            lists[g, count] = jnp.int32(k)
            near = down * down + across * across < (2 * LOC_HALF) ** 2
            count = count + near.astype(jnp.int32)
        lists[g, count] = jnp.int32(total)
        lists[g, total + 1] = count


def taper_kernel(nx, block, cells, values_ref, errors_ref, loc_ref, near_ref, meta_ref, out, lists, sem):
    total = near_ref.shape[0]
    depth = loc_ref.shape[1]
    at = lax.broadcasted_iota(jnp.int32, (depth, LANES), 0)
    cell_row = (lax.axis_index("mem") * block + at % block).astype(jnp.float32)
    cell_col = (
        at // block * LANES + lax.broadcasted_iota(jnp.int32, (depth, LANES), 1)
    ).astype(jnp.float32)
    lane = lax.broadcasted_iota(jnp.int32, (1, LANES), 1)
    row_of = jnp.zeros((1, LANES), jnp.float32)
    col_of = jnp.zeros((1, LANES), jnp.float32)
    for k in range(total):
        row, col = row_col(place(cells, k), nx)
        row, col = row.astype(jnp.float32), col.astype(jnp.float32)
        row_of = jnp.where(lane == k, row, row_of)
        col_of = jnp.where(lane == k, col, col_of)
        loc_ref[k] = taper(cell_row - row, cell_col - col)
        meta_ref[k, 0:1, :] = jnp.full((1, LANES), place(errors_ref, k), jnp.float32)
        meta_ref[k, 1:2, :] = jnp.full((1, LANES), place(values_ref, k), jnp.float32)
    loc_ref[total] = jnp.zeros((depth, LANES), jnp.float32)
    reach(cells, lists, nx, block, depth // TILE)
    copy = pltpu.make_async_copy(lists, out, sem)
    copy.start()
    diagonal = lax.broadcasted_iota(jnp.int32, (total, LANES), 0) == lax.broadcasted_iota(
        jnp.int32, (total, LANES), 1
    )
    own_row = jnp.sum(jnp.where(diagonal, row_of, 0.0), axis=1, keepdims=True)
    own_col = jnp.sum(jnp.where(diagonal, col_of, 0.0), axis=1, keepdims=True)
    near_ref[...] = taper(row_of - own_row, col_of - own_col)
    copy.wait()


def list_shape(depth):
    return (-(-depth // TILE // TILE) * TILE, LANES)


def taper_tables(nx, block, cells, values, errors):
    total = cells.size
    depth = block * nx // LANES
    return pl.pallas_call(
        functools.partial(taper_kernel, nx, block),
        in_specs=[SMEM] * 3,
        out_specs=[VMEM] * 4,
        out_shape=[
            jax.ShapeDtypeStruct((total + 1, depth, LANES), jnp.float32),
            jax.ShapeDtypeStruct((total, LANES), jnp.float32),
            jax.ShapeDtypeStruct((total, TILE, LANES), jnp.float32),
            jax.ShapeDtypeStruct(list_shape(depth), jnp.int32),
        ],
        scratch_shapes=[pltpu.SMEM(list_shape(depth), jnp.int32), pltpu.SemaphoreType.DMA(())],
        cost_estimate=cost(60 * total * depth * LANES, 4 * total * depth * LANES),
        compiler_params=params(),
        name="taper_tables",
    )(cells, values, errors)


def settle_blocks(n, mem_dev, count, depth, lists, anom_ref, incr_ref, loc_ref, ins, outs):
    total = loc_ref.shape[0] - 1
    members = n * mem_dev
    group = max(g for g in range(1, count + 1) if count % g == 0 and (g == 1 or g * members <= 48))
    turns = count // group

    def spread(ref, k, m):
        return ref[k, pl.ds(m, TILE, stride=0), :]

    def part(i, carry):
        tile, slab = i // turns, i % turns * group
        at = tile * TILE

        def spot(m, g):
            row = ((m % mem_dev) * count + slab + g) * depth + at
            return m // mem_dev, pl.ds(pl.multiple_of(row, TILE), TILE)

        xs = []
        for m in range(members):
            for g in range(group):
                src, row = spot(m, g)
                xs.append(ins[src][0][row, :])

        def step(k, xs):
            terms = [[] for _ in range(group)]
            for m in range(members):
                a = spread(anom_ref, k, m)
                for g in range(group):
                    terms[g].append(a * xs[m * group + g])
            loc = loc_ref[k, pl.ds(pl.multiple_of(at, TILE), TILE), :]
            for g in range(group):
                while len(terms[g]) > 1:
                    odd = terms[g][len(terms[g]) // 2 * 2 :]
                    terms[g] = [a + b for a, b in zip(terms[g][::2], terms[g][1::2])] + odd
            sums = [terms[g][0] * loc for g in range(group)]
            new = []
            for m in range(members):
                b = spread(incr_ref, k, m)
                for g in range(group):
                    new.append(xs[m * group + g] + b * sums[g])
            return new

        def two(i, xs):
            return tuple(step(lists[tile, 2 * i + 1], step(lists[tile, 2 * i], list(xs))))

        xs = lax.fori_loop(
            0, lax.shift_right_logical(lists[tile, total + 1] + 1, 1), two, tuple(xs)
        )
        for m in range(members):
            for g in range(group):
                src, row = spot(m, g)
                outs[src][0][row, :] = xs[m * group + g]
        return carry

    lax.fori_loop(0, depth // TILE * turns, part, 0)


def plan_kernel(n, mem_dev, count, lev, loc_ref, near_ref, meta_ref, lists_ref, *refs):
    seen_refs, refs = refs[:lev], refs[lev:]
    ins, refs = blocks_in(refs[:n], n, False), refs[n:]
    anom_ref, incr_ref = refs[:2]
    outs = blocks_in(refs[2 : 2 + n], n, False)
    lists, sem = refs[2 + n :]
    copy = pltpu.make_async_copy(lists_ref, lists, sem)
    copy.start()
    total, depth = near_ref.shape[0], loc_ref.shape[1]
    rows = seen_refs[0][...]
    for other in seen_refs[1:]:
        rows = rows + other[...]
    members = rows.shape[0]
    mean = jnp.sum(rows, axis=0, keepdims=True) * (1.0 / members)
    rows = rows - mean
    for k in range(total):
        error, value = meta_ref[k, 0:1, :], meta_ref[k, 1:2, :]
        anomaly = jnp.broadcast_to(rows[:, k : k + 1], rows.shape)
        ybar = jnp.broadcast_to(mean[:, k : k + 1], mean.shape)
        variance = jnp.sum(anomaly * anomaly, axis=0, keepdims=True) / (members - 1) + 1e-06
        shared = jnp.sum(rows * anomaly, axis=0, keepdims=True)
        scale = 1.0 / ((members - 1) * variance)
        shift = (ybar * error + value * variance) / (variance + error) - ybar
        shrink = jnp.sqrt(error / (variance + error)) - 1.0
        anom_ref[k, 0:members, :] = anomaly * scale
        incr_ref[k, 0:members, :] = shift + shrink * anomaly
        weight = near_ref[k : k + 1, :] * shared * scale
        mean = mean + weight * shift
        rows = rows + (weight * shrink) * anomaly
    anom_ref[total] = jnp.zeros(anom_ref.shape[1:], jnp.float32)
    incr_ref[total] = jnp.zeros(incr_ref.shape[1:], jnp.float32)
    copy.wait()
    settle_blocks(n, mem_dev, count, depth, lists, anom_ref, incr_ref, loc_ref, ins, outs)


def filter_plan(mem_dev, count, places, seen, xs):
    members = seen[0].shape[0]
    n = len(xs)
    total, depth = places[1].shape[0], places[0].shape[1]
    table = jax.ShapeDtypeStruct((total + 1, members + TILE, LANES), jnp.float32)
    shapes = [table, table] + block_shapes(n, False, mem_dev * count * depth)
    got = pl.pallas_call(
        functools.partial(plan_kernel, n, mem_dev, count, len(seen)),
        in_specs=[VMEM] * (4 + len(seen) + n),
        out_specs=[VMEM] * len(shapes),
        out_shape=shapes,
        scratch_shapes=[pltpu.SMEM(list_shape(depth), jnp.int32), pltpu.SemaphoreType.DMA(())],
        cost_estimate=cost(20_000_000, 4 * total * (2 * members + depth) * LANES),
        compiler_params=params(),
        name="filter_plan",
    )(*places, *seen, *xs)
    return got[:2], list(got[2:])


def settle_kernel(n, mem_dev, count, depth, whole, lists_ref, anom, incr, loc, *refs):
    width = 1 if whole else n
    ins, outs = blocks_in(refs[:width], n, whole), blocks_in(refs[width:-2], n, False)
    lists, sem = refs[-2:]
    copy = pltpu.make_async_copy(lists_ref, lists, sem)
    copy.start()
    copy.wait()
    settle_blocks(n, mem_dev, count, depth, lists, anom, incr, loc, ins, outs)


def settle(n, mem_dev, count, whole, places, tables, xs):
    loc, lists = places[0], places[3]
    depth = loc.shape[1]
    shapes = block_shapes(n, False, mem_dev * count * depth)
    size = n * mem_dev * count * depth * LANES
    return pl.pallas_call(
        functools.partial(settle_kernel, n, mem_dev, count, depth, whole),
        in_specs=[VMEM] * (4 + len(xs)),
        out_specs=[VMEM] * len(shapes),
        out_shape=shapes,
        scratch_shapes=[pltpu.SMEM(list_shape(depth), jnp.int32), pltpu.SemaphoreType.DMA(())],
        cost_estimate=cost(4 * loc.shape[0] * size, 8 * size),
        compiler_params=params(),
        name="settle",
    )(lists, *tables, loc, *xs)


def assemble_kernel(n, start, count, *refs):
    out_ref, stage, turn, sem = refs[-4:]
    blocks = blocks_in(refs[:n], n, False)
    mem_dev, _, ny, nx = out_ref.shape
    block = ny // n
    tiles = nx // LANES
    depth = block * tiles
    copies = []
    for slab in range(count):
        for m in range(mem_dev):
            at = (m * count + slab) * depth
            for t in range(tiles):
                lanes = slice(t * LANES, (t + 1) * LANES)
                lines = slice(at + t * block, at + (t + 1) * block)
                for j, (ref, d) in enumerate(blocks):
                    if block % TILE == 0:
                        row = pl.multiple_of(d * block, block)
                        stage[m, slab, pl.ds(row, block), lanes] = ref[lines, :]
                    else:
                        turn[j * block : (j + 1) * block, :] = ref[lines, :]
                if block % TILE:
                    for d, (_, j) in enumerate(blocks):
                        stage[m, slab, d * block : (d + 1) * block, lanes] = turn[
                            pl.ds(j * block, block), :
                        ]
        copies.append(
            pltpu.make_async_copy(
                stage.at[:, slab], out_ref.at[:, start + slab], sem.at[slab]
            )
        )
        copies[-1].start()
    for copy in copies:
        copy.wait()


def assemble(n, start, count, recv, shape, before):
    mem_dev, _, ny, nx = shape
    extra = [] if before is None else [before]
    return pl.pallas_call(
        functools.partial(assemble_kernel, n, start, count),
        in_specs=[VMEM] * n + [pl.BlockSpec(memory_space=pl.ANY)] * len(extra),
        out_specs=pl.BlockSpec(memory_space=pl.ANY),
        out_shape=jax.ShapeDtypeStruct(shape, jnp.float32),
        scratch_shapes=[
            pltpu.VMEM((mem_dev, count, ny, nx), jnp.float32),
            pltpu.VMEM((ny, LANES), jnp.float32),
            pltpu.SemaphoreType.DMA((count,)),
        ],
        input_output_aliases={} if before is None else {n: 0},
        cost_estimate=cost(0, 8 * n * recv[0].size),
        compiler_params=params(),
        name="assemble",
    )(*recv, *extra)


def order_of(n, first):
    far, near = list(range(n // 2, n)), list(range(2, n // 2)) + [1]
    if first == "far":
        return far + near
    if first == "near":
        return near + far
    return [j for pair in zip(far, near) for j in pair] + far[len(near) :]


def exchange(blocks, n, whole, first):
    if whole:
        return [lax.all_to_all(blocks[0], "mem", split_axis=0, concat_axis=0, tiled=True)]
    got = {}
    for j in order_of(n, first):
        got[j] = lax.ppermute(blocks[j], "mem", [(i, i ^ j) for i in range(n)])
    return blocks[:1] + [got[j] for j in range(1, n)]


def body(x, cv, ch, spread, obs_cells, obs_slabs, obs_values, obs_error):
    mem_dev, slab_dev, ny, nx = x.shape
    n, lev = lax.axis_size("mem"), lax.axis_size("lev")
    block = ny // n
    depth = block * nx // LANES
    parts = chunks_of(slab_dev)
    sends = forecast(parts, n, obs_cells, obs_slabs, spread, x, cv, ch)
    states = []
    for c, blocks in enumerate(sends):
        states.append(exchange(blocks, n, parts[c][2], "far"))
    per = TILE // mem_dev
    seen = [s[mem_dev * parts[0][1] * depth :, :] for s in states[0]]
    seen = jnp.concatenate([sum(seen[g : g + per]) for g in range(0, n, per)])
    tiles = [seen] + [
        lax.ppermute(seen, "lev", [(i, (i + d) % lev) for i in range(lev)])
        for d in range(1, lev)
    ]
    places = taper_tables(nx, block, obs_cells, obs_values, obs_error)
    result = None
    for c, ((start, count, whole), state) in enumerate(zip(parts, states)):
        if c == 0:
            tables, new = filter_plan(mem_dev, count, places, tiles, state)
        else:
            new = settle(n, mem_dev, count, whole, places, tables, state)
        back = exchange(list(new), n, False, "near" if c == 0 else "turns")
        result = assemble(n, start, count, back, x.shape, result)
    return result


def solution(mesh):
    in_specs = (
        P("mem", "lev", None, None),
        P("lev", None, None),
        P("lev", None, None),
        P("lev"),
        P(),
        P(),
        P(),
        P(),
    )
    out_specs = P("mem", "lev", None, None)
    return jax.shard_map(body, mesh=mesh, in_specs=in_specs, out_specs=out_specs, check_vma=False)
```

```python
import functools

import jax
import jax.numpy as jnp
from jax import lax
from jax.experimental import pallas as pl
from jax.experimental.pallas import tpu as pltpu
from jax.sharding import PartitionSpec as P


STEPS = 2
LOC_HALF = 64
LANES = 128
GRANT = 24 * 1024 * 1024
TILE = 8
VMEM = pl.BlockSpec(memory_space=pltpu.VMEM)
SMEM = pl.BlockSpec(memory_space=pltpu.SMEM)


def cost(flops, nbytes):
    return pl.CostEstimate(flops=flops, bytes_accessed=nbytes, transcendentals=0)


def taper(row_gap, col_gap):
    scaled = jnp.sqrt(row_gap * row_gap + col_gap * col_gap) * (1.0 / LOC_HALF)
    inner = (
        ((-0.25 * scaled + 0.5) * scaled + 0.625) * scaled - 5.0 / 3.0
    ) * scaled * scaled + 1.0
    safe = jnp.maximum(scaled, 1.0)
    outer = (
        ((((scaled * (1.0 / 12.0) - 0.5) * scaled + 0.625) * scaled + 5.0 / 3.0) * scaled - 5.0)
        * scaled
        + 4.0
        - (2.0 / 3.0) / safe
    )
    return jnp.where(scaled <= 1.0, inner, jnp.where(scaled < 2.0, outer, 0.0))


def chunks_of(slab_dev):
    first = max(1, (2 * slab_dev) // 5)
    if slab_dev == 1:
        return ((0, 1, False),)
    return ((0, first, False), (first, slab_dev - first, True))


def row_col(cell, nx):
    if nx & (nx - 1):
        return cell // nx, cell % nx
    return lax.shift_right_logical(cell, nx.bit_length() - 1), cell & (nx - 1)


def place(ref, k):
    return ref[k // ref.shape[1], k % ref.shape[1]]


def params():
    return pltpu.CompilerParams(vmem_limit_bytes=GRANT)


def blocks_in(refs, n, whole):
    me = lax.axis_index("mem")
    return [(refs[0].at[me ^ j] if whole else refs[j], me ^ j) for j in range(n)]


def block_shapes(n, whole, rows):
    if whole:
        return [jax.ShapeDtypeStruct((n, rows, LANES), jnp.float32)]
    return [jax.ShapeDtypeStruct((rows, LANES), jnp.float32)] * n


def forecast_kernel(parts, n, cells_hbm, slabs_hbm, spread_hbm, x_hbm, cv_hbm, ch_hbm, *rest):
    outs, arrays = [], []
    for start, count, whole in parts:
        width = 1 if whole else n
        arrays.append(rest[:width])
        outs.append(blocks_in(rest[:width], n, whole))
        rest = rest[width:]
    x_buf, cv_buf, ch_buf, cells, slabs, spread, spots, field, half, weights, picks = rest[:-2]
    sem, small = rest[-2:]
    mem_dev, slab_dev, tiles = x_buf.shape[:3]
    ny, nx = x_buf.shape[3] - 2 * TILE, tiles * LANES
    block = ny // n
    depth = block * tiles
    total = cells.shape[0] * cells.shape[1]

    def loads(c):
        slabs_of = slice(parts[c][0], parts[c][0] + parts[c][1])
        return [
            pltpu.make_async_copy(cv_hbm.at[slabs_of], cv_buf.at[slabs_of], sem.at[tiles, c]),
            pltpu.make_async_copy(ch_hbm.at[slabs_of], ch_buf.at[slabs_of], sem.at[tiles + 1, c]),
        ] + [
            pltpu.make_async_copy(
                x_hbm.at[:, slabs_of, :, t * LANES : (t + 1) * LANES],
                x_buf.at[:, slabs_of, t, TILE : TILE + ny, :],
                sem.at[t, c],
            )
            for t in range(tiles)
        ]

    lists = (
        pltpu.make_async_copy(spread_hbm, spread, small.at[0]),
        pltpu.make_async_copy(cells_hbm, cells, small.at[1]),
        pltpu.make_async_copy(slabs_hbm, slabs, small.at[2]),
    )
    for copy in [*lists, *loads(0)] + [copy for c in range(1, len(parts)) for copy in loads(c)]:
        copy.start()
    for copy in lists:
        copy.wait()
    for k in range(total):
        row, col = row_col(place(cells, k), nx)
        across, wanted = row_col(col, LANES)
        off = place(slabs, k) - lax.axis_index("lev") * slab_dev
        inside = (off >= 0) & (off < slab_dev)
        spots[0, k] = jnp.where(inside, off, 0) * mem_dev
        spots[1, k] = across * ny + row
        spots[2, k] = jnp.where(inside, wanted, LANES)
    sub = lax.broadcasted_iota(jnp.int32, (TILE, LANES), 0)
    lane = lax.broadcasted_iota(jnp.int32, (TILE, LANES), 1)
    east_edge, west_edge = lane == LANES - 1, lane == 0
    high = ny // TILE

    def spot(r, t):
        return slice(t * ny + r * TILE, t * ny + (r + 1) * TILE)

    def advance(turn, load, keep, store):
        for r in range(high):
            row = TILE + r * TILE
            ahead, behind = {}, {}
            for m in range(mem_dev):
                for t in range(tiles):
                    f = load(m, t, row)
                    ahead[m, t] = pltpu.roll(f, LANES - 1, 1)
                    behind[m, t] = pltpu.roll(f, 1, 1)
            for t in range(tiles):
                at = spot(r, t)
                east_w, west_w = weights[turn, 0, at, :], weights[turn, 1, at, :]
                north_w, south_w = weights[turn, 2, at, :], weights[turn, 3, at, :]
                for m in range(mem_dev):
                    f = load(m, t, row)
                    east = jnp.where(east_edge, ahead.get((m, t + 1), f), ahead[m, t])
                    west = jnp.where(west_edge, behind.get((m, t - 1), f), behind[m, t])
                    if r + 1 < high:
                        north = load(m, t, row + 1)
                    else:
                        north = jnp.where(sub == TILE - 1, f, pltpu.roll(f, TILE - 1, 0))
                    if r > 0:
                        south = load(m, t, row - 1)
                    else:
                        south = jnp.where(sub == 0, f, pltpu.roll(f, 1, 0))
                    store(
                        m,
                        r,
                        t,
                        (keep * f + east_w * east)
                        + (west_w * west + north_w * north)
                        + south_w * south,
                    )

    for c, ((start, count, whole), blocks) in enumerate(zip(parts, outs)):
        direct = whole and block % TILE == 0
        for copy in loads(c):
            copy.wait()
        for s in range(count):
            slab = start + s
            diffuse = spread[slab]
            keep = 1.0 - 4.0 * diffuse
            for r in range(high):
                for t in range(tiles):
                    tile = (slice(r * TILE, (r + 1) * TILE), slice(t * LANES, (t + 1) * LANES))
                    half_v, half_h = 0.5 * cv_buf[slab, *tile], 0.5 * ch_buf[slab, *tile]
                    weights[s % 2, 0, spot(r, t), :] = diffuse - half_v
                    weights[s % 2, 1, spot(r, t), :] = diffuse + half_v
                    weights[s % 2, 2, spot(r, t), :] = diffuse - half_h
                    weights[s % 2, 3, spot(r, t), :] = diffuse + half_h

            def first(m, t, row):
                return x_buf[m, slab, t, row : row + TILE, :]

            def later(m, t, row):
                return half[s % 2 * mem_dev + m, t, row : row + TILE, :]

            def between(m, r, t, value):
                row = TILE + r * TILE
                half[s % 2 * mem_dev + m, t, row : row + TILE, :] = value

            def final(m, r, t, value):
                field[slab * mem_dev + m, spot(r, t), :] = value
                if direct:
                    at = (m * count + s) * depth + t * block + r * TILE % block
                    arrays[c][0][r * TILE // block, at : at + TILE, :] = value

            for step in range(STEPS):
                load, store = later if step else first, between if step < STEPS - 1 else final
                advance(s % 2, load, keep, store)

        def send(i, carry):
            level = start * mem_dev + i
            at = pl.multiple_of((i % mem_dev * count + i // mem_dev) * depth, TILE)
            for ref, d in blocks:
                for t in range(tiles):
                    row = pl.multiple_of(t * ny + d * block, block)
                    ref[pl.ds(at + t * block, block), :] = field[level, pl.ds(row, block), :]
            return carry

        if not direct:
            lax.fori_loop(0, count * mem_dev, send, 0)

    line_lane = lax.broadcasted_iota(jnp.int32, (1, LANES), 1)
    for k in range(total):
        level, row, wanted = spots[0, k], spots[1, k], spots[2, k]
        for m in range(mem_dev):
            line = field[level + m, pl.ds(row, 1), :]
            picks[m, pl.ds(k, 1), :] = jnp.where(line_lane == wanted, line, 0.0)
    diagonal = lax.broadcasted_iota(jnp.int32, (total, LANES), 0) == lax.broadcasted_iota(
        jnp.int32, (total, LANES), 1
    )
    values = []
    for m in range(mem_dev):
        value = jnp.sum(picks[m], axis=1, keepdims=True)
        values.append(jnp.sum(jnp.where(diagonal, value, 0.0), axis=0, keepdims=True))
    for j in range(n):
        seen = jnp.zeros((TILE, LANES), jnp.float32)
        for m in range(mem_dev):
            seen = jnp.where(sub == (j * mem_dev + m) % TILE, values[m], seen)
        outs[0][j][0][pl.ds(mem_dev * parts[0][1] * depth, TILE), :] = seen


def forecast(parts, n, cells, slabs, spread, x, cv, ch):
    mem_dev, slab_dev, ny, nx = x.shape
    depth = ny // n * nx // LANES
    shapes = []
    for i, (_, count, whole) in enumerate(parts):
        shapes.append(block_shapes(n, whole, mem_dev * count * depth + (0 if i else TILE)))
    outs = pl.pallas_call(
        functools.partial(forecast_kernel, parts, n),
        in_specs=[pl.BlockSpec(memory_space=pltpu.HBM)] * 6,
        out_specs=[VMEM for group in shapes for _ in group],
        out_shape=[shape for group in shapes for shape in group],
        scratch_shapes=[
            pltpu.VMEM((mem_dev, slab_dev, nx // LANES, ny + 2 * TILE, LANES), jnp.float32),
            pltpu.VMEM(cv.shape, jnp.float32),
            pltpu.VMEM(ch.shape, jnp.float32),
            pltpu.SMEM(cells.shape, jnp.int32),
            pltpu.SMEM(slabs.shape, jnp.int32),
            pltpu.SMEM(spread.shape, jnp.float32),
            pltpu.SMEM((3, cells.size), jnp.int32),
            pltpu.VMEM((slab_dev * mem_dev, ny * nx // LANES, LANES), jnp.float32),
            pltpu.VMEM((2 * mem_dev, nx // LANES, ny + 2 * TILE, LANES), jnp.float32),
            pltpu.VMEM((2, 4, ny * nx // LANES, LANES), jnp.float32),
            pltpu.VMEM((mem_dev, cells.size, LANES), jnp.float32),
            pltpu.SemaphoreType.DMA((2 + nx // LANES, len(parts))),
            pltpu.SemaphoreType.DMA((3,)),
        ],
        cost_estimate=cost(60 * x.size, 4 * (2 * x.size + 2 * cv.size)),
        compiler_params=params(),
        name="forecast",
    )(*[pltpu.with_memory_space_constraint(a, pltpu.HBM) for a in (cells, slabs, spread, x, cv, ch)])
    sends = []
    for group in shapes:
        sends.append(list(outs[: len(group)]))
        outs = outs[len(group) :]
    return sends


def reach(cells, lists, nx, block, groups):
    total = cells.shape[0] * cells.shape[1]
    me = lax.axis_index("mem")
    for g in range(groups):
        count = jnp.int32(0)
        low_col = g * TILE // block * LANES
        high_col = (g * TILE + TILE - 1) // block * LANES + LANES - 1
        low_row = me * block + g * TILE % block
        high_row = low_row + min(block, TILE) - 1
        for k in range(total):
            row, col = row_col(place(cells, k), nx)
            down = jnp.maximum(jnp.maximum(low_row - row, row - high_row), 0)
            across = jnp.maximum(jnp.maximum(low_col - col, col - high_col), 0)
            lists[g, count] = jnp.int32(k)
            near = down * down + across * across < (2 * LOC_HALF) ** 2
            count = count + near.astype(jnp.int32)
        lists[g, count] = jnp.int32(total)
        lists[g, total + 1] = count


def taper_kernel(nx, block, cells, values_ref, errors_ref, loc_ref, near_ref, meta_ref, out, lists, sem):
    total = near_ref.shape[0]
    depth = loc_ref.shape[1]
    at = lax.broadcasted_iota(jnp.int32, (depth, LANES), 0)
    cell_row = (lax.axis_index("mem") * block + at % block).astype(jnp.float32)
    cell_col = (
        at // block * LANES + lax.broadcasted_iota(jnp.int32, (depth, LANES), 1)
    ).astype(jnp.float32)
    lane = lax.broadcasted_iota(jnp.int32, (1, LANES), 1)
    row_of = jnp.zeros((1, LANES), jnp.float32)
    col_of = jnp.zeros((1, LANES), jnp.float32)
    for k in range(total):
        row, col = row_col(place(cells, k), nx)
        row, col = row.astype(jnp.float32), col.astype(jnp.float32)
        row_of = jnp.where(lane == k, row, row_of)
        col_of = jnp.where(lane == k, col, col_of)
        loc_ref[k] = taper(cell_row - row, cell_col - col)
        meta_ref[k, 0:1, :] = jnp.full((1, LANES), place(errors_ref, k), jnp.float32)
        meta_ref[k, 1:2, :] = jnp.full((1, LANES), place(values_ref, k), jnp.float32)
    loc_ref[total] = jnp.zeros((depth, LANES), jnp.float32)
    reach(cells, lists, nx, block, depth // TILE)
    copy = pltpu.make_async_copy(lists, out, sem)
    copy.start()
    diagonal = lax.broadcasted_iota(jnp.int32, (total, LANES), 0) == lax.broadcasted_iota(
        jnp.int32, (total, LANES), 1
    )
    own_row = jnp.sum(jnp.where(diagonal, row_of, 0.0), axis=1, keepdims=True)
    own_col = jnp.sum(jnp.where(diagonal, col_of, 0.0), axis=1, keepdims=True)
    near_ref[...] = taper(row_of - own_row, col_of - own_col)
    copy.wait()


def list_shape(depth):
    return (-(-depth // TILE // TILE) * TILE, LANES)


def taper_tables(nx, block, cells, values, errors):
    total = cells.size
    depth = block * nx // LANES
    return pl.pallas_call(
        functools.partial(taper_kernel, nx, block),
        in_specs=[SMEM] * 3,
        out_specs=[VMEM] * 4,
        out_shape=[
            jax.ShapeDtypeStruct((total + 1, depth, LANES), jnp.float32),
            jax.ShapeDtypeStruct((total, LANES), jnp.float32),
            jax.ShapeDtypeStruct((total, TILE, LANES), jnp.float32),
            jax.ShapeDtypeStruct(list_shape(depth), jnp.int32),
        ],
        scratch_shapes=[pltpu.SMEM(list_shape(depth), jnp.int32), pltpu.SemaphoreType.DMA(())],
        cost_estimate=cost(60 * total * depth * LANES, 4 * total * depth * LANES),
        compiler_params=params(),
        name="taper_tables",
    )(cells, values, errors)


def settle_blocks(n, mem_dev, count, depth, lists, anom_ref, incr_ref, loc_ref, ins, outs):
    total = loc_ref.shape[0] - 1
    members = n * mem_dev
    group = max(g for g in range(1, count + 1) if count % g == 0 and (g == 1 or g * members <= 48))
    turns = count // group

    def spread(ref, k, m):
        return ref[k, pl.ds(m, TILE, stride=0), :]

    def part(i, carry):
        tile, slab = i // turns, i % turns * group
        at = tile * TILE

        def spot(m, g):
            row = ((m % mem_dev) * count + slab + g) * depth + at
            return m // mem_dev, pl.ds(pl.multiple_of(row, TILE), TILE)

        xs = []
        for m in range(members):
            for g in range(group):
                src, row = spot(m, g)
                xs.append(ins[src][0][row, :])

        def step(k, xs):
            terms = [[] for _ in range(group)]
            for m in range(members):
                a = spread(anom_ref, k, m)
                for g in range(group):
                    terms[g].append(a * xs[m * group + g])
            loc = loc_ref[k, pl.ds(pl.multiple_of(at, TILE), TILE), :]
            for g in range(group):
                while len(terms[g]) > 1:
                    odd = terms[g][len(terms[g]) // 2 * 2 :]
                    terms[g] = [a + b for a, b in zip(terms[g][::2], terms[g][1::2])] + odd
            sums = [terms[g][0] * loc for g in range(group)]
            new = []
            for m in range(members):
                b = spread(incr_ref, k, m)
                for g in range(group):
                    new.append(xs[m * group + g] + b * sums[g])
            return new

        def two(i, xs):
            return tuple(step(lists[tile, 2 * i + 1], step(lists[tile, 2 * i], list(xs))))

        xs = lax.fori_loop(
            0, lax.shift_right_logical(lists[tile, total + 1] + 1, 1), two, tuple(xs)
        )
        for m in range(members):
            for g in range(group):
                src, row = spot(m, g)
                outs[src][0][row, :] = xs[m * group + g]
        return carry

    lax.fori_loop(0, depth // TILE * turns, part, 0)


def plan_kernel(n, mem_dev, count, lev, loc_ref, near_ref, meta_ref, lists_ref, *refs):
    seen_refs, refs = refs[:lev], refs[lev:]
    ins, refs = blocks_in(refs[:n], n, False), refs[n:]
    anom_ref, incr_ref = refs[:2]
    outs = blocks_in(refs[2 : 2 + n], n, False)
    lists, sem = refs[2 + n :]
    copy = pltpu.make_async_copy(lists_ref, lists, sem)
    copy.start()
    total, depth = near_ref.shape[0], loc_ref.shape[1]
    rows = seen_refs[0][...]
    for other in seen_refs[1:]:
        rows = rows + other[...]
    members = rows.shape[0]
    mean = jnp.sum(rows, axis=0, keepdims=True) * (1.0 / members)
    rows = rows - mean
    for k in range(total):
        error, value = meta_ref[k, 0:1, :], meta_ref[k, 1:2, :]
        anomaly = jnp.broadcast_to(rows[:, k : k + 1], rows.shape)
        ybar = jnp.broadcast_to(mean[:, k : k + 1], mean.shape)
        variance = jnp.sum(anomaly * anomaly, axis=0, keepdims=True) / (members - 1) + 1e-06
        shared = jnp.sum(rows * anomaly, axis=0, keepdims=True)
        scale = 1.0 / ((members - 1) * variance)
        shift = (ybar * error + value * variance) / (variance + error) - ybar
        shrink = jnp.sqrt(error / (variance + error)) - 1.0
        anom_ref[k, 0:members, :] = anomaly * scale
        incr_ref[k, 0:members, :] = shift + shrink * anomaly
        weight = near_ref[k : k + 1, :] * shared * scale
        mean = mean + weight * shift
        rows = rows + (weight * shrink) * anomaly
    anom_ref[total] = jnp.zeros(anom_ref.shape[1:], jnp.float32)
    incr_ref[total] = jnp.zeros(incr_ref.shape[1:], jnp.float32)
    copy.wait()
    settle_blocks(n, mem_dev, count, depth, lists, anom_ref, incr_ref, loc_ref, ins, outs)


def filter_plan(mem_dev, count, places, seen, xs):
    members = seen[0].shape[0]
    n = len(xs)
    total, depth = places[1].shape[0], places[0].shape[1]
    table = jax.ShapeDtypeStruct((total + 1, members + TILE, LANES), jnp.float32)
    shapes = [table, table] + block_shapes(n, False, mem_dev * count * depth)
    got = pl.pallas_call(
        functools.partial(plan_kernel, n, mem_dev, count, len(seen)),
        in_specs=[VMEM] * (4 + len(seen) + n),
        out_specs=[VMEM] * len(shapes),
        out_shape=shapes,
        scratch_shapes=[pltpu.SMEM(list_shape(depth), jnp.int32), pltpu.SemaphoreType.DMA(())],
        cost_estimate=cost(20_000_000, 4 * total * (2 * members + depth) * LANES),
        compiler_params=params(),
        name="filter_plan",
    )(*places, *seen, *xs)
    return got[:2], list(got[2:])


def settle_kernel(n, mem_dev, count, depth, whole, lists_ref, anom, incr, loc, *refs):
    width = 1 if whole else n
    ins, outs = blocks_in(refs[:width], n, whole), blocks_in(refs[width:-2], n, False)
    lists, sem = refs[-2:]
    copy = pltpu.make_async_copy(lists_ref, lists, sem)
    copy.start()
    copy.wait()
    settle_blocks(n, mem_dev, count, depth, lists, anom, incr, loc, ins, outs)


def settle(n, mem_dev, count, whole, places, tables, xs):
    loc, lists = places[0], places[3]
    depth = loc.shape[1]
    shapes = block_shapes(n, False, mem_dev * count * depth)
    size = n * mem_dev * count * depth * LANES
    return pl.pallas_call(
        functools.partial(settle_kernel, n, mem_dev, count, depth, whole),
        in_specs=[VMEM] * (4 + len(xs)),
        out_specs=[VMEM] * len(shapes),
        out_shape=shapes,
        scratch_shapes=[pltpu.SMEM(list_shape(depth), jnp.int32), pltpu.SemaphoreType.DMA(())],
        cost_estimate=cost(4 * loc.shape[0] * size, 8 * size),
        compiler_params=params(),
        name="settle",
    )(lists, *tables, loc, *xs)


def assemble_kernel(n, start, count, *refs):
    out_ref, stage, turn, sem = refs[-4:]
    blocks = blocks_in(refs[:n], n, False)
    mem_dev, _, ny, nx = out_ref.shape
    block = ny // n
    tiles = nx // LANES
    depth = block * tiles
    copies = []
    for slab in range(count):
        for m in range(mem_dev):
            at = (m * count + slab) * depth
            for t in range(tiles):
                lanes = slice(t * LANES, (t + 1) * LANES)
                lines = slice(at + t * block, at + (t + 1) * block)
                for j, (ref, d) in enumerate(blocks):
                    if block % TILE == 0:
                        row = pl.multiple_of(d * block, block)
                        stage[m, slab, pl.ds(row, block), lanes] = ref[lines, :]
                    else:
                        turn[j * block : (j + 1) * block, :] = ref[lines, :]
                if block % TILE:
                    for d, (_, j) in enumerate(blocks):
                        stage[m, slab, d * block : (d + 1) * block, lanes] = turn[
                            pl.ds(j * block, block), :
                        ]
        copies.append(
            pltpu.make_async_copy(
                stage.at[:, slab], out_ref.at[:, start + slab], sem.at[slab]
            )
        )
        copies[-1].start()
    for copy in copies:
        copy.wait()


def assemble(n, start, count, recv, shape, before):
    mem_dev, _, ny, nx = shape
    extra = [] if before is None else [before]
    return pl.pallas_call(
        functools.partial(assemble_kernel, n, start, count),
        in_specs=[VMEM] * n + [pl.BlockSpec(memory_space=pl.ANY)] * len(extra),
        out_specs=pl.BlockSpec(memory_space=pl.ANY),
        out_shape=jax.ShapeDtypeStruct(shape, jnp.float32),
        scratch_shapes=[
            pltpu.VMEM((mem_dev, count, ny, nx), jnp.float32),
            pltpu.VMEM((ny, LANES), jnp.float32),
            pltpu.SemaphoreType.DMA((count,)),
        ],
        input_output_aliases={} if before is None else {n: 0},
        cost_estimate=cost(0, 8 * n * recv[0].size),
        compiler_params=params(),
        name="assemble",
    )(*recv, *extra)


def order_of(n, near_first=False):
    far, near = list(range(n // 2, n)), list(range(2, n // 2)) + [1]
    if near_first:
        return near + far
    return [j for pair in zip(far, near) for j in pair] + far[len(near) :]


def exchange(blocks, n, whole, near_first=False):
    if whole:
        return [lax.all_to_all(blocks[0], "mem", split_axis=0, concat_axis=0, tiled=True)]
    got = {}
    for j in order_of(n, near_first):
        got[j] = lax.ppermute(blocks[j], "mem", [(i, i ^ j) for i in range(n)])
    return blocks[:1] + [got[j] for j in range(1, n)]


def body(x, cv, ch, spread, obs_cells, obs_slabs, obs_values, obs_error):
    mem_dev, slab_dev, ny, nx = x.shape
    n, lev = lax.axis_size("mem"), lax.axis_size("lev")
    block = ny // n
    depth = block * nx // LANES
    parts = chunks_of(slab_dev)
    sends = forecast(parts, n, obs_cells, obs_slabs, spread, x, cv, ch)
    states = []
    for c, blocks in enumerate(sends):
        states.append(exchange(blocks, n, parts[c][2]))
    per = TILE // mem_dev
    seen = [s[mem_dev * parts[0][1] * depth :, :] for s in states[0]]
    seen = jnp.concatenate([sum(seen[g : g + per]) for g in range(0, n, per)])
    tiles = [seen] + [
        lax.ppermute(seen, "lev", [(i, (i + d) % lev) for i in range(lev)])
        for d in range(1, lev)
    ]
    places = taper_tables(nx, block, obs_cells, obs_values, obs_error)
    result = None
    for c, ((start, count, whole), state) in enumerate(zip(parts, states)):
        if c == 0:
            tables, new = filter_plan(mem_dev, count, places, tiles, state)
        else:
            new = settle(n, mem_dev, count, whole, places, tables, state)
        back = exchange(list(new), n, False, near_first=c == 0)
        result = assemble(n, start, count, back, x.shape, result)
    return result


def solution(mesh):
    in_specs = (
        P("mem", "lev", None, None),
        P("lev", None, None),
        P("lev", None, None),
        P("lev"),
        P(),
        P(),
        P(),
        P(),
    )
    out_specs = P("mem", "lev", None, None)
    return jax.shard_map(body, mesh=mesh, in_specs=in_specs, out_specs=out_specs, check_vma=False)
```
